128 devices in a mesh: row: 16 (over z, y_hi, core), col: 8 (over y_lo, x).
Axes of the slice: x: 4, y: 4 (y_hi: 2, y_lo: 2; y = y_hi * 2 + y_lo), z: 4, core: 2. Of those that a mesh axis runs over, the one named last changes fastest.
Arguments:
- layer_input: bfloat16 [2, 8192, 1024], P(None, 'row', 'col'), may hold values from -96 to 96
- out_grad: bfloat16 [2, 8192, 1024], P(None, 'row', 'col'), may hold values from -6 to 6
- token_route: int32 [2, 8192], P(None, 'row'), may hold values from 0 to 8191, as said below
- seq_lengths: int32 [2, 16, 4], P(None, 'row'), may hold values from 0 to 512, as said below
- positions: int32 [2, 8192], P(None, 'row'), may hold values from 0 to 3580, as said below
- attn_gain: bfloat16 [1024], replicated, may hold values from 0.099609375 to 1.8984375
- query_weight: bfloat16 [1024, 2048], P('row', 'col'), may hold values from -0.1875 to 0.1875
- key_weight: bfloat16 [1024, 1024], P('row', 'col'), may hold values from -0.1875 to 0.1875
- value_weight: bfloat16 [1024, 1024], P('row', 'col'), may hold values from -0.1875 to 0.1875
- query_gain: bfloat16 [128], replicated, may hold values from 0.099609375 to 1.8984375
- key_gain: bfloat16 [128], replicated, may hold values from 0.099609375 to 1.8984375
- out_weight: bfloat16 [2048, 1024], P('col', 'row'), may hold values from -0.5 to 0.5
- mlp_gain: bfloat16 [1024], replicated, may hold values from 0.099609375 to 1.8984375
- gate_weight: bfloat16 [1024, 3072], P('row', 'col'), may hold values from -0.1875 to 0.1875
- up_weight: bfloat16 [1024, 3072], P('row', 'col'), may hold values from -0.1875 to 0.1875
- down_weight: bfloat16 [3072, 1024], P('col', 'row'), may hold values from -0.109375 to 0.109375
Outputs:
- layer_output: bfloat16 [2, 8192, 1024], P(None, 'row', 'col')
- input_grad: bfloat16 [2, 8192, 1024], P(None, 'row', 'col')
- attn_gain_grad: float32 [1024], replicated
- query_grad: float32 [1024, 2048], P('row', 'col')
- key_grad: float32 [1024, 1024], P('row', 'col')
- value_grad: float32 [1024, 1024], P('row', 'col')
- query_gain_grad: float32 [128], replicated
- key_gain_grad: float32 [128], replicated
- out_proj_grad: float32 [2048, 1024], P('col', 'row')
- mlp_gain_grad: float32 [1024], replicated
- gate_grad: float32 [1024, 3072], P('row', 'col')
- up_grad: float32 [1024, 3072], P('row', 'col')
- down_grad: float32 [3072, 1024], P('col', 'row')
The draws below stay inside these ranges and needn't reach their ends.
Inputs may be any that keep to these rules, and one draw needn't show every extreme that they name: Each row of token_route holds every number from 0 to 8191 once. Each aligned block of 512 entries holds the same number of entries of every group (g * 512 to (g + 1) * 512 - 1). `seq_lengths`: each row of 4 lengths sums to 512; nonzero lengths come first and zeros mark unused slots. Some row holds a single sequence of 512 tokens. Within each sequence of the group layout, positions rise by 1 to 3 from one token to the next.
All inputs are finite; a program needn't handle non-finite values.
Results may differ from the reference program's by a relative error of at most 0.018.
Values may be sent and summed in bfloat16 or wider, within the bound.
No kernel may reach another device: no remote copies, remote signals or barrier semaphores. Data moves between devices by JAX's collectives and lax.ppermute only.
A program may use at most 128 MiB of HBM per device.

```python
import math
import jax
import jax.numpy as jnp
from jax import lax

D = 1024
QUERY_HEADS = 16
KEY_VALUE_HEADS = 8
HEAD_SIZE = 128
FF = 3072
GROUP_TOK = 512
MICRO = 2
SLOTS = 4
QW = 2048
KVW = 1024
MB_TOKENS = 8192


def draw_layer_input(key, part):
    key_list = jax.random.split(key, 3)
    full_shape = (MICRO, MB_TOKENS, D)
    columns = jnp.exp(jax.random.uniform(key_list[2], (1, 1, D), jnp.float32, math.log(0.4), math.log(4.0)))
    base_value = jax.random.normal(key_list[0], full_shape, jnp.float32)
    scales = jnp.exp(jax.random.uniform(key_list[1], (MICRO, MB_TOKENS, 1), jnp.float32, math.log(0.3), math.log(3.0)))
    base_value = jnp.clip(base_value, -6.0, 6.0)
    return (base_value * scales * columns).astype(jnp.bfloat16)


def draw_token_route(key, part):
    first_key, second_key = jax.random.split(key)
    groups = MB_TOKENS // GROUP_TOK
    piece_rows = GROUP_TOK // groups
    slots = jnp.broadcast_to(jnp.arange(GROUP_TOK, dtype=jnp.int32), (MICRO, groups, GROUP_TOK))
    slots = jax.random.permutation(first_key, slots, axis=2, independent=True)
    target = slots + (jnp.arange(groups, dtype=jnp.int32) * GROUP_TOK)[None, :, None]
    target = target.reshape(MICRO, groups, groups, piece_rows)
    target = jnp.transpose(target, (0, 2, 1, 3)).reshape(MICRO, groups, GROUP_TOK)
    target = jax.random.permutation(second_key, target, axis=2, independent=True)
    return target.reshape(MICRO, MB_TOKENS).astype(jnp.int32)


def sequence_layout(key):
    inner_key = jax.random.fold_in(key, 17)
    key_list = jax.random.split(inner_key, 5)
    groups = MB_TOKENS // GROUP_TOK
    row_count = MICRO * groups
    row_ids = jnp.arange(row_count, dtype=jnp.int32)
    counts = jax.random.randint(key_list[0], (row_count,), 1, SLOTS + 1)
    single = jax.random.randint(key_list[1], (), 0, row_count).astype(jnp.int32)
    other = (single + 1) % row_count
    counts = jnp.where(row_ids == single, 1, counts)
    cut_points = jnp.broadcast_to(jnp.arange(1, GROUP_TOK, dtype=jnp.int32), (row_count, GROUP_TOK - 1))
    cut_points = jax.random.permutation(key_list[2], cut_points, axis=1, independent=True)[:, :SLOTS - 1]
    cut_points = jnp.where(jnp.arange(SLOTS - 1)[None, :] < counts[:, None] - 1, cut_points, GROUP_TOK)
    cut_points = jnp.sort(cut_points, axis=1).astype(jnp.int32)
    seq_edges = jnp.concatenate([jnp.zeros((row_count, 1), jnp.int32), cut_points, jnp.full((row_count, 1), GROUP_TOK, jnp.int32)], axis=1)
    lengths = (seq_edges[:, 1:] - seq_edges[:, :-1]).astype(jnp.int32)
    places = jnp.arange(GROUP_TOK, dtype=jnp.int32)
    segment = jnp.sum((places[None, :, None] >= cut_points[:, None, :]).astype(jnp.int32), axis=2)
    strides = jax.random.randint(key_list[3], (row_count, GROUP_TOK), 1, 4).astype(jnp.int32)
    strides = jnp.where((row_ids == single)[:, None], 3, strides).astype(jnp.int32)
    before = jnp.cumsum(strides, axis=1).astype(jnp.int32) - strides
    starts = jnp.minimum(seq_edges[:, :-1], GROUP_TOK - 1)
    start_of = jnp.take_along_axis(starts, segment, axis=1)
    base_value = jnp.take_along_axis(before, start_of, axis=1)
    offsets = jax.random.randint(key_list[4], (row_count, SLOTS), 0, 2048).astype(jnp.int32)
    first_slot = (jnp.arange(SLOTS, dtype=jnp.int32) == 0)[None, :]
    offsets = jnp.where((row_ids == single)[:, None] & first_slot, 2047, offsets)
    offsets = jnp.where((row_ids == other)[:, None] & first_slot, 0, offsets).astype(jnp.int32)
    position_rows = jnp.take_along_axis(offsets, segment, axis=1) + before - base_value
    return (lengths.reshape(MICRO, groups, SLOTS), position_rows.reshape(MICRO, MB_TOKENS).astype(jnp.int32))


def draw_seq_lengths(key, part):
    lengths, position_rows = sequence_layout(key)
    return lengths


def draw_positions(key, part):
    lengths, position_rows = sequence_layout(key)
    return position_rows


def block_levels(stream_key, dims, cuts, low, largest):
    factor_of = 1.0
    for axis_at, blocks in cuts:
        steps = jax.random.uniform(jax.random.fold_in(jax.random.fold_in(stream_key, 6), axis_at), (blocks,), jnp.float32, low / len(cuts), largest / len(cuts))
        factor_of = factor_of * jnp.repeat(jnp.exp(steps), dims[axis_at] // blocks).reshape((-1,) + (1,) * (len(dims) - 1 - axis_at))
    return factor_of


def normal_values(key, extent, scale, reach, cuts=(), held_as=jnp.bfloat16):
    values = scale * jax.random.normal(key, extent, jnp.float32)
    if cuts:
        values = values * block_levels(key, extent, cuts, -0.22, 0.18)
    return jnp.clip(values, -reach, reach).astype(held_as)


def setup_inputs(seed: int = 0) -> dict:
    keys = jax.random.split(jax.random.key(seed), 17)
    layer_input = draw_layer_input(jax.random.fold_in(keys[16], 71), 0)
    out_grad = normal_values(keys[1], (MICRO, MB_TOKENS, D), 1.0, 6.0, ((1, 16), (2, 8)))
    token_route = draw_token_route(jax.random.fold_in(keys[16], 71), 0)
    seq_lengths = draw_seq_lengths(jax.random.fold_in(keys[16], 71), 0)
    positions = draw_positions(jax.random.fold_in(keys[16], 71), 0)
    attn_gain = jnp.clip(1.0 + 0.18 * jax.random.normal(keys[5], (D,), jnp.float32), 0.099609375, 1.8984375).astype(jnp.bfloat16)
    query_weight = normal_values(keys[6], (D, QW), D ** -0.5, 0.1875, ((0, 16), (1, 8)))
    key_weight = normal_values(keys[7], (D, KVW), D ** -0.5, 0.1875, ((0, 16), (1, 8)))
    value_weight = normal_values(keys[8], (D, KVW), D ** -0.5, 0.1875, ((0, 16), (1, 8)))
    query_gain = jnp.clip(1.0 + 0.18 * jax.random.normal(keys[9], (HEAD_SIZE,), jnp.float32), 0.099609375, 1.8984375).astype(jnp.bfloat16)
    key_gain = jnp.clip(1.0 + 0.18 * jax.random.normal(keys[10], (HEAD_SIZE,), jnp.float32), 0.099609375, 1.8984375).astype(jnp.bfloat16)
    out_weight = normal_values(keys[11], (QW, D), (QW // 16) ** -0.5, 0.5, ((0, 8), (1, 16)))
    mlp_gain = jnp.clip(1.0 + 0.18 * jax.random.normal(keys[12], (D,), jnp.float32), 0.099609375, 1.8984375).astype(jnp.bfloat16)
    gate_weight = normal_values(keys[13], (D, FF), D ** -0.5, 0.1875, ((0, 16), (1, 8)))
    up_weight = normal_values(keys[14], (D, FF), D ** -0.5, 0.1875, ((0, 16), (1, 8)))
    down_weight = normal_values(keys[15], (FF, D), FF ** -0.5, 0.109375, ((0, 8), (1, 16)))
    return {"layer_input": layer_input, "out_grad": out_grad, "token_route": token_route, "seq_lengths": seq_lengths, "positions": positions, "attn_gain": attn_gain, "query_weight": query_weight, "key_weight": key_weight, "value_weight": value_weight, "query_gain": query_gain, "key_gain": key_gain, "out_weight": out_weight, "mlp_gain": mlp_gain, "gate_weight": gate_weight, "up_weight": up_weight, "down_weight": down_weight}


EPSILON = 1e-06
ROPE_BASE = 1000000.0
NEGATIVE = -1e+30
precise = lax.Precision.HIGHEST

@jax.custom_vjp
def reduced_precision(v):
    return lax.optimization_barrier(v.astype(jnp.bfloat16)).astype(jnp.float32)

@jax.custom_vjp
def reduced_precision_backward(v):
    return v

def low_keep(v):
    return (reduced_precision(v), None)

def low_pass(kept, grad):
    return (grad,)

def back_keep(v):
    return (v, None)

def back_low(kept, grad):
    return (reduced_precision(grad),)
reduced_precision.defvjp(low_keep, low_pass)
reduced_precision_backward.defvjp(back_keep, back_low)

def matrix_product(left_side, right_side):
    return jnp.dot(left_side, right_side, precision=precise)

def rms_scale(tensor, gain):
    return tensor * lax.rsqrt(lax.optimization_barrier(jnp.mean(tensor * tensor, axis=-1, keepdims=True)) + EPSILON) * gain

def rotate(tensor):
    half_size = tensor.shape[-1] // 2
    return jnp.concatenate([-tensor[..., half_size:], tensor[..., :half_size]], axis=-1)

def rope_tables(position):
    freq_steps = jnp.arange(0, HEAD_SIZE, 2).astype(jnp.float32) / HEAD_SIZE
    frequency = 1.0 / ROPE_BASE ** freq_steps
    angles = position.astype(jnp.float32)[:, None] * frequency[None, :]
    angles = jnp.concatenate([angles, angles], axis=-1)
    return (jnp.cos(angles), jnp.sin(angles))

def segment_ids(lengths, group_rows):
    bounds = jnp.cumsum(lengths)[:-1]
    places = jnp.arange(group_rows, dtype=jnp.int32)
    return lax.optimization_barrier(jnp.sum((places[:, None] >= bounds[None, :]).astype(jnp.int32), axis=1))

def pick_rows(table, index):
    return jax.vmap(lambda rows_in, rows_at: jnp.take(rows_in, rows_at, axis=0))(table, index)

def layer_forward(input_value, weight_set, cosine, sine_table, allowed):
    gain_one, query_matrix, key_projection_matrix, value_projection_matrix, query_scale, key_scale, out_matrix, gain_two, gate_matrix, up_matrix, down_matrix = weight_set
    token_rows = input_value.shape[0]
    first_normed_input = reduced_precision(rms_scale(input_value, gain_one))
    query_proj = reduced_precision_backward(matrix_product(first_normed_input, query_matrix)).reshape(token_rows, QUERY_HEADS, HEAD_SIZE)
    projected_keys = reduced_precision_backward(matrix_product(first_normed_input, key_projection_matrix)).reshape(token_rows, KEY_VALUE_HEADS, HEAD_SIZE)
    projected_values = reduced_precision(reduced_precision_backward(matrix_product(first_normed_input, value_projection_matrix))).reshape(token_rows, KEY_VALUE_HEADS, HEAD_SIZE)
    query_norm = rms_scale(query_proj, query_scale)
    key_norm = rms_scale(projected_keys, key_scale)
    rotated_queries = reduced_precision(query_norm * cosine[:, None, :] + rotate(query_norm) * sine_table[:, None, :])
    key_rot = reduced_precision(key_norm * cosine[:, None, :] + rotate(key_norm) * sine_table[:, None, :])
    grouped_queries = rotated_queries.reshape(token_rows, KEY_VALUE_HEADS, QUERY_HEADS // KEY_VALUE_HEADS, HEAD_SIZE)
    raw_scores = jnp.einsum('qkrd,tkd->krqt', grouped_queries, key_rot, precision=precise) * (1.0 / math.sqrt(HEAD_SIZE))
    scores = jnp.where(allowed[None, None], reduced_precision_backward(raw_scores), NEGATIVE)
    row_top = lax.optimization_barrier(jnp.max(scores, axis=-1, keepdims=True))
    exp_scores = jnp.exp(scores - row_top)
    softmax = exp_scores / lax.optimization_barrier(jnp.sum(exp_scores, axis=-1, keepdims=True))
    weights = reduced_precision(softmax)
    head_out = jnp.einsum('krqt,tkd->qkrd', weights, projected_values, precision=precise).reshape(token_rows, QUERY_HEADS * HEAD_SIZE)
    attended = reduced_precision(reduced_precision_backward(head_out))
    residual = input_value + reduced_precision_backward(matrix_product(attended, out_matrix))
    normed_two = reduced_precision(rms_scale(residual, gain_two))
    gate_value = reduced_precision_backward(matrix_product(normed_two, gate_matrix))
    up_value = reduced_precision_backward(matrix_product(normed_two, up_matrix))
    hidden = reduced_precision(gate_value * jax.nn.sigmoid(gate_value) * up_value)
    return residual + matrix_product(hidden, down_matrix)

def reference(layer_input, out_grad, token_route, seq_lengths, positions, attn_gain, query_weight, key_weight, value_weight, query_gain, key_gain, out_weight, mlp_gain, gate_weight, up_weight, down_weight):
    params = tuple((weight_item.astype(jnp.float32) for weight_item in (attn_gain, query_weight, key_weight, value_weight, query_gain, key_gain, out_weight, mlp_gain, gate_weight, up_weight, down_weight)))
    route_order = jnp.argsort(token_route, axis=1)
    group_total = MICRO * MB_TOKENS // GROUP_TOK
    grouped_in = pick_rows(layer_input, route_order).reshape(group_total, GROUP_TOK, D)
    grouped_grad = pick_rows(out_grad, route_order).reshape(group_total, GROUP_TOK, D)
    group_pos = positions.reshape(group_total, GROUP_TOK)
    group_lens = seq_lengths.reshape(group_total, SLOTS)

    def one_group(grad_sum, group_item):
        input_rows, grad_rows, pos_rows, len_rows = group_item
        segment = segment_ids(len_rows, GROUP_TOK)
        places = jnp.arange(GROUP_TOK, dtype=jnp.int32)
        allowed = (segment[:, None] == segment[None, :]) & (places[None, :] <= places[:, None])
        cosine, sine_table = rope_tables(pos_rows)

        def forward(input_value, weight_set):
            return layer_forward(input_value, weight_set, cosine, sine_table, allowed)
        result, pullback = jax.vjp(forward, input_rows.astype(jnp.float32), params)
        input_delta, weight_delta = pullback(grad_rows.astype(jnp.float32))
        grad_sum = jax.tree.map(lambda left_side, right_side: left_side + right_side, grad_sum, weight_delta)
        return (grad_sum, (result.astype(jnp.bfloat16), input_delta.astype(jnp.bfloat16)))
    zero_grads = tuple((jnp.zeros(weight_item.shape, jnp.float32) for weight_item in params))
    grad_sum, outcome = lax.scan(one_group, zero_grads, (grouped_in, grouped_grad, group_pos, group_lens))
    outputs, deltas = outcome
    layer_output = pick_rows(outputs.reshape(MICRO, MB_TOKENS, D), token_route)
    input_grad = pick_rows(deltas.reshape(MICRO, MB_TOKENS, D), token_route)
    return (layer_output, input_grad, grad_sum[0], grad_sum[1], grad_sum[2], grad_sum[3], grad_sum[4], grad_sum[5], grad_sum[6], grad_sum[7], grad_sum[8], grad_sum[9], grad_sum[10])
```

```python
import math

import jax
import jax.numpy as jnp
from jax import lax
from jax.sharding import PartitionSpec as P

D = 1024
HEAD_SIZE = 128
EPSILON = 1e-06
ROPE_BASE = 1000000.0
NEGATIVE = -1e30
BOTH = ("row", "col")
ROWS = 16
BF = jnp.bfloat16
F32 = jnp.float32


def flat(row, col):
    return row * 8 + col


SAME_X = [[0, 1, 2, 3], [4, 5, 6, 7]]
CORES = [[2 * k, 2 * k + 1] for k in range(8)]
PLANE = [
    [flat(2 * k + core, 4 * y_lo + x) for k in range(8) for y_lo in range(2)]
    for x in range(4)
    for core in range(2)
]


def dot(a, b, dims):
    return lax.dot_general(a, b, (dims, ((), ())), preferred_element_type=F32)


def nn(a, b):
    return dot(a, b, ((1,), (0,)))


def nt(a, b):
    return dot(a, b, ((1,), (1,)))


def tn(a, b):
    return dot(a, b, ((0,), (0,)))


def exchange(blocks, axis, groups=None):
    return lax.all_to_all(blocks, axis, 0, 0, axis_index_groups=groups, tiled=True)


def rotate(t):
    half = t.shape[-1] // 2
    return jnp.concatenate([-t[..., half:], t[..., :half]], axis=-1)


def unrotate(t):
    half = t.shape[-1] // 2
    return jnp.concatenate([t[..., half:], -t[..., :half]], axis=-1)


def collect_weight(shard):
    n = shard.shape[1]
    plane = exchange(jnp.broadcast_to(shard[None], (16, 64, n)), BOTH, PLANE)
    pair = exchange(jnp.broadcast_to(plane[None], (2, 16, 64, n)), "row", CORES)
    pair = pair.reshape(2, 8, 2, 64, n)
    return jnp.transpose(pair, (1, 0, 3, 2, 4)).reshape(1024, 2, n)


def reduce_weight(grad):
    n = grad.shape[2]
    parts = jnp.transpose(grad.reshape(8, 2, 64, 2, n), (1, 0, 3, 2, 4)).astype(BF)
    parts = exchange(parts, "row", CORES)
    half = (parts[0].astype(F32) + parts[1].astype(F32)).astype(BF)
    got = exchange(half.reshape(16, 64, n), BOTH, PLANE)
    return jnp.sum(got.astype(F32), axis=0)


def send_tokens(rows):
    parts = jnp.transpose(rows.reshape(2, ROWS, 32, 128), (1, 0, 2, 3))
    parts = jnp.broadcast_to(parts[:, :, None], (ROWS, 2, 4, 32, 128)).reshape(128, 32, 128)
    got = exchange(parts, BOTH).reshape(ROWS, 8, 32, 128)
    return jnp.transpose(got, (0, 2, 1, 3)).reshape(512, 1024)


def return_tokens(part):
    parts = jnp.transpose(part.astype(BF).reshape(ROWS, 32, 8, 128), (0, 2, 1, 3))
    got = exchange(parts.reshape(128, 32, 128), BOTH).reshape(ROWS, 2, 4, 32, 128)
    total = jnp.sum(got.astype(F32), axis=2)
    return jnp.transpose(total, (1, 0, 2, 3)).reshape(2, 512, 128)


def scatter_sum(part):
    parts = jnp.transpose(part.astype(BF).reshape(512, 2, 4, 128), (2, 0, 1, 3))
    got = exchange(parts, "col", SAME_X)
    return jnp.sum(got.astype(F32), axis=0)


def collect_features(mine):
    got = exchange(jnp.broadcast_to(mine[None], (4, 512, 2, 128)), "col", SAME_X)
    return jnp.transpose(got, (1, 2, 0, 3)).reshape(512, 1024)


def body(
    layer_input,
    out_grad,
    token_route,
    seq_lengths,
    positions,
    attn_gain,
    query_weight,
    key_weight,
    value_weight,
    query_gain,
    key_gain,
    out_weight,
    mlp_gain,
    gate_weight,
    up_weight,
    down_weight,
):
    col = lax.axis_index("col")
    y_lo = col // 4
    x = col % 4
    places = jnp.arange(512, dtype=jnp.int32)

    rank = jnp.sum((token_route[:, None, :] < token_route[:, :, None]).astype(jnp.int32), axis=2)
    chosen = places[None, :, None] == rank[:, None, :]
    pick = chosen.astype(BF)
    slots_out = jnp.sum(jnp.where(chosen, (token_route % 512)[:, None, :], 0), axis=2)
    slots_all = exchange(jnp.transpose(slots_out.reshape(2, ROWS, 32), (1, 0, 2)), "row")
    slots = lax.dynamic_index_in_dim(slots_all, y_lo, 1, keepdims=False).reshape(512)

    def sort_rows(table):
        return jnp.stack([nn(pick[m], table[m]).astype(BF) for m in range(2)])

    def unsort_rows(table):
        return jnp.stack([tn(pick[m], table[m].astype(BF)).astype(BF) for m in range(2)])

    inputs = send_tokens(sort_rows(layer_input))
    grads = send_tokens(sort_rows(out_grad))

    qkv_full = collect_weight(jnp.concatenate([query_weight, key_weight, value_weight], axis=1))
    rest_full = collect_weight(
        jnp.concatenate([out_weight.T, gate_weight, up_weight, down_weight.T], axis=1)
    )
    wq, wk, wv = qkv_full[:, :, :256], qkv_full[:, :, 256:384], qkv_full[:, :, 384:]
    wq, wk, wv = wq.reshape(1024, 512), wk.reshape(1024, 256), wv.reshape(1024, 256)
    wo, wg, wu, wd = (
        rest_full[:, :, :256].reshape(1024, 512),
        rest_full[:, :, 256:640].reshape(1024, 768),
        rest_full[:, :, 640:1024].reshape(1024, 768),
        rest_full[:, :, 1024:].reshape(1024, 768),
    )
    gain_one = attn_gain.astype(F32)
    gain_two = mlp_gain.astype(F32)
    query_scale = query_gain.astype(F32)
    key_scale = key_gain.astype(F32)

    lengths = lax.dynamic_index_in_dim(seq_lengths, y_lo, 0, keepdims=False)[0]
    bound_one = lengths[0]
    bound_two = bound_one + lengths[1]
    bound_three = bound_two + lengths[2]
    segment = (
        (slots >= bound_one).astype(jnp.int32)
        + (slots >= bound_two).astype(jnp.int32)
        + (slots >= bound_three).astype(jnp.int32)
    )
    allowed = (segment[:, None] == segment[None, :]) & (slots[None, :] <= slots[:, None])
    my_positions = lax.dynamic_index_in_dim(positions, y_lo, 0, keepdims=False)
    position = jnp.sum(
        jnp.where(slots[:, None] == places[None, :], my_positions[None, :], 0), axis=1
    )
    freq_steps = jnp.arange(0, HEAD_SIZE, 2).astype(F32) / HEAD_SIZE
    frequency = 1.0 / ROPE_BASE**freq_steps
    angles = position.astype(F32)[:, None] * frequency[None, :]
    angles = jnp.concatenate([angles, angles], axis=-1)
    cosine, sine = jnp.cos(angles)[:, None, :], jnp.sin(angles)[:, None, :]

    input_float = inputs.astype(F32)
    scale_one = lax.rsqrt(jnp.mean(input_float * input_float, axis=-1, keepdims=True) + EPSILON)
    hat_one = input_float * scale_one
    normed_one = (hat_one * gain_one).astype(BF)
    query_proj = nn(normed_one, wq).reshape(512, 4, HEAD_SIZE)
    key_proj = nn(normed_one, wk).reshape(512, 2, HEAD_SIZE)
    value_rows = nn(normed_one, wv).astype(BF).reshape(512, 2, HEAD_SIZE)
    query_inv = lax.rsqrt(jnp.mean(query_proj * query_proj, axis=-1, keepdims=True) + EPSILON)
    query_hat = query_proj * query_inv
    query_norm = query_hat * query_scale
    key_inv = lax.rsqrt(jnp.mean(key_proj * key_proj, axis=-1, keepdims=True) + EPSILON)
    key_hat = key_proj * key_inv
    key_norm = key_hat * key_scale
    query_rows = (query_norm * cosine + rotate(query_norm) * sine).astype(BF)
    key_rows = (key_norm * cosine + rotate(key_norm) * sine).astype(BF)
    grouped = query_rows.reshape(512, 2, 2, HEAD_SIZE)
    scores = jnp.einsum("qkrd,tkd->krqt", grouped, key_rows, preferred_element_type=F32)
    scores = jnp.where(allowed[None, None], scores * (1.0 / math.sqrt(HEAD_SIZE)), NEGATIVE)
    row_top = jnp.max(scores, axis=-1, keepdims=True)
    exp_scores = jnp.exp(scores - row_top)
    softmax = exp_scores / jnp.sum(exp_scores, axis=-1, keepdims=True)
    softmax_low = softmax.astype(BF)
    attended = jnp.einsum("krqt,tkd->qkrd", softmax_low, value_rows, preferred_element_type=F32)
    attended = attended.astype(BF).reshape(512, 512)
    summed = scatter_sum(nt(attended, wo))
    my_input = lax.dynamic_index_in_dim(inputs.reshape(512, 2, 4, 128), x, 2, keepdims=False)
    resid_mine = my_input.astype(F32) + summed
    resid = collect_features(resid_mine.astype(BF)).astype(F32)

    scale_two = lax.rsqrt(jnp.mean(resid * resid, axis=-1, keepdims=True) + EPSILON)
    hat_two = resid * scale_two
    normed_two = (hat_two * gain_two).astype(BF)
    gate = nn(normed_two, wg)
    up = nn(normed_two, wu)
    sigma = jax.nn.sigmoid(gate)
    activated = gate * sigma
    hidden = (activated * up).astype(BF)
    mine_mask = ((jnp.arange(8, dtype=jnp.int32) % 4) == x).astype(F32)[None, :, None]

    def place(mine):
        wide = jnp.broadcast_to(mine[:, :, None, :], (512, 2, 4, 128)).reshape(512, 8, 128)
        return (wide * mine_mask).reshape(512, 1024)

    output_home = return_tokens(nt(hidden, wd) + place(resid_mine))

    delta_hidden = nn(grads, wd)
    delta_gate = (delta_hidden * up * sigma * (1.0 + gate * (1.0 - sigma))).astype(BF)
    delta_up = (delta_hidden * activated).astype(BF)
    delta_two = nt(delta_gate, wg) + nt(delta_up, wu)
    mlp_gain_sum = jnp.sum(delta_two * hat_two, axis=0)
    scaled = delta_two * gain_two
    inner = jnp.mean(scaled * hat_two, axis=-1, keepdims=True)
    my_grad = lax.dynamic_index_in_dim(grads.reshape(512, 2, 4, 128), x, 2, keepdims=False)
    resid_delta = my_grad.astype(F32) + scatter_sum(scale_two * (scaled - hat_two * inner))
    resid_low = collect_features(resid_delta.astype(BF))

    delta_attended = nn(resid_low, wo).astype(BF).reshape(512, 2, 2, HEAD_SIZE)
    rest_grad = jnp.concatenate(
        [
            tn(resid_low, attended).reshape(1024, 2, 256),
            tn(normed_two, delta_gate).reshape(1024, 2, 384),
            tn(normed_two, delta_up).reshape(1024, 2, 384),
            tn(grads, hidden).reshape(1024, 2, 384),
        ],
        axis=2,
    )
    rest_total = reduce_weight(rest_grad)
    delta_probs = jnp.einsum(
        "qkrd,tkd->krqt", delta_attended, value_rows, preferred_element_type=F32
    )
    delta_value = jnp.einsum(
        "krqt,qkrd->tkd", softmax_low, delta_attended, preferred_element_type=F32
    )
    delta_scores = (
        softmax * (delta_probs - jnp.sum(delta_probs * softmax, axis=-1, keepdims=True))
    ).astype(BF)
    delta_query = jnp.einsum(
        "krqt,tkd->qkrd", delta_scores, key_rows, preferred_element_type=F32
    ) * (1.0 / math.sqrt(HEAD_SIZE))
    delta_key = jnp.einsum(
        "krqt,qkrd->tkd", delta_scores, grouped, preferred_element_type=F32
    ) * (1.0 / math.sqrt(HEAD_SIZE))
    delta_query = delta_query.reshape(512, 4, HEAD_SIZE)
    delta_query_norm = delta_query * cosine + unrotate(delta_query * sine)
    delta_key_norm = delta_key * cosine + unrotate(delta_key * sine)
    query_gain_sum = jnp.sum(delta_query_norm * query_hat, axis=(0, 1))
    key_gain_sum = jnp.sum(delta_key_norm * key_hat, axis=(0, 1))

    def norm_back(delta, hat, inv, gain):
        part = delta * gain
        part = inv * (part - hat * jnp.mean(part * hat, axis=-1, keepdims=True))
        return part.astype(BF).reshape(512, -1)

    delta_query_proj = norm_back(delta_query_norm, query_hat, query_inv, query_scale)
    delta_key_proj = norm_back(delta_key_norm, key_hat, key_inv, key_scale)
    delta_value_proj = delta_value.astype(BF).reshape(512, -1)
    delta_one = nt(delta_query_proj, wq) + nt(delta_key_proj, wk) + nt(delta_value_proj, wv)
    attn_gain_sum = jnp.sum(delta_one * hat_one, axis=0)
    scaled = delta_one * gain_one
    inner = jnp.mean(scaled * hat_one, axis=-1, keepdims=True)
    delta_home = return_tokens(scale_one * (scaled - hat_one * inner) + place(resid_delta))
    qkv_grad = jnp.concatenate(
        [
            tn(normed_one, delta_query_proj).reshape(1024, 2, 256),
            tn(normed_one, delta_key_proj).reshape(1024, 2, 128),
            tn(normed_one, delta_value_proj).reshape(1024, 2, 128),
        ],
        axis=2,
    )
    qkv_total = reduce_weight(qkv_grad)

    attn_gain_grad, mlp_gain_grad, query_gain_grad, key_gain_grad = lax.psum(
        (attn_gain_sum, mlp_gain_sum, query_gain_sum, key_gain_sum), BOTH
    )
    return (
        unsort_rows(output_home),
        unsort_rows(delta_home),
        attn_gain_grad,
        qkv_total[:, :256],
        qkv_total[:, 256:384],
        qkv_total[:, 384:],
        query_gain_grad,
        key_gain_grad,
        rest_total[:, :256].T,
        mlp_gain_grad,
        rest_total[:, 256:640],
        rest_total[:, 640:1024],
        rest_total[:, 1024:].T,
    )


def solution(mesh):
    in_specs = (
        P(None, "row", "col"),
        P(None, "row", "col"),
        P(None, "row"),
        P(None, "row", None),
        P(None, "row"),
        P(),
        P("row", "col"),
        P("row", "col"),
        P("row", "col"),
        P(),
        P(),
        P("col", "row"),
        P(),
        P("row", "col"),
        P("row", "col"),
        P("col", "row"),
    )
    out_specs = (
        P(None, "row", "col"),
        P(None, "row", "col"),
        P(),
        P("row", "col"),
        P("row", "col"),
        P("row", "col"),
        P(),
        P(),
        P("col", "row"),
        P(),
        P("row", "col"),
        P("row", "col"),
        P("col", "row"),
    )
    return jax.shard_map(body, mesh=mesh, in_specs=in_specs, out_specs=out_specs, check_vma=False)
```

```python
import functools
import math

import jax
import jax.numpy as jnp
from jax import lax
from jax.experimental import pallas as pl
from jax.experimental.pallas import tpu as pltpu
from jax.sharding import PartitionSpec as P

D = 1024
HEAD_SIZE = 128
EPSILON = 1e-06
ROPE_BASE = 1000000.0
NEGATIVE = -1e30
BOTH = ("row", "col")
ROWS = 16
TOK = 512
TILE = 256
BF = jnp.bfloat16
F32 = jnp.float32
SCALE = 1.0 / math.sqrt(HEAD_SIZE)


def flat(row, col):
    return row * 8 + col


def spot(z, y, core, x):
    return flat(z * 4 + (y // 2) * 2 + core, (y % 2) * 4 + x)


PLANE = [
    [flat(2 * k + core, 4 * y_lo + x) for k in range(8) for y_lo in range(2)]
    for x in range(4)
    for core in range(2)
]
TEAM = [[flat(row, 4 * y_lo + x) for y_lo in range(2) for row in range(ROWS)] for x in range(4)]


def moves(dz=0, dy=0, dcore=0, dx=0):
    return [
        (spot(z, y, core, x), spot((z + dz) % 4, (y + dy) % 4, core ^ dcore, (x + dx) % 4))
        for z in range(4)
        for y in range(4)
        for core in range(2)
        for x in range(4)
    ]


def shift(value, **step):
    return lax.ppermute(value, BOTH, moves(**step))


def dot(a, b, dims):
    return lax.dot_general(a, b, (dims, ((), ())), preferred_element_type=F32)


def nn(a, b):
    return dot(a, b, ((1,), (0,)))


def nt(a, b):
    return dot(a, b, ((1,), (1,)))


def tn(a, b):
    return dot(a, b, ((0,), (0,)))


def call(body, outs, scratch, flops, traffic, *args, smem=0):
    vmem = pl.BlockSpec(memory_space=pltpu.VMEM)
    return pl.pallas_call(
        body,
        out_shape=[jax.ShapeDtypeStruct(s, t) for s, t in outs],
        in_specs=[pl.BlockSpec(memory_space=pltpu.SMEM)] * smem + [vmem] * (len(args) - smem),
        out_specs=[vmem] * len(outs),
        scratch_shapes=[pltpu.VMEM(s, t) for s, t in scratch],
        compiler_params=pltpu.CompilerParams(vmem_limit_bytes=44 * 1024 * 1024),
        cost_estimate=pl.CostEstimate(flops=flops, bytes_accessed=traffic, transcendentals=0),
    )(*args)


def ranks(row):
    column = jnp.transpose(jnp.broadcast_to(row, (8, TOK)))[:, 0:1]
    across = jnp.sum((column < row).astype(F32), axis=0, keepdims=True)
    down = jnp.sum((row < column).astype(F32), axis=1, keepdims=True)
    return column, across, down


def sort_body(route_ref, x_ref, g_ref, out_ref):
    for m in range(2):
        column, across, down = ranks(route_ref[m : m + 1, :].astype(F32))
        place = lax.broadcasted_iota(jnp.int32, (TOK, TOK), 0).astype(F32)
        pick = (place == across).astype(BF)
        out_ref[m, :, 0:32, :] = nn(pick, x_ref[m]).astype(BF).reshape(ROWS, 32, 128)
        out_ref[m, :, 32:64, :] = nn(pick, g_ref[m]).astype(BF).reshape(ROWS, 32, 128)
        slot = column - jnp.floor(column * (1.0 / TOK)) * TOK
        high = jnp.floor(slot * (1.0 / 16))
        low = slot - high * 16
        group = jnp.floor(down * (1.0 / 32))
        inner = down - group * 32
        lane = lax.broadcasted_iota(jnp.int32, (TOK, 128), 1).astype(F32)
        spread = jnp.where(lane == inner, high, jnp.where(lane == inner + 32, low, 0.0)).astype(BF)
        owner = jnp.floor(across * (1.0 / 32))
        member = (lax.broadcasted_iota(jnp.int32, (ROWS, TOK), 0).astype(F32) == owner).astype(BF)
        codes = nn(member, spread).astype(BF)
        out_ref[m, :, 64:72, :] = jnp.broadcast_to(codes[:, None, :], (ROWS, 8, 128))


def unsort_body(route_ref, home_ref, out_ref):
    for m in range(2):
        _, _, down = ranks(route_ref[m : m + 1, :].astype(F32))
        lane = lax.broadcasted_iota(jnp.int32, (TOK, TOK), 1).astype(F32)
        pick = (lane == down).astype(BF)
        total = home_ref[:, m, 0].astype(F32)
        for x in range(1, 4):
            total = total + home_ref[:, m, x].astype(F32)
        out_ref[m] = nn(pick, total.astype(BF).reshape(TOK, 128)).astype(BF)


def gather_features(full_ref, x, blocks):
    for k, block in enumerate(blocks):
        source = lax.rem(x + 4 - k, 4)
        for y in range(2):
            at = pl.multiple_of(y * 512 + source * 128, 128)
            full_ref[:, pl.ds(at, 128)] = block[y]


def split_features(part_ref, x, rows, extra, own_ref, send_refs):
    for y in range(2):
        at = pl.multiple_of(y * 512 + x * 128, 128)
        own_ref[y, rows, :] = part_ref[:, pl.ds(at, 128)] + extra[y, rows, :].astype(F32)
        for k in range(1, 4):
            at = pl.multiple_of(y * 512 + lax.rem(x + k, 4) * 128, 128)
            send_refs[k - 1][y, rows, :] = part_ref[:, pl.ds(at, 128)].astype(BF)


def gather_early(where_ref, blocks, qkv_ref, o_ref):
    z, y, core = where_ref[1], where_ref[2], where_ref[3]
    for other in range(2):
        for dz in range(4):
            for dy in range(4):
                from_z = lax.rem(z + 4 - dz, 4)
                from_y = lax.rem(y + 4 - dy, 4)
                from_core = core if other == 0 else 1 - core
                at = pl.multiple_of((from_z * 4 + (from_y // 2) * 2 + from_core) * 64, 64)
                y_lo = lax.rem(from_y, 2)
                block = blocks[other * 4 + dz]
                qkv_ref[y_lo, pl.ds(at, 64), :] = block[dy, :, 0:512]
                o_ref[y_lo, pl.ds(at, 64), :] = block[dy, :, 512:768]


def norm_rope(proj, gain, cosine, sine):
    inv = lax.rsqrt(jnp.mean(proj * proj, axis=-1, keepdims=True) + EPSILON)
    normed = proj * inv * gain
    return normed * cosine + pltpu.roll(normed, 64, 1) * sine


def bias_of(table_ref, bias_ref):
    columns = jnp.transpose(table_ref[...])
    slot_row = table_ref[0:1, :]
    allowed = (slot_row <= columns[:, 0:1]) & (slot_row >= columns[:, 1:2])
    bias_ref[...] = jnp.where(allowed, 0.0, NEGATIVE)


def attend_body(
    where_ref, x0, x1, x2, x3, w0, w1, w2, w3, v0, v1, v2, v3, table_ref, cos_ref, sin_ref, gain_ref, qg_ref, kg_ref,
    own_ref, send1, send2, send3, full_ref, proj_ref, q_ref, k_ref, v_ref, a_ref, lse_ref,
    qkv_ref, o_ref, bias_ref, part_ref,
):
    x = where_ref[0]
    gather_features(full_ref, x, (x0, x1, x2, x3))
    gather_early(where_ref, (w0, w1, w2, w3, v0, v1, v2, v3), qkv_ref, o_ref)
    bias_of(table_ref, bias_ref)

    def project(i, carry):
        rows = pl.ds(pl.multiple_of(i * TILE, TILE), TILE)
        value = full_ref[rows, :].astype(F32)
        inv = lax.rsqrt(jnp.mean(value * value, axis=-1, keepdims=True) + EPSILON)
        normed = (value * inv * gain_ref[...]).astype(BF)
        cosine, sine = cos_ref[rows, :], sin_ref[rows, :]
        for y in range(2):
            out = nn(normed, qkv_ref[y])
            proj_ref[y, rows, :] = out[:, 0:384]
            for h in range(2):
                lanes = slice(h * 128, h * 128 + 128)
                q_ref[y, rows, lanes] = norm_rope(out[:, lanes], qg_ref[...], cosine, sine).astype(BF)
            k_ref[y, rows, :] = norm_rope(out[:, 256:384], kg_ref[...], cosine, sine).astype(BF)
            v_ref[y, rows, :] = out[:, 384:512].astype(BF)
        return carry

    lax.fori_loop(0, TOK // TILE, project, 0)

    def attend(i, carry):
        rows = pl.ds(pl.multiple_of(i * TILE, TILE), TILE)
        bias = bias_ref[rows, :]
        for y in range(2):
            for h in range(2):
                lanes = slice(h * 128, h * 128 + 128)
                scores = nt(q_ref[y, rows, lanes], k_ref[y]) * SCALE + bias
                top = jnp.max(scores, axis=-1, keepdims=True)
                power = jnp.exp(scores - top)
                total = jnp.sum(power, axis=-1, keepdims=True)
                weights = (power / total).astype(BF)
                a_ref[y, rows, lanes] = nn(weights, v_ref[y]).astype(BF)
                lse_ref[y * 2 + h, rows, :] = top + jnp.log(total)
        part_ref[...] = nt(a_ref[0, rows, :], o_ref[0]) + nt(a_ref[1, rows, :], o_ref[1])
        split_features(part_ref, x, rows, x0, own_ref, (send1, send2, send3))
        return carry

    lax.fori_loop(0, TOK // TILE, attend, 0)


def feed_body(
    where_ref, h0, h1, h2, h3, g0, g1, g2, g3, w_ref, v_ref, gain_ref,
    own_ref, send1, send2, send3, dy_ref, n_ref, hid_ref, dgate_ref, dup_ref, wd_ref, sum_ref,
    full_ref, wg_ref, wu_ref, part_ref,
):
    x, core = where_ref[0], where_ref[3]
    gather_features(full_ref, x, (h0, h1, h2, h3))
    gather_features(dy_ref, x, (g0, g1, g2, g3))
    for other, source in enumerate((w_ref, v_ref)):
        from_core = core if other == 0 else 1 - core
        for k in range(8):
            at = pl.multiple_of((k * 2 + from_core) * 64, 64)
            for y in range(2):
                wg_ref[y, pl.ds(at, 64), :] = source[k * 2 + y, :, 0:384]
                wu_ref[y, pl.ds(at, 64), :] = source[k * 2 + y, :, 384:768]
                wd_ref[y, pl.ds(at, 64), :] = source[k * 2 + y, :, 768:1152]
    sum_ref[...] = jnp.zeros_like(sum_ref)

    def step(i, carry):
        rows = pl.ds(pl.multiple_of(i * TILE, TILE), TILE)
        value = full_ref[rows, :].astype(F32)
        inv = lax.rsqrt(jnp.mean(value * value, axis=-1, keepdims=True) + EPSILON)
        hat = value * inv
        normed = (hat * gain_ref[...]).astype(BF)
        n_ref[rows, :] = normed
        delta = dy_ref[rows, :]
        for y in range(2):
            gate = nn(normed, wg_ref[y])
            up = nn(normed, wu_ref[y])
            down = nn(delta, wd_ref[y])
            sigma = 1.0 / (1.0 + jnp.exp(-gate))
            act = gate * sigma
            hid_ref[y, rows, :] = (act * up).astype(BF)
            dgate = (down * up * sigma * (1.0 + gate * (1.0 - sigma))).astype(BF)
            dup = (down * act).astype(BF)
            dgate_ref[y, rows, :] = dgate
            dup_ref[y, rows, :] = dup
            out = nt(dgate, wg_ref[y]) + nt(dup, wu_ref[y])
            if y == 0:
                part_ref[...] = out
            else:
                out = part_ref[...] + out
                sum_ref[0:1, :] += jnp.sum(out * hat, axis=0, keepdims=True)
                scaled = out * gain_ref[...]
                inner = jnp.mean(scaled * hat, axis=-1, keepdims=True)
                part_ref[...] = inv * (scaled - hat * inner)
        split_features(part_ref, x, rows, g0, own_ref, (send1, send2, send3))
        return carry

    lax.fori_loop(0, TOK // TILE, step, 0)


def store_grad(value_ref, core, chunk, y, lanes, keep_ref, give_ref):
    for k in range(2):
        mine = pl.multiple_of((k * 2 + core) * 64, 64)
        theirs = pl.multiple_of((k * 2 + 1 - core) * 64, 64)
        keep_ref[(chunk * 2 + k) * 2 + y, :, lanes] = value_ref[pl.ds(mine, 64), :]
        give_ref[(chunk * 2 + k) * 2 + y, :, lanes] = value_ref[pl.ds(theirs, 64), :]


def feed_grad_body(
    where_ref, hid_ref, dgate_ref, dup_ref, n_ref, dy_ref, wd_ref, resid_ref,
    back_ref, keep_ref, give_ref,
    part_ref, chunk_ref,
):
    x, core = where_ref[0], where_ref[3]

    def step(i, carry):
        rows = pl.ds(pl.multiple_of(i * TILE, TILE), TILE)
        part_ref[...] = nt(hid_ref[0, rows, :], wd_ref[0]) + nt(hid_ref[1, rows, :], wd_ref[1])
        for y in range(2):
            part_ref[:, pl.ds(pl.multiple_of(y * 512 + x * 128, 128), 128)] += resid_ref[y, rows, :]
        places = pl.ds(pl.multiple_of(i * (TILE // 32), TILE // 32), TILE // 32)
        for c in range(8):
            back_ref[places, c] = (
                part_ref[:, c * 128 : c * 128 + 128].astype(BF).reshape(TILE // 32, 32, 128)
            )
        return carry

    lax.fori_loop(0, TOK // TILE, step, 0)
    def grads(j, carry):
        lanes = pl.ds(pl.multiple_of(j * 256, 256), 256)
        normed = n_ref[:, lanes]
        delta = dy_ref[:, lanes]
        for y in range(2):
            for n, (left, right) in enumerate(
                ((normed, dgate_ref), (normed, dup_ref), (delta, hid_ref))
            ):
                chunk_ref[...] = tn(left, right[y]).astype(BF)
                store_grad(chunk_ref, core, j, y, slice(n * 384, n * 384 + 384), keep_ref, give_ref)
        return carry

    lax.fori_loop(0, 4, grads, 0)


def attend_back_body(
    where_ref, d0, d1, d2, d3, w0, w1, w2, w3, v0, v1, v2, v3, full_ref, proj_ref, q_ref, k_ref, v_ref, lse_ref,
    table_ref, cos_ref, sin_ref, gain_ref, qg_ref, kg_ref, resid_ref,
    back_ref, delta_ref, dproj_ref, n_ref, sum_ref, head_ref,
    qkv_ref, o_ref, bias_ref, part_ref, dk_ref, dv_ref, da_ref,
):
    x = where_ref[0]
    gather_features(delta_ref, x, (d0, d1, d2, d3))
    gather_early(where_ref, (w0, w1, w2, w3, v0, v1, v2, v3), qkv_ref, o_ref)
    bias_of(table_ref, bias_ref)
    sum_ref[...] = jnp.zeros_like(sum_ref)
    head_ref[...] = jnp.zeros_like(head_ref)
    dk_ref[...] = jnp.zeros_like(dk_ref)
    dv_ref[...] = jnp.zeros_like(dv_ref)

    def back(rotated, proj, gain, rows, at):
        turned = rotated * cos_ref[rows, :] - pltpu.roll(rotated, 64, 1) * sin_ref[rows, :]
        inv = lax.rsqrt(jnp.mean(proj * proj, axis=-1, keepdims=True) + EPSILON)
        hat = proj * inv
        head_ref[at : at + 1, :] += jnp.sum(turned * hat, axis=0, keepdims=True)
        scaled = turned * gain
        return (inv * (scaled - hat * jnp.mean(scaled * hat, axis=-1, keepdims=True))).astype(BF)

    def attend(i, carry):
        rows = pl.ds(pl.multiple_of(i * TILE, TILE), TILE)
        bias = bias_ref[rows, :]
        for y in range(2):
            da_ref[...] = nn(delta_ref[rows, :], o_ref[y]).astype(BF)
            for h in range(2):
                lanes = slice(h * 128, h * 128 + 128)
                query = q_ref[y, rows, lanes]
                da = da_ref[:, lanes]
                scores = nt(query, k_ref[y]) * SCALE + bias
                soft = jnp.exp(scores - lse_ref[y * 2 + h, rows, :])
                dp = nt(da, v_ref[y])
                dv_ref[y] += tn(soft.astype(BF), da)
                ds = (soft * (dp - jnp.sum(dp * soft, axis=-1, keepdims=True))).astype(BF)
                dk_ref[y] += tn(ds, query)
                dq = nn(ds, k_ref[y]) * SCALE
                dproj_ref[y, rows, lanes] = back(dq, proj_ref[y, rows, lanes], qg_ref[...], rows, 0)
        return carry

    lax.fori_loop(0, TOK // TILE, attend, 0)

    def project(i, carry):
        rows = pl.ds(pl.multiple_of(i * TILE, TILE), TILE)
        value = full_ref[rows, :].astype(F32)
        inv = lax.rsqrt(jnp.mean(value * value, axis=-1, keepdims=True) + EPSILON)
        hat = value * inv
        n_ref[rows, :] = (hat * gain_ref[...]).astype(BF)
        for y in range(2):
            dproj_ref[y, rows, 256:384] = back(
                dk_ref[y, rows, :] * SCALE, proj_ref[y, rows, 256:384], kg_ref[...], rows, 1
            )
            dproj_ref[y, rows, 384:512] = dv_ref[y, rows, :].astype(BF)
        out = nt(dproj_ref[0, rows, :], qkv_ref[0]) + nt(dproj_ref[1, rows, :], qkv_ref[1])
        sum_ref[0:1, :] += jnp.sum(out * hat, axis=0, keepdims=True)
        scaled = out * gain_ref[...]
        inner = jnp.mean(scaled * hat, axis=-1, keepdims=True)
        part_ref[...] = inv * (scaled - hat * inner)
        for y in range(2):
            part_ref[:, pl.ds(pl.multiple_of(y * 512 + x * 128, 128), 128)] += resid_ref[y, rows, :]
        places = pl.ds(pl.multiple_of(i * (TILE // 32), TILE // 32), TILE // 32)
        for c in range(8):
            back_ref[places, c] = (
                part_ref[:, c * 128 : c * 128 + 128].astype(BF).reshape(TILE // 32, 32, 128)
            )
        return carry

    lax.fori_loop(0, TOK // TILE, project, 0)


def attend_grad_body(
    where_ref, dproj_ref, n_ref, delta_ref, a_ref, keep_ref, give_ref, wide_ref, thin_ref
):
    core = where_ref[3]

    def grads(j, carry):
        lanes = pl.ds(pl.multiple_of(j * 256, 256), 256)
        normed = n_ref[:, lanes]
        delta = delta_ref[:, lanes]
        for y in range(2):
            wide_ref[...] = tn(normed, dproj_ref[y]).astype(BF)
            store_grad(wide_ref, core, j, y, slice(0, 512), keep_ref, give_ref)
            thin_ref[...] = tn(delta, a_ref[y]).astype(BF)
            store_grad(thin_ref, core, j, y, slice(512, 768), keep_ref, give_ref)
        return carry

    lax.fori_loop(0, 4, grads, 0)


def spread(value):
    return [value] + [shift(value, dx=k) for k in (1, 2, 3)]


def collect(sends):
    return [shift(sends[k - 1], dx=k) for k in (1, 2, 3)]


def add_up(own, parts):
    return own + (parts[0].astype(F32) + parts[1].astype(F32) + parts[2].astype(F32))


def exchange(blocks, groups):
    return lax.all_to_all(blocks, BOTH, 0, 0, axis_index_groups=groups, tiled=True)


FEATURES = (2, TOK, 128)


fence = lax.optimization_barrier


def take(blocks, at):
    return lax.dynamic_index_in_dim(blocks, at % 4, 0, keepdims=False)


def blocks_z(where, keep, other):
    shape = (4, 4) + keep.shape[1:]
    keep, other = keep.reshape(shape), other.reshape(shape)

    def block(k):
        return take(keep, where[1] + k).astype(F32) + take(other, where[1] + k).astype(F32)

    return block(0), [block(k).astype(BF) for k in (1, 2, 3)]


def reduce_y(where, total):
    return add_up(
        take(total, where[2]), [shift(take(total, where[2] + k).astype(BF), dy=k) for k in (1, 2, 3)]
    )


def body(
    layer_input,
    out_grad,
    token_route,
    seq_lengths,
    positions,
    attn_gain,
    query_weight,
    key_weight,
    value_weight,
    query_gain,
    key_gain,
    out_weight,
    mlp_gain,
    gate_weight,
    up_weight,
    down_weight,
):
    row = lax.axis_index("row")
    col = lax.axis_index("col")
    y_lo = col // 4
    x = col % 4
    where = jnp.stack([x, row // 4, ((row // 2) % 2) * 2 + y_lo, row % 2]).astype(jnp.int32)
    places = jnp.arange(TOK, dtype=jnp.int32)
    gain_one = attn_gain.astype(F32)[None, :]
    gain_two = mlp_gain.astype(F32)[None, :]
    query_scale = query_gain.astype(F32)[None, :]
    key_scale = key_gain.astype(F32)[None, :]

    early = jnp.concatenate([query_weight, key_weight, value_weight, out_weight.T], axis=1)
    early = [early] + [shift(early, dy=k) for k in (1, 2, 3)]

    (sorted_rows,) = call(
        sort_body,
        [((2, ROWS, 72, 128), BF)],
        [],
        2 * 2 * 2 * TOK * TOK * 128,
        4 << 20,
        token_route,
        layer_input,
        out_grad,
    )
    sorted_rows, early = fence((sorted_rows, early))
    arrived = exchange(sorted_rows.reshape(32, 72, 128), TEAM).reshape(2, ROWS, 72, 128)
    early = jnp.stack(early)
    early = [early] + [shift(early, dz=k) for k in (1, 2, 3)]
    inputs = spread(arrived[:, :, 0:32, :].reshape(FEATURES))
    codes = arrived[0, :, 64, 0:64].astype(F32)
    slots = (codes[:, 0:32] * 16 + codes[:, 32:64]).astype(jnp.int32).reshape(TOK)

    late = jnp.concatenate([gate_weight, up_weight, down_weight.T], axis=1)
    late, early, arrived = fence((late, early, arrived))
    late = jnp.broadcast_to(late[None], (16, 64, 1152))
    grads = spread(arrived[:, :, 32:64, :].reshape(FEATURES))
    early = early + [shift(e, dcore=1) for e in early]
    late, early, inputs = fence((late, early, inputs))
    late = exchange(late, PLANE)

    lengths = lax.dynamic_index_in_dim(seq_lengths, y_lo, 0, keepdims=False)[0]
    bound_one = lengths[0]
    bound_two = bound_one + lengths[1]
    bound_three = bound_two + lengths[2]
    first = jnp.where(slots >= bound_one, bound_one, 0)
    first = jnp.where(slots >= bound_two, bound_two, first)
    first = jnp.where(slots >= bound_three, bound_three, first)
    table = jnp.concatenate(
        [slots.astype(F32)[None], first.astype(F32)[None], jnp.zeros((6, TOK), F32)], axis=0
    )
    my_positions = lax.dynamic_index_in_dim(positions, y_lo, 0, keepdims=False)
    position = jnp.sum(
        jnp.where(slots[:, None] == places[None, :], my_positions[None, :], 0), axis=1
    )
    freq_steps = jnp.arange(0, HEAD_SIZE, 2).astype(F32) / HEAD_SIZE
    frequency = 1.0 / ROPE_BASE**freq_steps
    angles = position.astype(F32)[:, None] * frequency[None, :]
    cosine = jnp.cos(angles)
    sine = jnp.sin(angles)
    cosine = jnp.concatenate([cosine, cosine], axis=-1)
    sine = jnp.concatenate([-sine, sine], axis=-1)

    own, *sends, full, proj, q_rows, k_rows, v_rows, attended, lse = call(
        attend_body,
        [(FEATURES, F32), (FEATURES, BF), (FEATURES, BF), (FEATURES, BF), ((TOK, D), BF), ((2, TOK, 384), F32),
         ((2, TOK, 256), BF), (FEATURES, BF), (FEATURES, BF), ((2, TOK, 256), BF), ((4, TOK, 1), F32)],
        [((2, D, 512), BF), ((2, D, 256), BF), ((TOK, TOK), F32), ((TILE, D), F32)],
        3 << 30,
        16 << 20,
        where, *inputs, *early, table, cosine, sine, gain_one, query_scale, key_scale,
        smem=1,
    )
    sends, grads = fence((sends, grads))
    parts, late = fence((collect(sends), late))
    resid = add_up(own, parts)
    wide = spread(resid.astype(BF))
    late = [late, shift(late, dcore=1)]

    own, *sends, delta_out, normed_two, hidden, dgate, dup, down_full, mlp_sum = call(
        feed_body,
        [(FEATURES, F32), (FEATURES, BF), (FEATURES, BF), (FEATURES, BF), ((TOK, D), BF), ((TOK, D), BF),
         ((2, TOK, 384), BF), ((2, TOK, 384), BF), ((2, TOK, 384), BF), ((2, D, 384), BF), ((8, D), F32)],
        [((TOK, D), BF), ((2, D, 384), BF), ((2, D, 384), BF), ((TILE, D), F32)],
        5 << 30,
        16 << 20,
        where, *wide, *grads, *late, gain_two,
        smem=1,
    )
    parts = collect(sends)
    back, keep, give = call(
        feed_grad_body,
        [((ROWS, 8, 32, 128), BF), ((16, 64, 1152), BF), ((16, 64, 1152), BF)],
        [((TILE, D), F32), ((256, 384), BF)],
        4 << 30,
        16 << 20,
        where, hidden, dgate, dup, normed_two, delta_out, down_full, resid,
        smem=1,
    )
    parts, back, keep, give = fence((parts, back, keep, give))
    resid_delta = add_up(own, parts)
    wide = spread(resid_delta.astype(BF))
    output_home = exchange(back.reshape(128, 32, 128), None)
    late_own, late_sends = blocks_z(where, keep, shift(give, dcore=1))
    wide, late_sends = fence((wide, late_sends))
    late_parts = [shift(late_sends[k - 1], dz=k) for k in (1, 2, 3)]

    back, delta_wide, dproj, normed_one, attn_sum, head_sum = call(
        attend_back_body,
        [((ROWS, 8, 32, 128), BF), ((TOK, D), BF), ((2, TOK, 512), BF), ((TOK, D), BF), ((8, D), F32), ((8, 128), F32)],
        [((2, D, 512), BF), ((2, D, 256), BF), ((TOK, TOK), F32), ((TILE, D), F32), (FEATURES, F32), (FEATURES, F32),
         ((TILE, 256), BF)],
        5 << 30,
        16 << 20,
        where, *wide, *early, full, proj, q_rows, k_rows, v_rows, lse, table, cosine, sine, gain_one, query_scale,
        key_scale, resid_delta,
        smem=1,
    )
    back, delta_wide, dproj, normed_one, attn_sum, head_sum, output_home, late_parts = fence(
        (back, delta_wide, dproj, normed_one, attn_sum, head_sum, output_home, late_parts)
    )
    input_home = exchange(back.reshape(128, 32, 128), None)
    late_total = reduce_y(where, add_up(late_own, late_parts))
    keep, give = call(
        attend_grad_body,
        [((16, 64, 768), BF), ((16, 64, 768), BF)],
        [((256, 512), BF), ((256, 256), BF)],
        2 << 30,
        8 << 20,
        where, dproj, normed_one, delta_wide, attended,
        smem=1,
    )

    early_own, early_sends = blocks_z(where, keep, shift(give, dcore=1))
    early_parts = [shift(early_sends[k - 1], dz=k) for k in (1, 2, 3)]
    early_total = reduce_y(where, add_up(early_own, early_parts))

    def unsort(home):
        return call(
            unsort_body,
            [((2, TOK, 128), BF)],
            [],
            2 * 2 * TOK * TOK * 128,
            2 << 20,
            token_route,
            home.reshape(ROWS, 2, 4, 32, 128),
        )[0]

    layer_output = unsort(output_home)
    input_grad = unsort(input_home)
    gains = jnp.concatenate(
        [attn_sum[0:1].reshape(8, 128), mlp_sum[0:1].reshape(8, 128), head_sum], axis=0
    )
    gains = gains + shift(gains, dcore=1)
    for axis in ("dx", "dy", "dz"):
        gains = gains + shift(gains, **{axis: 1}) + shift(gains, **{axis: 2}) + shift(gains, **{axis: 3})
    return (
        layer_output,
        input_grad,
        gains[0:8].reshape(D),
        early_total[:, 0:256],
        early_total[:, 256:384],
        early_total[:, 384:512],
        gains[16],
        gains[17],
        early_total[:, 512:768].T,
        gains[8:16].reshape(D),
        late_total[:, 0:384],
        late_total[:, 384:768],
        late_total[:, 768:1152].T,
    )


def solution(mesh):
    in_specs = (
        P(None, "row", "col"),
        P(None, "row", "col"),
        P(None, "row"),
        P(None, "row", None),
        P(None, "row"),
        P(),
        P("row", "col"),
        P("row", "col"),
        P("row", "col"),
        P(),
        P(),
        P("col", "row"),
        P(),
        P("row", "col"),
        P("row", "col"),
        P("col", "row"),
    )
    out_specs = (
        P(None, "row", "col"),
        P(None, "row", "col"),
        P(),
        P("row", "col"),
        P("row", "col"),
        P("row", "col"),
        P(),
        P(),
        P("col", "row"),
        P(),
        P("row", "col"),
        P("row", "col"),
        P("col", "row"),
    )
    return jax.shard_map(body, mesh=mesh, in_specs=in_specs, out_specs=out_specs, check_vma=False)
```

```python
import functools
import math

import jax
import jax.numpy as jnp
from jax import lax
from jax.experimental import pallas as pl
from jax.experimental.pallas import tpu as pltpu
from jax.sharding import PartitionSpec as P

D = 1024
HEAD_SIZE = 128
EPSILON = 1e-06
ROPE_BASE = 1000000.0
NEGATIVE = -1e30
BOTH = ("row", "col")
ROWS = 16
TOK = 512
TILE = 256
SENT = 40
BF = jnp.bfloat16
F32 = jnp.float32
SCALE = 1.0 / math.sqrt(HEAD_SIZE)


def flat(row, col):
    return row * 8 + col


def spot(z, y, core, x):
    return flat(z * 4 + (y // 2) * 2 + core, (y % 2) * 4 + x)


SQUAD = [
    [flat(2 * k + core, 4 * y_lo + x) for k in range(8) for y_lo in range(2) for core in range(2)]
    for x in range(4)
]
SAME_X = [[flat(row, 4 * y_lo + x) for x in range(4)] for row in range(ROWS) for y_lo in range(2)]
TEAM = [[flat(row, 4 * y_lo + x) for y_lo in range(2) for row in range(ROWS)] for x in range(4)]


def moves(dz=0, dy=0, dcore=0, dx=0):
    return [
        (spot(z, y, core, x), spot((z + dz) % 4, (y + dy) % 4, core ^ dcore, (x + dx) % 4))
        for z in range(4)
        for y in range(4)
        for core in range(2)
        for x in range(4)
    ]


def shift(value, **step):
    return lax.ppermute(value, BOTH, moves(**step))


def dot(a, b, dims):
    return lax.dot_general(a, b, (dims, ((), ())), preferred_element_type=F32)


def nn(a, b):
    return dot(a, b, ((1,), (0,)))


def nt(a, b):
    return dot(a, b, ((1,), (1,)))


def tn(a, b):
    return dot(a, b, ((0,), (0,)))


def call(body, ins, outs, scratch, copies, flops, traffic, *args, limit=60):
    spaces = {"s": pltpu.SMEM, "v": pltpu.VMEM, "h": pl.ANY}
    return pl.pallas_call(
        body,
        out_shape=[jax.ShapeDtypeStruct(s, t) for _, s, t in outs],
        in_specs=[pl.BlockSpec(memory_space=spaces[k]) for k in ins],
        out_specs=[pl.BlockSpec(memory_space=spaces[k]) for k, _, _ in outs],
        scratch_shapes=[pltpu.VMEM(s, t) for s, t in scratch] + [pltpu.SemaphoreType.DMA((copies,))],
        compiler_params=pltpu.CompilerParams(vmem_limit_bytes=limit * 1024 * 1024),
        cost_estimate=pl.CostEstimate(flops=flops >> 6, bytes_accessed=traffic >> 6, transcendentals=0),
    )(*args)


class Mover:
    def __init__(self, sems):
        self.sems = sems
        self.used = 0

    def start(self, source, target):
        copy = pltpu.make_async_copy(source, target, self.sems.at[self.used])
        self.used += 1
        copy.start()
        return copy


def wait(copies):
    for copy in copies:
        copy.wait()


def ranks(row):
    column = jnp.transpose(jnp.broadcast_to(row, (8, TOK)))[:, 0:1]
    across = jnp.sum((column < row).astype(F32), axis=0, keepdims=True)
    down = jnp.sum((row < column).astype(F32), axis=1, keepdims=True)
    return column, across, down


def sort_body(route_ref, x_hbm, g_hbm, out_ref, x_ref, g_ref, sems):
    mover = Mover(sems)
    loads = [mover.start(x_hbm, x_ref), mover.start(g_hbm, g_ref)]
    for m in range(2):
        column, across, down = ranks(route_ref[m : m + 1, :].astype(F32))
        place = lax.broadcasted_iota(jnp.int32, (TOK, TOK), 0).astype(F32)
        pick = (place == across).astype(BF)
        slot = column - jnp.floor(column * (1.0 / TOK)) * TOK
        high = jnp.floor(slot * (1.0 / 16))
        low = slot - high * 16
        group = jnp.floor(down * (1.0 / 32))
        inner = down - group * 32
        lane = lax.broadcasted_iota(jnp.int32, (TOK, 128), 1).astype(F32)
        spread = jnp.where(lane == inner, high, jnp.where(lane == inner + 32, low, 0.0)).astype(BF)
        owner = jnp.floor(across * (1.0 / 32))
        member = (lax.broadcasted_iota(jnp.int32, (ROWS, TOK), 0).astype(F32) == owner).astype(BF)
        codes = nn(member, spread).astype(BF)
        out_ref[m, :, 64:72, :] = jnp.broadcast_to(codes[:, None, :], (ROWS, 8, 128))
        if m == 0:
            wait(loads)
        out_ref[m, :, 0:32, :] = nn(pick, x_ref[m]).astype(BF).reshape(ROWS, 32, 128)
        out_ref[m, :, 32:64, :] = nn(pick, g_ref[m]).astype(BF).reshape(ROWS, 32, 128)


def unsort_body(route_ref, home_hbm, y_ref, dx_ref, home_ref, sems):
    mover = Mover(sems)
    loads = [mover.start(home_hbm.at[:, m], home_ref.at[m]) for m in range(2)]
    for m in range(2):
        _, _, down = ranks(route_ref[m : m + 1, :].astype(F32))
        lane = lax.broadcasted_iota(jnp.int32, (TOK, TOK), 1).astype(F32)
        pick = (lane == down).astype(BF)
        loads[m].wait()
        total = home_ref[m, :, 0, 0:32, :].astype(F32)
        for x in range(1, 4):
            total = total + home_ref[m, :, x, 0:32, :].astype(F32)
        dx_ref[m] = nn(pick, total.astype(BF).reshape(TOK, 128)).astype(BF)
        output = home_ref[m, :, :, 32:40, :].astype(F32).reshape(TOK, 128).astype(BF)
        y_ref[m] = nn(pick, output).astype(BF)


def features_of(mover, blocks, x, full_ref):
    return [
        mover.start(block.at[y], full_ref.at[:, mine(lax.rem(x + 4 - k, 4), y)])
        for k, block in enumerate(blocks)
        for y in range(2)
    ]


def features_in_order(mover, blocks, full_ref):
    return [
        mover.start(blocks.at[k, y], full_ref.at[:, pl.ds(y * 512 + k * 128, 128)])
        for k in range(4)
        for y in range(2)
    ]


def weight(w_ref, y, lanes):
    value = w_ref[(slice(None),) * (len(w_ref.shape) - 4) + (y, slice(None), slice(None), lanes)]
    return value.reshape(D, value.shape[-1])


def mine(x, y):
    return pl.ds(pl.multiple_of(y * 512 + x * 128, 128), 128)


def split_features(part_ref, rows, send_ref):
    for k in range(4):
        for y in range(2):
            lanes = slice(y * 512 + k * 128, y * 512 + k * 128 + 128)
            send_ref[k, y, rows, :] = part_ref[:, lanes].astype(BF)


def merge_body(got_ref, base_ref, total_ref, wide_ref, sems):
    for y in range(2):
        total = base_ref[y].astype(F32)
        for k in range(4):
            total = total + got_ref[k, y].astype(F32)
        total_ref[y] = total
        for k in range(4):
            wide_ref[k, y] = total.astype(BF)


def sent_tiles(send_ref, send_hbm, sems):
    return [
        pltpu.make_async_copy(
            send_ref.at[:, :, pl.ds(i * TILE, TILE)], send_hbm.at[:, :, pl.ds(i * TILE, TILE)], sems.at[SENT + i]
        )
        for i in range(TOK // TILE)
    ]


def norm_rope(proj, gain, cosine, sine):
    inv = lax.rsqrt(jnp.mean(proj * proj, axis=-1, keepdims=True) + EPSILON)
    normed = proj * inv * gain
    return normed * cosine + pltpu.roll(normed, 64, 1) * sine


def bias_of(table_ref, bias_ref):
    columns = jnp.transpose(table_ref[...])
    slot_row = table_ref[0:1, :]
    allowed = (slot_row <= columns[:, 0:1]) & (slot_row >= columns[:, 1:2])
    bias_ref[...] = jnp.where(allowed, 0.0, NEGATIVE)


def tile(i):
    return pl.ds(pl.multiple_of(i * TILE, TILE), TILE)


def attend_body(
    x_hbm, w_hbm, table_hbm, rope_hbm, gain_hbm,
    send_hbm, full_hbm, n_hbm, proj_hbm, q_hbm, k_hbm, v_hbm, a_hbm, lse_hbm,
    full_ref, w_ref, table_ref, rope_ref, gain_ref, bias_ref, part_ref, n_ref, proj_ref, q_ref, k_ref, v_ref, a_ref,
    lse_ref, send_ref, sems,
):
    mover = Mover(sems)
    cut = pl.ds(0, 512)
    rest = pl.ds(512, 256)
    first = features_in_order(mover, x_hbm, full_ref) + [mover.start(gain_hbm, gain_ref)]
    load_table = mover.start(table_hbm, table_ref)
    loads = [
        mover.start(w_hbm.at[:, :, :, :, cut], w_ref.at[:, :, :, :, cut]),
        mover.start(rope_hbm, rope_ref),
    ]
    load_rest = mover.start(w_hbm.at[:, :, :, :, rest], w_ref.at[:, :, :, :, rest])
    load_table.wait()
    bias_of(table_ref, bias_ref)
    wait(first)
    stores = [mover.start(full_ref, full_hbm)]

    def norm(i, carry):
        rows = tile(i)
        value = full_ref[rows, :].astype(F32)
        inv = lax.rsqrt(jnp.mean(value * value, axis=-1, keepdims=True) + EPSILON)
        n_ref[rows, :] = (value * inv * gain_ref[0:1, :]).astype(BF)
        return carry

    lax.fori_loop(0, TOK // TILE, norm, 0)
    stores.append(mover.start(n_ref, n_hbm))
    wait(loads)

    def project(i, carry):
        rows = tile(i)
        cosine, sine = rope_ref[rows, 0:128], rope_ref[rows, 128:256]
        for y in range(2):
            out = nn(n_ref[rows, :], weight(w_ref, y, slice(0, 512)))
            proj_ref[y, rows, :] = out[:, 0:384]
            for h in range(2):
                lanes = slice(h * 128, h * 128 + 128)
                q_ref[y, rows, lanes] = norm_rope(
                    out[:, lanes], gain_ref[2:3, 0:128], cosine, sine
                ).astype(BF)
            k_ref[y, rows, :] = norm_rope(
                out[:, 256:384], gain_ref[2:3, 128:256], cosine, sine
            ).astype(BF)
            v_ref[y, rows, :] = out[:, 384:512].astype(BF)
        return carry

    lax.fori_loop(0, TOK // TILE, project, 0)
    stores += [
        mover.start(proj_ref, proj_hbm),
        mover.start(q_ref, q_hbm),
        mover.start(k_ref, k_hbm),
        mover.start(v_ref, v_hbm),
    ]
    load_rest.wait()

    def attend(i, carry):
        rows = tile(i)
        bias = bias_ref[rows, :]
        lane = lax.broadcasted_iota(jnp.int32, (TILE, 128), 1)
        logs = jnp.zeros((TILE, 128), F32)
        for y in range(2):
            for h in range(2):
                lanes = slice(h * 128, h * 128 + 128)
                scores = nt(q_ref[y, rows, lanes], k_ref[y]) * SCALE + bias
                top = jnp.max(scores, axis=-1, keepdims=True)
                power = jnp.exp(scores - top)
                total = jnp.sum(power, axis=-1, keepdims=True)
                weights = (power * (1.0 / total)).astype(BF)
                a_ref[y, rows, lanes] = nn(weights, v_ref[y]).astype(BF)
                logs = jnp.where(lane == y * 2 + h, top + jnp.log(total), logs)
        lse_ref[rows, :] = logs
        return carry

    lax.fori_loop(0, TOK // TILE, attend, 0)
    stores += [mover.start(a_ref, a_hbm), mover.start(lse_ref, lse_hbm)]

    def leave(i, carry):
        rows = tile(i)
        part_ref[...] = nt(a_ref[0, rows, :], weight(w_ref, 0, slice(512, 768))) + nt(
            a_ref[1, rows, :], weight(w_ref, 1, slice(512, 768))
        )
        split_features(part_ref, rows, send_ref)
        pltpu.make_async_copy(send_ref.at[:, :, rows], send_hbm.at[:, :, rows], sems.at[SENT + i]).start()
        return carry

    lax.fori_loop(0, TOK // TILE, leave, 0)
    wait(stores + sent_tiles(send_ref, send_hbm, sems))


def feed_body(
    where_ref, h_hbm, g0, g1, g2, g3, w_hbm, gain_hbm,
    send_hbm, dy_hbm, n_hbm, hid_hbm, dgu_hbm, sum_ref,
    full_ref, w_ref, part_ref, gain_ref, dy_ref, n_ref, hid_ref, dgu_ref, send_ref, sems,
):
    mover = Mover(sems)
    cut = pl.ds(0, 768)
    rest = pl.ds(768, 384)
    loads = features_in_order(mover, h_hbm, full_ref)
    loads.append(mover.start(gain_hbm, gain_ref))
    loads.append(mover.start(w_hbm.at[:, :, :, :, cut], w_ref.at[:, :, :, :, cut]))
    later = features_of(mover, (g0, g1, g2, g3), where_ref[0], dy_ref)
    later.append(mover.start(w_hbm.at[:, :, :, :, rest], w_ref.at[:, :, :, :, rest]))
    sum_ref[...] = jnp.zeros_like(sum_ref)
    wait(loads + later)
    stores = [mover.start(dy_ref, dy_hbm)]

    def step(i, carry):
        rows = tile(i)
        gain = gain_ref[1:2, :]
        value = full_ref[rows, :].astype(F32)
        inv = lax.rsqrt(jnp.mean(value * value, axis=-1, keepdims=True) + EPSILON)
        hat = value * inv
        normed = (hat * gain).astype(BF)
        n_ref[rows, :] = normed
        delta = dy_ref[rows, :]
        for y in range(2):
            gate = nn(normed, weight(w_ref, y, slice(0, 384)))
            up = nn(normed, weight(w_ref, y, slice(384, 768)))
            down = nn(delta, weight(w_ref, y, slice(768, 1152)))
            sigma = jax.nn.sigmoid(gate)
            act = gate * sigma
            hid_ref[y, rows, :] = (act * up).astype(BF)
            dgu_ref[y, rows, 0:384] = (down * up * sigma * (1.0 + gate * (1.0 - sigma))).astype(BF)
            dgu_ref[y, rows, 384:768] = (down * act).astype(BF)
            out = nt(dgu_ref[y, rows, :], weight(w_ref, y, slice(0, 768)))
            if y == 0:
                part_ref[...] = out
            else:
                out = part_ref[...] + out
                sum_ref[0:1, :] += jnp.sum(out * hat, axis=0, keepdims=True)
                scaled = out * gain
                inner = jnp.mean(scaled * hat, axis=-1, keepdims=True)
                part_ref[...] = inv * (scaled - hat * inner)
        split_features(part_ref, rows, send_ref)
        pltpu.make_async_copy(send_ref.at[:, :, rows], send_hbm.at[:, :, rows], sems.at[SENT + i]).start()
        pltpu.make_async_copy(n_ref.at[rows], n_hbm.at[rows], sems.at[SENT + 2 + i]).start()
        pltpu.make_async_copy(hid_ref.at[:, rows], hid_hbm.at[:, rows], sems.at[SENT + 4 + i]).start()
        pltpu.make_async_copy(dgu_ref.at[:, rows], dgu_hbm.at[:, rows], sems.at[SENT + 6 + i]).start()
        return carry

    lax.fori_loop(0, TOK // TILE, step, 0)
    for i in range(TOK // TILE):
        rows = pl.ds(i * TILE, TILE)
        stores.append(pltpu.make_async_copy(n_ref.at[rows], n_hbm.at[rows], sems.at[SENT + 2 + i]))
        stores.append(pltpu.make_async_copy(hid_ref.at[:, rows], hid_hbm.at[:, rows], sems.at[SENT + 4 + i]))
        stores.append(pltpu.make_async_copy(dgu_ref.at[:, rows], dgu_hbm.at[:, rows], sems.at[SENT + 6 + i]))
    wait(stores + sent_tiles(send_ref, send_hbm, sems))


def store_grad(value_ref, core, chunk, y, lanes, keep_ref, give_ref):
    for k in range(2):
        kept = pl.multiple_of((k * 2 + core) * 64, 64)
        given = pl.multiple_of((k * 2 + 1 - core) * 64, 64)
        keep_ref[(chunk * 2 + k) * 2 + y, 0:64, lanes] = value_ref[pl.ds(kept, 64), :]
        give_ref[(chunk * 2 + k) * 2 + y, 0:64, lanes] = value_ref[pl.ds(given, 64), :]


def feed_grad_body(
    where_ref, hid_hbm, dgu_hbm, n_hbm, dy_hbm, w_hbm, resid_hbm,
    quarter_hbm, keep_hbm, give_hbm,
    hid_ref, dgu_ref, n_ref, dy_ref, w_ref, resid_ref, part_ref, wide_ref, thin_ref, stage_ref, quarter_ref, keep_ref,
    give_ref, sems,
):
    x, core = where_ref[0], where_ref[3]
    mover = Mover(sems)
    first = [
        mover.start(hid_hbm, hid_ref),
        mover.start(w_hbm.at[:, :, :, :, pl.ds(768, 384)], w_ref),
        mover.start(resid_hbm, resid_ref),
    ]
    loads = [
        mover.start(n_hbm, n_ref),
        mover.start(dgu_hbm, dgu_ref),
        mover.start(dy_hbm, dy_ref),
    ]
    wait(first)

    def step(i, carry):
        rows = tile(i)
        part_ref[...] = nt(hid_ref[0, rows, :], weight(w_ref, 0, slice(0, 384))) + nt(
            hid_ref[1, rows, :], weight(w_ref, 1, slice(0, 384))
        )
        for y in range(2):
            part_ref[:, mine(x, y)] += resid_ref[y, rows, :]
        places = pl.ds(pl.multiple_of(i * (TILE // 32), TILE // 32), TILE // 32)
        stage_ref[places] = part_ref[...].reshape(TILE // 32, 4, 8, D)
        return carry

    lax.fori_loop(0, TOK // TILE, step, 0)
    for k in range(4):
        quarter_ref[k] = stage_ref[:, k].reshape(128, D).astype(BF)
    stores = [mover.start(quarter_ref, quarter_hbm)]
    wait(loads)
    for j in range(4):
        lanes = slice(j * 256, j * 256 + 256)
        normed = jnp.transpose(n_ref[:, lanes])
        delta = jnp.transpose(dy_ref[:, lanes])
        for y in range(2):
            wide_ref[...] = nn(normed, dgu_ref[y]).astype(BF)
            store_grad(wide_ref, core, j, y, slice(0, 768), keep_ref, give_ref)
            thin_ref[...] = nn(delta, hid_ref[y]).astype(BF)
            store_grad(thin_ref, core, j, y, slice(768, 1152), keep_ref, give_ref)
        done = pl.ds(j * 4, 4)
        stores.append(mover.start(give_ref.at[done], give_hbm.at[done]))
        stores.append(mover.start(keep_ref.at[done], keep_hbm.at[done]))
    wait(stores)


def attend_back_body(
    where_ref, d_hbm, w_hbm, proj_hbm, q_hbm, k_hbm, v_hbm, lse_hbm, table_hbm,
    rope_hbm, gain_hbm, full_hbm, resid_hbm,
    back_hbm, dproj_hbm, delta_hbm, head_ref, sum_ref,
    delta_ref, w_ref, proj_ref, q_ref, k_ref, v_ref, lse_ref, table_ref, rope_ref, gain_ref, bias_ref, dk_ref, dv_ref,
    da_ref, dproj_ref, full_ref, resid_ref, part_ref, back_ref, sems,
):
    x = where_ref[0]
    mover = Mover(sems)
    loads = [
        mover.start(table_hbm, table_ref),
        mover.start(lse_hbm, lse_ref),
        mover.start(q_hbm, q_ref),
        mover.start(k_hbm, k_ref),
        mover.start(v_hbm, v_ref),
    ]
    loads += features_in_order(mover, d_hbm, delta_ref)
    loads.append(mover.start(w_hbm.at[:, :, :, :, pl.ds(512, 256)], w_ref.at[:, :, :, :, pl.ds(512, 256)]))
    loads += [
        mover.start(proj_hbm, proj_ref),
        mover.start(rope_hbm, rope_ref),
        mover.start(gain_hbm, gain_ref),
    ]
    more = [
        mover.start(w_hbm.at[:, :, :, :, pl.ds(0, 512)], w_ref.at[:, :, :, :, pl.ds(0, 512)]),
        mover.start(full_hbm, full_ref),
        mover.start(resid_hbm, resid_ref),
    ]
    head_ref[...] = jnp.zeros_like(head_ref)
    sum_ref[...] = jnp.zeros_like(sum_ref)
    dk_ref[...] = jnp.zeros_like(dk_ref)
    dv_ref[...] = jnp.zeros_like(dv_ref)
    loads[0].wait()
    bias_of(table_ref, bias_ref)
    wait(loads[1:])
    stores = [mover.start(delta_ref, delta_hbm)]

    def back(rotated, proj, gain, rows, at):
        turned = rotated * rope_ref[rows, 0:128] - pltpu.roll(rotated, 64, 1) * rope_ref[rows, 128:256]
        inv = lax.rsqrt(jnp.mean(proj * proj, axis=-1, keepdims=True) + EPSILON)
        hat = proj * inv
        head_ref[at : at + 1, :] += jnp.sum(turned * hat, axis=0, keepdims=True)
        scaled = turned * gain
        return (inv * (scaled - hat * jnp.mean(scaled * hat, axis=-1, keepdims=True))).astype(BF)

    def attend(i, carry):
        rows = tile(i)
        bias = bias_ref[rows, :]
        logs = lse_ref[rows, :]
        for y in range(2):
            da_ref[...] = nn(delta_ref[rows, :], weight(w_ref, y, slice(512, 768))).astype(BF)
            for h in range(2):
                lanes = slice(h * 128, h * 128 + 128)
                query = q_ref[y, rows, lanes]
                da = da_ref[:, lanes]
                scores = nt(query, k_ref[y]) * SCALE + bias
                soft = jnp.exp(scores - logs[:, y * 2 + h : y * 2 + h + 1])
                dp = nt(da, v_ref[y])
                dv_ref[y] += tn(da, soft.astype(BF))
                ds = (soft * (dp - jnp.sum(dp * soft, axis=-1, keepdims=True))).astype(BF)
                dk_ref[y] += tn(query, ds)
                dq = nn(ds, k_ref[y]) * SCALE
                dproj_ref[y, rows, lanes] = back(
                    dq, proj_ref[y, rows, lanes], gain_ref[2:3, 0:128], rows, 0
                )
        return carry

    lax.fori_loop(0, TOK // TILE, attend, 0)

    for i in range(TOK // TILE):
        rows = pl.ds(i * TILE, TILE)
        for y in range(2):
            dproj_ref[y, rows, 256:384] = back(
                jnp.transpose(dk_ref[y, :, rows]) * SCALE, proj_ref[y, rows, 256:384], gain_ref[2:3, 128:256], rows, 1
            )
            dproj_ref[y, rows, 384:512] = jnp.transpose(dv_ref[y, :, rows]).astype(BF)
    stores.append(mover.start(dproj_ref, dproj_hbm))
    wait(more)
    for i in range(TOK // TILE):
        rows = pl.ds(i * TILE, TILE)
        value = full_ref[rows, :].astype(F32)
        inv = lax.rsqrt(jnp.mean(value * value, axis=-1, keepdims=True) + EPSILON)
        hat = value * inv
        out = nt(dproj_ref[0, rows, :], weight(w_ref, 0, slice(0, 512))) + nt(
            dproj_ref[1, rows, :], weight(w_ref, 1, slice(0, 512))
        )
        sum_ref[0:1, :] += jnp.sum(out * hat, axis=0, keepdims=True)
        scaled = out * gain_ref[0:1, :]
        inner = jnp.mean(scaled * hat, axis=-1, keepdims=True)
        part_ref[...] = inv * (scaled - hat * inner)
        for y in range(2):
            part_ref[:, mine(x, y)] += resid_ref[y, rows, :]
        places = pl.ds(i * (TILE // 32), TILE // 32)
        for c in range(8):
            back_ref[places, c] = (
                part_ref[:, c * 128 : c * 128 + 128].astype(BF).reshape(TILE // 32, 32, 128)
            )
        stores.append(mover.start(back_ref.at[places], back_hbm.at[places, :, pl.ds(0, 32)]))
    wait(stores)


def attend_grad_body(
    where_ref, dproj_hbm, n_hbm, delta_hbm, a_hbm,
    keep_hbm, give_hbm,
    dproj_ref, n_ref, delta_ref, a_ref, wide_ref, thin_ref, keep_ref, give_ref, sems,
):
    core = where_ref[3]
    mover = Mover(sems)
    wait(
        [
            mover.start(n_hbm, n_ref),
            mover.start(dproj_hbm, dproj_ref),
            mover.start(a_hbm, a_ref),
            mover.start(delta_hbm, delta_ref),
        ]
    )
    stores = []
    for j in range(4):
        lanes = slice(j * 256, j * 256 + 256)
        normed = jnp.transpose(n_ref[:, lanes])
        delta = jnp.transpose(delta_ref[:, lanes])
        for y in range(2):
            wide_ref[...] = nn(normed, dproj_ref[y]).astype(BF)
            store_grad(wide_ref, core, j, y, slice(0, 512), keep_ref, give_ref)
            thin_ref[...] = nn(delta, a_ref[y]).astype(BF)
            store_grad(thin_ref, core, j, y, slice(512, 768), keep_ref, give_ref)
        done = pl.ds(j * 4, 4)
        stores.append(mover.start(give_ref.at[done], give_hbm.at[done]))
        stores.append(mover.start(keep_ref.at[done], keep_hbm.at[done]))
    wait(stores)


def spread(value):
    return [value] + [shift(value, dx=k) for k in (1, 2, 3)]


def collect(sends):
    return [shift(sends[k - 1], dx=k) for k in (1, 2, 3)]


def repeat(value):
    return jnp.broadcast_to(value[None], (4,) + value.shape)


def collect_weight(parts):
    shard = jnp.concatenate(parts, axis=1)
    full = lax.all_gather(shard, BOTH, axis=0, tiled=False, axis_index_groups=SQUAD)
    return full.reshape(8, 2, 2, 64, shard.shape[1])


def merge(got, base):
    return call(
        merge_body, "vv", [("v", FEATURES, F32), ("v", WIDE, BF)], [], 1, 1 << 20, 4 << 20, got, base, limit=16
    )


def add_up(own, parts):
    return own.astype(F32) + (
        parts[0].astype(F32) + parts[1].astype(F32) + parts[2].astype(F32)
    )


def exchange(blocks, groups):
    return lax.all_to_all(blocks, BOTH, 0, 0, axis_index_groups=groups, tiled=True)


FEATURES = (2, TOK, 128)
EARLY = (8, 2, 2, 64)
WIDE = (4, 2, TOK, 128)
LATE = (8, 2, 2, 64)


fence = lax.optimization_barrier


def take(blocks, at):
    return lax.dynamic_index_in_dim(blocks, at % 4, 0, keepdims=False)


def blocks_z(where, keep, other, gains=None):
    shape = (4, 4) + keep.shape[1:]
    keep, other = keep.reshape(shape), other.reshape(shape)

    def block(k):
        total = take(keep, where[1] + k).astype(F32) + take(other, where[1] + k).astype(F32)
        if gains is None:
            return total if k == 0 else total.astype(BF)
        rows = jnp.broadcast_to(gains[None], (4,) + gains.shape)
        return jnp.concatenate([total.astype(BF), rows], axis=1)

    own, *sends = [block(k) for k in range(4)]
    return own, sends


def reduce_y(where, total):
    return add_up(
        take(total, where[2]), [shift(take(total, where[2] + k).astype(BF), dy=k) for k in (1, 2, 3)]
    )


def body(
    layer_input,
    out_grad,
    token_route,
    seq_lengths,
    positions,
    attn_gain,
    query_weight,
    key_weight,
    value_weight,
    query_gain,
    key_gain,
    out_weight,
    mlp_gain,
    gate_weight,
    up_weight,
    down_weight,
):
    row = lax.axis_index("row")
    col = lax.axis_index("col")
    y_lo = col // 4
    x = col % 4
    where = jnp.stack([x, row // 4, ((row // 2) % 2) * 2 + y_lo, row % 2]).astype(jnp.int32)
    places = jnp.arange(TOK, dtype=jnp.int32)
    heads = jnp.concatenate([query_gain, key_gain, jnp.zeros((D - 256,), BF)])
    all_gains = jnp.stack([attn_gain, mlp_gain, heads] + [jnp.zeros((D,), BF)] * 5).astype(F32)

    early = collect_weight([query_weight, key_weight, value_weight, out_weight.T])
    late = collect_weight([gate_weight, up_weight, down_weight.T])

    (sorted_rows,) = call(
        sort_body,
        "vhh",
        [("v", (2, ROWS, 72, 128), BF)],
        [((2, TOK, 128), BF)] * 2,
        2,
        2 * 2 * 2 * TOK * TOK * 128,
        4 << 20,
        token_route,
        layer_input,
        out_grad,
        limit=60,
    )
    arrived = exchange(sorted_rows.reshape(32, 72, 128), TEAM).reshape(2, ROWS, 72, 128)
    my_input = arrived[:, :, 0:32, :].reshape(FEATURES)
    inputs = exchange(repeat(my_input), SAME_X)
    grads = spread(arrived[:, :, 32:64, :].reshape(FEATURES))
    codes = arrived[0, :, 64, 0:64].astype(F32)
    slots = (codes[:, 0:32] * 16 + codes[:, 32:64]).astype(jnp.int32).reshape(TOK)

    lengths = lax.dynamic_index_in_dim(seq_lengths, y_lo, 0, keepdims=False)[0]
    bound_one = lengths[0]
    bound_two = bound_one + lengths[1]
    bound_three = bound_two + lengths[2]
    first = jnp.where(slots >= bound_one, bound_one, 0)
    first = jnp.where(slots >= bound_two, bound_two, first)
    first = jnp.where(slots >= bound_three, bound_three, first)
    table = jnp.concatenate(
        [slots.astype(F32)[None], first.astype(F32)[None], jnp.zeros((6, TOK), F32)], axis=0
    )
    my_positions = lax.dynamic_index_in_dim(positions, y_lo, 0, keepdims=False)
    position = jnp.sum(
        jnp.where(slots[:, None] == places[None, :], my_positions[None, :], 0), axis=1
    )
    freq_steps = jnp.arange(0, HEAD_SIZE, 2).astype(F32) / HEAD_SIZE
    frequency = 1.0 / ROPE_BASE**freq_steps
    angles = position.astype(F32)[:, None] * frequency[None, :]
    cosine = jnp.cos(angles)
    sine = jnp.sin(angles)
    rope = jnp.concatenate([cosine, cosine, -sine, sine], axis=-1)
    inputs, table, rope = fence((inputs, table, rope))

    sent = [("h", WIDE, BF)]
    send, full, normed_one, proj, q_rows, k_rows, v_rows, attended, lse = call(
        attend_body,
        "hhhhh",
        sent + [("h", (TOK, D), BF), ("h", (TOK, D), BF), ("h", (2, TOK, 384), F32), ("h", (2, TOK, 256), BF),
                ("h", FEATURES, BF), ("h", FEATURES, BF), ("h", (2, TOK, 256), BF), ("h", (TOK, 128), F32)],
        [((TOK, D), BF), (EARLY + (768,), BF), ((8, TOK), F32), ((TOK, 256), F32), ((8, D), F32), ((TOK, TOK), F32),
         ((TILE, D), F32), ((TOK, D), BF), ((2, TOK, 384), F32), ((2, TOK, 256), BF), (FEATURES, BF), (FEATURES, BF),
         ((2, TOK, 256), BF), ((TOK, 128), F32), (WIDE, BF)],
        SENT + 2,
        3 << 30,
        16 << 20,
        inputs, early, table, rope, all_gains,
    )
    send, grads = fence((send, grads))
    resid, wide = merge(exchange(send, SAME_X), my_input)
    wide = exchange(wide, SAME_X)

    send, delta_out, normed_two, hidden, dgu, mlp_sum = call(
        feed_body,
        "s" + "h" * 7,
        sent + [("h", (TOK, D), BF)] * 2 + [("h", (2, TOK, 384), BF), ("h", (2, TOK, 768), BF), ("v", (8, D), F32)],
        [((TOK, D), BF), (LATE + (1152,), BF), ((TILE, D), F32), ((8, D), F32), ((TOK, D), BF), ((TOK, D), BF),
         ((2, TOK, 384), BF), ((2, TOK, 768), BF), (WIDE, BF)],
        SENT + 8,
        5 << 30,
        16 << 20,
        where, wide, *grads, late, all_gains,
    )
    parts = exchange(send, SAME_X)
    quarters, keep, give = call(
        feed_grad_body,
        "s" + "h" * 6,
        [("h", (4, 128, D), BF)] + [("h", (16, 64, 1152), BF)] * 2,
        [((2, TOK, 384), BF), ((2, TOK, 768), BF), ((TOK, D), BF), ((TOK, D), BF), (LATE + (384,), BF), (FEATURES, F32),
         ((TILE, D), F32), ((256, 768), BF), ((256, 384), BF), ((ROWS, 4, 8, D), F32), ((4, 128, D), BF)]
        + [((16, 64, 1152), BF)] * 2,
        20,
        4 << 30,
        16 << 20,
        where, hidden, dgu, normed_two, delta_out, late, resid,
    )
    parts, quarters, keep, give = fence((parts, quarters, keep, give))
    resid_delta, wide = merge(parts, grads[0])
    wide = exchange(wide, SAME_X)
    output_mine = lax.psum_scatter(
        quarters.reshape(TOK, D), BOTH, scatter_dimension=0, tiled=True, axis_index_groups=SAME_X
    ).reshape(ROWS, 8, 8, 128)
    late_own, late_sends = blocks_z(where, keep, shift(give, dcore=1))
    late_parts = [shift(late_sends[k - 1], dz=k) for k in (1, 2, 3)]
    wide, _ = fence((wide, late_sends))

    back, dproj, delta_wide, head_sum, attn_sum = call(
        attend_back_body,
        "s" + "h" * 12,
        [("h", (ROWS, 8, 40, 128), BF), ("h", (2, TOK, 512), BF), ("h", (TOK, D), BF), ("v", (8, 128), F32),
         ("v", (8, D), F32)],
        [((TOK, D), BF), (EARLY + (768,), BF), ((2, TOK, 384), F32), ((2, TOK, 256), BF), (FEATURES, BF), (FEATURES, BF),
         ((TOK, 128), F32), ((8, TOK), F32), ((TOK, 256), F32), ((8, D), F32), ((TOK, TOK), F32), ((2, 128, TOK), F32),
         ((2, 128, TOK), F32), ((TILE, 256), BF), ((2, TOK, 512), BF), ((TOK, D), BF), (FEATURES, F32), ((TILE, D), F32),
         ((ROWS, 8, 32, 128), BF)],
        40,
        7 << 30,
        32 << 20,
        where, wide, early, proj, q_rows, k_rows, v_rows, lse, table, rope, all_gains, full, resid_delta,
    )
    back, dproj, delta_wide, head_sum, attn_sum, late_parts = fence(
        (back, dproj, delta_wide, head_sum, attn_sum, late_parts)
    )
    back = back.at[:, :, 32:40, :].set(jnp.transpose(output_mine, (0, 2, 1, 3)))
    gains = jnp.concatenate([attn_sum[0], mlp_sum[0], head_sum[0], head_sum[1]]).reshape(3, 768)
    gains = jnp.concatenate([gains, jnp.zeros((5, 768), F32)], axis=0)
    gain_parts = [shift(gains, dx=k) for k in (1, 2, 3)]
    keep, give = call(
        attend_grad_body,
        "shhhh",
        [("h", (16, 64, 768), BF)] * 2,
        [((2, TOK, 512), BF), ((TOK, D), BF), ((TOK, D), BF), ((2, TOK, 256), BF), ((256, 512), BF), ((256, 256), BF)]
        + [((16, 64, 768), BF)] * 2,
        20,
        2 << 30,
        8 << 20,
        where, dproj, normed_one, delta_wide, attended,
        limit=60,
    )
    keep, give, gain_parts = fence((keep, give, gain_parts))
    gains = add_up(gains, gain_parts)
    gains = (gains + shift(gains, dcore=1)).astype(BF)
    own, sends = blocks_z(where, keep, shift(give, dcore=1), gains)
    home = exchange(back.reshape(128, 40, 128), None)
    early_parts = [shift(sends[k - 1], dz=k) for k in (1, 2, 3)]
    early_parts[0], late_own, late_parts = fence((early_parts[0], late_own, late_parts))
    late_total = add_up(late_own, late_parts)
    late_parts = [shift(take(late_total, where[2] + k).astype(BF), dy=k) for k in (1, 2, 3)]
    early_parts, late_parts = fence((early_parts, late_parts))
    late_total = add_up(take(late_total, where[2]), late_parts)
    early_total = add_up(own, early_parts)
    early_total = reduce_y(where, early_total)
    layer_output, input_grad = call(
        unsort_body,
        "vh",
        [("v", (2, TOK, 128), BF)] * 2,
        [((2, ROWS, 4, 40, 128), BF)],
        2,
        4 * 2 * TOK * TOK * 128,
        2 << 20,
        token_route,
        home.reshape(ROWS, 2, 4, 40, 128),
        limit=60,
    )
    gains = early_total[64:67].reshape(3 * 768)
    early_total = early_total[0:64]
    return (
        layer_output,
        input_grad,
        gains[0:D],
        early_total[:, 0:256],
        early_total[:, 256:384],
        early_total[:, 384:512],
        gains[2 * D : 2 * D + 128],
        gains[2 * D + 128 :],
        early_total[:, 512:768].T,
        gains[D : 2 * D],
        late_total[:, 0:384],
        late_total[:, 384:768],
        late_total[:, 768:1152].T,
    )


def solution(mesh):
    in_specs = (
        P(None, "row", "col"),
        P(None, "row", "col"),
        P(None, "row"),
        P(None, "row", None),
        P(None, "row"),
        P(),
        P("row", "col"),
        P("row", "col"),
        P("row", "col"),
        P(),
        P(),
        P("col", "row"),
        P(),
        P("row", "col"),
        P("row", "col"),
        P("col", "row"),
    )
    out_specs = (
        P(None, "row", "col"),
        P(None, "row", "col"),
        P(),
        P("row", "col"),
        P("row", "col"),
        P("row", "col"),
        P(),
        P(),
        P("col", "row"),
        P(),
        P("row", "col"),
        P("row", "col"),
        P("col", "row"),
    )
    return jax.shard_map(body, mesh=mesh, in_specs=in_specs, out_specs=out_specs, check_vma=False)
```

```python
import functools
import math

import jax
import jax.numpy as jnp
from jax import lax
from jax.experimental import pallas as pl
from jax.experimental.pallas import tpu as pltpu
from jax.sharding import PartitionSpec as P

D = 1024
HEAD_SIZE = 128
EPSILON = 1e-06
ROPE_BASE = 1000000.0
NEGATIVE = -1e30
BOTH = ("row", "col")
ROWS = 16
TOK = 512
TILE = 256
SENT = 40
BF = jnp.bfloat16
F32 = jnp.float32
SCALE = 1.0 / math.sqrt(HEAD_SIZE)


def flat(row, col):
    return row * 8 + col


def spot(z, y, core, x):
    return flat(z * 4 + (y // 2) * 2 + core, (y % 2) * 4 + x)


SQUAD = [
    [flat(2 * k + core, 4 * y_lo + x) for k in range(8) for y_lo in range(2) for core in range(2)]
    for x in range(4)
]
SAME_X = [[flat(row, 4 * y_lo + x) for x in range(4)] for row in range(ROWS) for y_lo in range(2)]
TEAM = [[flat(row, 4 * y_lo + x) for y_lo in range(2) for row in range(ROWS)] for x in range(4)]


def moves(dz=0, dy=0, dcore=0, dx=0):
    return [
        (spot(z, y, core, x), spot((z + dz) % 4, (y + dy) % 4, core ^ dcore, (x + dx) % 4))
        for z in range(4)
        for y in range(4)
        for core in range(2)
        for x in range(4)
    ]


def shift(value, **step):
    return lax.ppermute(value, BOTH, moves(**step))


def dot(a, b, dims):
    return lax.dot_general(a, b, (dims, ((), ())), preferred_element_type=F32)


def nn(a, b):
    return dot(a, b, ((1,), (0,)))


def nt(a, b):
    return dot(a, b, ((1,), (1,)))


def tn(a, b):
    return dot(a, b, ((0,), (0,)))


def call(body, ins, outs, scratch, copies, flops, traffic, *args, limit=60):
    spaces = {"s": pltpu.SMEM, "v": pltpu.VMEM, "h": pl.ANY}
    return pl.pallas_call(
        body,
        out_shape=[jax.ShapeDtypeStruct(s, t) for _, s, t in outs],
        in_specs=[pl.BlockSpec(memory_space=spaces[k]) for k in ins],
        out_specs=[pl.BlockSpec(memory_space=spaces[k]) for k, _, _ in outs],
        scratch_shapes=[pltpu.VMEM(s, t) for s, t in scratch] + [pltpu.SemaphoreType.DMA((copies,))],
        compiler_params=pltpu.CompilerParams(vmem_limit_bytes=limit * 1024 * 1024),
        cost_estimate=pl.CostEstimate(flops=flops >> 6, bytes_accessed=traffic >> 6, transcendentals=0),
    )(*args)


class Mover:
    def __init__(self, sems):
        self.sems = sems
        self.used = 0

    def start(self, source, target):
        copy = pltpu.make_async_copy(source, target, self.sems.at[self.used])
        self.used += 1
        copy.start()
        return copy


def wait(copies):
    for copy in copies:
        copy.wait()


def ranks(row):
    column = jnp.transpose(jnp.broadcast_to(row, (8, TOK)))[:, 0:1]
    across = jnp.sum((column < row).astype(F32), axis=0, keepdims=True)
    down = jnp.sum((row < column).astype(F32), axis=1, keepdims=True)
    return column, across, down


def sort_body(route_ref, x_hbm, g_hbm, out_ref, x_ref, g_ref, sems):
    mover = Mover(sems)
    loads = [mover.start(x_hbm, x_ref), mover.start(g_hbm, g_ref)]
    for m in range(2):
        column, across, down = ranks(route_ref[m : m + 1, :].astype(F32))
        place = lax.broadcasted_iota(jnp.int32, (TOK, TOK), 0).astype(F32)
        pick = (place == across).astype(BF)
        slot = column - jnp.floor(column * (1.0 / TOK)) * TOK
        high = jnp.floor(slot * (1.0 / 16))
        low = slot - high * 16
        group = jnp.floor(down * (1.0 / 32))
        inner = down - group * 32
        lane = lax.broadcasted_iota(jnp.int32, (TOK, 128), 1).astype(F32)
        spread = jnp.where(lane == inner, high, jnp.where(lane == inner + 32, low, 0.0)).astype(BF)
        owner = jnp.floor(across * (1.0 / 32))
        member = (lax.broadcasted_iota(jnp.int32, (ROWS, TOK), 0).astype(F32) == owner).astype(BF)
        codes = nn(member, spread).astype(BF)
        out_ref[m, :, 64:72, :] = jnp.broadcast_to(codes[:, None, :], (ROWS, 8, 128))
        if m == 0:
            wait(loads)
        out_ref[m, :, 0:32, :] = nn(pick, x_ref[m]).astype(BF).reshape(ROWS, 32, 128)
        out_ref[m, :, 32:64, :] = nn(pick, g_ref[m]).astype(BF).reshape(ROWS, 32, 128)


def unsort_body(route_ref, home_hbm, y_ref, dx_ref, home_ref, sems):
    mover = Mover(sems)
    loads = [mover.start(home_hbm.at[m], home_ref.at[m]) for m in range(2)]
    for m in range(2):
        _, _, down = ranks(route_ref[m : m + 1, :].astype(F32))
        lane = lax.broadcasted_iota(jnp.int32, (TOK, TOK), 1).astype(F32)
        pick = (lane == down).astype(BF)
        loads[m].wait()
        for at, target_ref in ((0, dx_ref), (32, y_ref)):
            rows = home_ref[m, :, at : at + 32, :].reshape(TOK, 128)
            target_ref[m] = nn(pick, rows).astype(BF)


def features_of(mover, blocks, x, full_ref):
    return [
        mover.start(block.at[y], full_ref.at[:, mine(lax.rem(x + 4 - k, 4), y)])
        for k, block in enumerate(blocks)
        for y in range(2)
    ]


def features_in_order(mover, blocks, full_ref):
    return [
        mover.start(blocks.at[k, y], full_ref.at[:, pl.ds(y * 512 + k * 128, 128)])
        for k in range(4)
        for y in range(2)
    ]


def weight(w_ref, y, lanes):
    value = w_ref[(slice(None),) * (len(w_ref.shape) - 4) + (y, slice(None), slice(None), lanes)]
    return value.reshape(D, value.shape[-1])


def mine(x, y):
    return pl.ds(pl.multiple_of(y * 512 + x * 128, 128), 128)


def split_features(part_ref, rows, send_ref):
    for k in range(4):
        for y in range(2):
            lanes = slice(y * 512 + k * 128, y * 512 + k * 128 + 128)
            send_ref[k, y, rows, :] = part_ref[:, lanes].astype(BF)


def merge_body(got_ref, base_ref, wide_ref, sems):
    for y in range(2):
        total = base_ref[y].astype(F32)
        for k in range(4):
            total = total + got_ref[k, y].astype(F32)
        for k in range(4):
            wide_ref[k, y] = total.astype(BF)


def sent_tiles(send_ref, send_hbm, sems):
    return [
        pltpu.make_async_copy(
            send_ref.at[:, :, pl.ds(i * TILE, TILE)], send_hbm.at[:, :, pl.ds(i * TILE, TILE)], sems.at[SENT + i]
        )
        for i in range(TOK // TILE)
    ]


def norm_rope(proj, gain, cosine, sine):
    inv = lax.rsqrt(jnp.mean(proj * proj, axis=-1, keepdims=True) + EPSILON)
    normed = proj * inv * gain
    return normed * cosine + pltpu.roll(normed, 64, 1) * sine


def bias_of(table_ref, bias_ref):
    columns = jnp.transpose(table_ref[...])
    slot_row = table_ref[0:1, :]
    allowed = (slot_row <= columns[:, 0:1]) & (slot_row >= columns[:, 1:2])
    bias_ref[...] = jnp.where(allowed, 0.0, NEGATIVE)


def tile(i):
    return pl.ds(pl.multiple_of(i * TILE, TILE), TILE)


def attend_body(
    x_hbm, w_hbm, table_hbm, rope_hbm, gain_hbm,
    send_hbm, full_hbm, n_hbm, proj_hbm, q_hbm, k_hbm, v_hbm, a_hbm, lse_hbm,
    full_ref, w_ref, table_ref, rope_ref, gain_ref, bias_ref, part_ref, n_ref, proj_ref, q_ref, k_ref, v_ref, a_ref,
    lse_ref, send_ref, sems,
):
    mover = Mover(sems)
    cut = pl.ds(0, 512)
    rest = pl.ds(512, 256)
    first = features_in_order(mover, x_hbm, full_ref) + [mover.start(gain_hbm, gain_ref)]
    load_table = mover.start(table_hbm, table_ref)
    loads = [
        mover.start(w_hbm.at[:, :, :, :, cut], w_ref.at[:, :, :, :, cut]),
        mover.start(rope_hbm, rope_ref),
    ]
    load_rest = mover.start(w_hbm.at[:, :, :, :, rest], w_ref.at[:, :, :, :, rest])
    load_table.wait()
    bias_of(table_ref, bias_ref)
    wait(first)
    stores = [mover.start(full_ref, full_hbm)]

    def norm(i, carry):
        rows = tile(i)
        value = full_ref[rows, :].astype(F32)
        inv = lax.rsqrt(jnp.mean(value * value, axis=-1, keepdims=True) + EPSILON)
        n_ref[rows, :] = (value * inv * gain_ref[0:1, :]).astype(BF)
        return carry

    lax.fori_loop(0, TOK // TILE, norm, 0)
    stores.append(mover.start(n_ref, n_hbm))
    wait(loads)

    def project(i, carry):
        rows = tile(i)
        cosine, sine = rope_ref[rows, 0:128], rope_ref[rows, 128:256]
        for y in range(2):
            out = nn(n_ref[rows, :], weight(w_ref, y, slice(0, 512)))
            proj_ref[y, rows, :] = out[:, 0:384]
            for h in range(2):
                lanes = slice(h * 128, h * 128 + 128)
                q_ref[y, rows, lanes] = norm_rope(
                    out[:, lanes], gain_ref[2:3, 0:128], cosine, sine
                ).astype(BF)
            k_ref[y, rows, :] = norm_rope(
                out[:, 256:384], gain_ref[2:3, 128:256], cosine, sine
            ).astype(BF)
            v_ref[y, rows, :] = out[:, 384:512].astype(BF)
        return carry

    lax.fori_loop(0, TOK // TILE, project, 0)
    stores += [
        mover.start(proj_ref, proj_hbm),
        mover.start(q_ref, q_hbm),
        mover.start(k_ref, k_hbm),
        mover.start(v_ref, v_hbm),
    ]
    load_rest.wait()

    def attend(i, carry):
        rows = tile(i)
        bias = bias_ref[rows, :]
        lane = lax.broadcasted_iota(jnp.int32, (TILE, 128), 1)
        logs = jnp.zeros((TILE, 128), F32)
        for y in range(2):
            for h in range(2):
                lanes = slice(h * 128, h * 128 + 128)
                scores = nt(q_ref[y, rows, lanes], k_ref[y]) * SCALE + bias
                top = jnp.max(scores, axis=-1, keepdims=True)
                power = jnp.exp(scores - top)
                total = jnp.sum(power, axis=-1, keepdims=True)
                weights = (power * (1.0 / total)).astype(BF)
                a_ref[y, rows, lanes] = nn(weights, v_ref[y]).astype(BF)
                logs = jnp.where(lane == y * 2 + h, top + jnp.log(total), logs)
        lse_ref[rows, :] = logs
        return carry

    lax.fori_loop(0, TOK // TILE, attend, 0)
    stores += [mover.start(a_ref, a_hbm), mover.start(lse_ref, lse_hbm)]

    def leave(i, carry):
        rows = tile(i)
        part_ref[...] = nt(a_ref[0, rows, :], weight(w_ref, 0, slice(512, 768))) + nt(
            a_ref[1, rows, :], weight(w_ref, 1, slice(512, 768))
        )
        split_features(part_ref, rows, send_ref)
        pltpu.make_async_copy(send_ref.at[:, :, rows], send_hbm.at[:, :, rows], sems.at[SENT + i]).start()
        return carry

    lax.fori_loop(0, TOK // TILE, leave, 0)
    wait(stores + sent_tiles(send_ref, send_hbm, sems))


def feed_body(
    where_ref, h_hbm, g0, g1, g2, g3, w_hbm, gain_hbm,
    send_hbm, dy_hbm, n_hbm, hid_hbm, dgu_hbm, sum_ref,
    full_ref, w_ref, part_ref, gain_ref, dy_ref, n_ref, hid_ref, dgu_ref, send_ref, sems,
):
    mover = Mover(sems)
    cut = pl.ds(0, 768)
    rest = pl.ds(768, 384)
    loads = features_in_order(mover, h_hbm, full_ref)
    loads.append(mover.start(gain_hbm, gain_ref))
    loads.append(mover.start(w_hbm.at[:, :, :, :, cut], w_ref.at[:, :, :, :, cut]))
    later = features_of(mover, (g0, g1, g2, g3), where_ref[0], dy_ref)
    later.append(mover.start(w_hbm.at[:, :, :, :, rest], w_ref.at[:, :, :, :, rest]))
    sum_ref[...] = jnp.zeros_like(sum_ref)
    wait(loads + later)
    stores = [mover.start(dy_ref, dy_hbm)]

    def step(i, carry):
        rows = tile(i)
        gain = gain_ref[1:2, :]
        value = full_ref[rows, :].astype(F32)
        inv = lax.rsqrt(jnp.mean(value * value, axis=-1, keepdims=True) + EPSILON)
        hat = value * inv
        normed = (hat * gain).astype(BF)
        n_ref[rows, :] = normed
        delta = dy_ref[rows, :]
        for y in range(2):
            gate = nn(normed, weight(w_ref, y, slice(0, 384)))
            up = nn(normed, weight(w_ref, y, slice(384, 768)))
            down = nn(delta, weight(w_ref, y, slice(768, 1152)))
            sigma = jax.nn.sigmoid(gate)
            act = gate * sigma
            hid_ref[y, rows, :] = (act * up).astype(BF)
            dgu_ref[y, rows, 0:384] = (down * up * sigma * (1.0 + gate * (1.0 - sigma))).astype(BF)
            dgu_ref[y, rows, 384:768] = (down * act).astype(BF)
            out = nt(dgu_ref[y, rows, :], weight(w_ref, y, slice(0, 768)))
            if y == 0:
                part_ref[...] = out
            else:
                out = part_ref[...] + out
                sum_ref[0:1, :] += jnp.sum(out * hat, axis=0, keepdims=True)
                scaled = out * gain
                inner = jnp.mean(scaled * hat, axis=-1, keepdims=True)
                part_ref[...] = inv * (scaled - hat * inner)
        split_features(part_ref, rows, send_ref)
        pltpu.make_async_copy(send_ref.at[:, :, rows], send_hbm.at[:, :, rows], sems.at[SENT + i]).start()
        pltpu.make_async_copy(n_ref.at[rows], n_hbm.at[rows], sems.at[SENT + 2 + i]).start()
        pltpu.make_async_copy(hid_ref.at[:, rows], hid_hbm.at[:, rows], sems.at[SENT + 4 + i]).start()
        pltpu.make_async_copy(dgu_ref.at[:, rows], dgu_hbm.at[:, rows], sems.at[SENT + 6 + i]).start()
        return carry

    lax.fori_loop(0, TOK // TILE, step, 0)
    for i in range(TOK // TILE):
        rows = pl.ds(i * TILE, TILE)
        stores.append(pltpu.make_async_copy(n_ref.at[rows], n_hbm.at[rows], sems.at[SENT + 2 + i]))
        stores.append(pltpu.make_async_copy(hid_ref.at[:, rows], hid_hbm.at[:, rows], sems.at[SENT + 4 + i]))
        stores.append(pltpu.make_async_copy(dgu_ref.at[:, rows], dgu_hbm.at[:, rows], sems.at[SENT + 6 + i]))
    wait(stores + sent_tiles(send_ref, send_hbm, sems))


def store_grad(value_ref, core, chunk, y, lanes, keep_ref, give_ref):
    for k in range(2):
        kept = pl.multiple_of((k * 2 + core) * 64, 64)
        given = pl.multiple_of((k * 2 + 1 - core) * 64, 64)
        keep_ref[(chunk * 2 + k) * 2 + y, :, lanes] = value_ref[pl.ds(kept, 64), :]
        give_ref[(chunk * 2 + k) * 2 + y, :, lanes] = value_ref[pl.ds(given, 64), :]


def feed_grad_body(
    where_ref, hid_hbm, dgu_hbm, n_hbm, dy_hbm, w_hbm, h_hbm,
    out_hbm, keep_hbm, give_hbm,
    hid_ref, dgu_ref, n_ref, dy_ref, w_ref, resid_ref, part_ref, wide_ref, thin_ref, out_ref, keep_ref,
    give_ref, sems,
):
    x, core = where_ref[0], where_ref[3]
    mover = Mover(sems)
    first = [
        mover.start(hid_hbm, hid_ref),
        mover.start(w_hbm.at[:, :, :, :, pl.ds(768, 384)], w_ref),
        mover.start(h_hbm.at[x], resid_ref),
    ]
    loads = [
        mover.start(n_hbm, n_ref),
        mover.start(dgu_hbm, dgu_ref),
        mover.start(dy_hbm, dy_ref),
    ]
    wait(first)

    def step(i, carry):
        rows = tile(i)
        part_ref[...] = nt(hid_ref[0, rows, :], weight(w_ref, 0, slice(0, 384))) + nt(
            hid_ref[1, rows, :], weight(w_ref, 1, slice(0, 384))
        )
        for y in range(2):
            part_ref[:, mine(x, y)] += resid_ref[y, rows, :].astype(F32)
        split_features(part_ref, rows, out_ref)
        return carry

    lax.fori_loop(0, TOK // TILE, step, 0)
    stores = [mover.start(out_ref, out_hbm)]
    wait(loads)
    for j in range(4):
        lanes = slice(j * 256, j * 256 + 256)
        normed = jnp.transpose(n_ref[:, lanes])
        delta = jnp.transpose(dy_ref[:, lanes])
        for y in range(2):
            wide_ref[...] = nn(normed, dgu_ref[y]).astype(BF)
            store_grad(wide_ref, core, j, y, slice(0, 768), keep_ref, give_ref)
            thin_ref[...] = nn(delta, hid_ref[y]).astype(BF)
            store_grad(thin_ref, core, j, y, slice(768, 1152), keep_ref, give_ref)
        done = pl.ds(j * 4, 4)
        stores.append(mover.start(give_ref.at[done], give_hbm.at[done]))
        stores.append(mover.start(keep_ref.at[done], keep_hbm.at[done]))
    wait(stores)


def attend_back_body(
    where_ref, d_hbm, w_hbm, proj_hbm, q_hbm, k_hbm, v_hbm, lse_hbm, table_hbm,
    rope_hbm, gain_hbm, full_hbm, n_hbm, a_hbm, mlp_sum_hbm,
    own_hbm, send1, send2, send3, keep_hbm, give_hbm,
    delta_ref, w_ref, proj_ref, q_ref, k_ref, v_ref, lse_ref, table_ref, rope_ref, gain_ref, bias_ref, dk_ref, dv_ref,
    da_ref, dproj_ref, full_ref, part_ref, own_ref, back_ref, n_ref, a_ref, wide_ref, thin_ref, keep_ref, give_ref,
    head_ref, sum_ref, mlp_sum_ref, rows_ref, sems,
):
    x, core = where_ref[0], where_ref[3]
    mover = Mover(sems)
    loads = [
        mover.start(table_hbm, table_ref),
        mover.start(lse_hbm, lse_ref),
        mover.start(q_hbm, q_ref),
        mover.start(k_hbm, k_ref),
        mover.start(v_hbm, v_ref),
    ]
    loads += features_in_order(mover, d_hbm, delta_ref)
    loads.append(mover.start(w_hbm.at[:, :, :, :, pl.ds(512, 256)], w_ref.at[:, :, :, :, pl.ds(512, 256)]))
    loads += [
        mover.start(proj_hbm, proj_ref),
        mover.start(rope_hbm, rope_ref),
        mover.start(gain_hbm, gain_ref),
        mover.start(mlp_sum_hbm, mlp_sum_ref),
    ]
    more = [
        mover.start(w_hbm.at[:, :, :, :, pl.ds(0, 512)], w_ref.at[:, :, :, :, pl.ds(0, 512)]),
        mover.start(full_hbm, full_ref),
    ]
    much = [mover.start(n_hbm, n_ref), mover.start(a_hbm, a_ref)]
    head_ref[...] = jnp.zeros_like(head_ref)
    sum_ref[...] = jnp.zeros_like(sum_ref)
    dk_ref[...] = jnp.zeros_like(dk_ref)
    dv_ref[...] = jnp.zeros_like(dv_ref)
    loads[0].wait()
    bias_of(table_ref, bias_ref)
    wait(loads[1:])
    stores = []

    def back(rotated, proj, gain, rows, at):
        turned = rotated * rope_ref[rows, 0:128] - pltpu.roll(rotated, 64, 1) * rope_ref[rows, 128:256]
        inv = lax.rsqrt(jnp.mean(proj * proj, axis=-1, keepdims=True) + EPSILON)
        hat = proj * inv
        head_ref[at : at + 1, :] += jnp.sum(turned * hat, axis=0, keepdims=True)
        scaled = turned * gain
        return (inv * (scaled - hat * jnp.mean(scaled * hat, axis=-1, keepdims=True))).astype(BF)

    def attend(i, carry):
        rows = tile(i)
        bias = bias_ref[rows, :]
        logs = lse_ref[rows, :]
        for y in range(2):
            da_ref[...] = nn(delta_ref[rows, :], weight(w_ref, y, slice(512, 768))).astype(BF)
            for h in range(2):
                lanes = slice(h * 128, h * 128 + 128)
                query = q_ref[y, rows, lanes]
                da = da_ref[:, lanes]
                scores = nt(query, k_ref[y]) * SCALE + bias
                soft = jnp.exp(scores - logs[:, y * 2 + h : y * 2 + h + 1])
                dp = nt(da, v_ref[y])
                dv_ref[y] += tn(da, soft.astype(BF))
                ds = (soft * (dp - jnp.sum(dp * soft, axis=-1, keepdims=True))).astype(BF)
                dk_ref[y] += tn(query, ds)
                dq = nn(ds, k_ref[y]) * SCALE
                dproj_ref[y, rows, lanes] = back(
                    dq, proj_ref[y, rows, lanes], gain_ref[2:3, 0:128], rows, 0
                )
        return carry

    lax.fori_loop(0, TOK // TILE, attend, 0)

    for i in range(TOK // TILE):
        rows = pl.ds(i * TILE, TILE)
        for y in range(2):
            dproj_ref[y, rows, 256:384] = back(
                jnp.transpose(dk_ref[y, :, rows]) * SCALE, proj_ref[y, rows, 256:384], gain_ref[2:3, 128:256], rows, 1
            )
            dproj_ref[y, rows, 384:512] = jnp.transpose(dv_ref[y, :, rows]).astype(BF)
    wait(much)
    for j in range(4):
        lanes = slice(j * 256, j * 256 + 256)
        normed = jnp.transpose(n_ref[:, lanes])
        delta = jnp.transpose(delta_ref[:, lanes])
        for y in range(2):
            wide_ref[...] = nn(normed, dproj_ref[y]).astype(BF)
            store_grad(wide_ref, core, j, y, slice(0, 512), keep_ref, give_ref)
            thin_ref[...] = nn(delta, a_ref[y]).astype(BF)
            store_grad(thin_ref, core, j, y, slice(512, 768), keep_ref, give_ref)
        done = pl.ds(j * 4, 4)
        stores.append(mover.start(give_ref.at[done], give_hbm.at[done, pl.ds(0, 64)]))
        stores.append(mover.start(keep_ref.at[done], keep_hbm.at[done, pl.ds(0, 64)]))
    wait(more)
    for i in range(TOK // TILE):
        rows = pl.ds(i * TILE, TILE)
        value = full_ref[rows, :].astype(F32)
        inv = lax.rsqrt(jnp.mean(value * value, axis=-1, keepdims=True) + EPSILON)
        hat = value * inv
        out = nt(dproj_ref[0, rows, :], weight(w_ref, 0, slice(0, 512))) + nt(
            dproj_ref[1, rows, :], weight(w_ref, 1, slice(0, 512))
        )
        sum_ref[0:1, :] += jnp.sum(out * hat, axis=0, keepdims=True)
        scaled = out * gain_ref[0:1, :]
        inner = jnp.mean(scaled * hat, axis=-1, keepdims=True)
        part_ref[...] = inv * (scaled - hat * inner)
        for y in range(2):
            part_ref[:, mine(x, y)] += delta_ref[rows, mine(x, y)].astype(F32)
        for y in range(2):
            own_ref[y, rows, :] = part_ref[:, mine(x, y)]
            for k in range(3):
                back_ref[k, y, rows, :] = part_ref[:, mine(lax.rem(x + k + 1, 4), y)].astype(BF)
        stores.append(mover.start(own_ref.at[:, rows], own_hbm.at[:, rows]))
        for k, send in enumerate((send1, send2, send3)):
            stores.append(mover.start(back_ref.at[k, :, rows], send.at[:, rows]))
    attn_sum, mlp_sum = sum_ref[0:1, :], mlp_sum_ref[0:1, :]
    gains = jnp.concatenate(
        [
            attn_sum[:, 0:768],
            jnp.concatenate([attn_sum[:, 768:1024], mlp_sum[:, 0:512]], axis=1),
            jnp.concatenate([mlp_sum[:, 512:1024], head_ref[0:1, :], head_ref[1:2, :]], axis=1),
            jnp.zeros((5, 768), F32),
        ],
        axis=0,
    )
    rows_ref[...] = jnp.broadcast_to(gains[None], (16, 8, 768)).astype(BF)
    stores.append(mover.start(rows_ref, keep_hbm.at[:, pl.ds(64, 8)]))
    stores.append(mover.start(rows_ref, give_hbm.at[:, pl.ds(64, 8)]))
    wait(stores)


def spread(value):
    return [value] + [shift(value, dx=k) for k in (1, 2, 3)]


def collect(sends):
    return [shift(sends[k - 1], dx=k) for k in (1, 2, 3)]


def repeat(value):
    return jnp.broadcast_to(value[None], (4,) + value.shape)


def collect_weight(parts):
    shard = jnp.concatenate(parts, axis=1)
    full = lax.all_gather(shard, BOTH, axis=0, tiled=False, axis_index_groups=SQUAD)
    return full.reshape(8, 2, 2, 64, shard.shape[1])


def merge(got, base):
    return call(
        merge_body, "vv", [("v", WIDE, BF)], [], 1, 1 << 20, 4 << 20, got, base, limit=16
    )[0]


def add_up(own, parts):
    return own.astype(F32) + (
        parts[0].astype(F32) + parts[1].astype(F32) + parts[2].astype(F32)
    )


def exchange(blocks, groups):
    return lax.all_to_all(blocks, BOTH, 0, 0, axis_index_groups=groups, tiled=True)


FEATURES = (2, TOK, 128)
EARLY = (8, 2, 2, 64)
WIDE = (4, 2, TOK, 128)
LATE = (8, 2, 2, 64)


fence = lax.optimization_barrier


def take(blocks, at):
    return lax.dynamic_index_in_dim(blocks, at % 4, 0, keepdims=False)


def blocks_z(where, keep, other):
    shape = (4, 4) + keep.shape[1:]
    keep, other = keep.reshape(shape), other.reshape(shape)

    def block(k):
        return take(keep, where[1] + k).astype(F32) + take(other, where[1] + k).astype(F32)

    return block(0), [block(k).astype(BF) for k in (1, 2, 3)]


def reduce_y(where, total):
    return add_up(
        take(total, where[2]), [shift(take(total, where[2] + k).astype(BF), dy=k) for k in (1, 2, 3)]
    )


def body(
    layer_input,
    out_grad,
    token_route,
    seq_lengths,
    positions,
    attn_gain,
    query_weight,
    key_weight,
    value_weight,
    query_gain,
    key_gain,
    out_weight,
    mlp_gain,
    gate_weight,
    up_weight,
    down_weight,
):
    row = lax.axis_index("row")
    col = lax.axis_index("col")
    y_lo = col // 4
    x = col % 4
    where = jnp.stack([x, row // 4, ((row // 2) % 2) * 2 + y_lo, row % 2]).astype(jnp.int32)
    places = jnp.arange(TOK, dtype=jnp.int32)
    heads = jnp.concatenate([query_gain, key_gain, jnp.zeros((D - 256,), BF)])
    all_gains = jnp.stack([attn_gain, mlp_gain, heads] + [jnp.zeros((D,), BF)] * 5).astype(F32)

    early = collect_weight([query_weight, key_weight, value_weight, out_weight.T])
    late = collect_weight([gate_weight, up_weight, down_weight.T])

    (sorted_rows,) = call(
        sort_body,
        "vhh",
        [("v", (2, ROWS, 72, 128), BF)],
        [((2, TOK, 128), BF)] * 2,
        2,
        2 * 2 * 2 * TOK * TOK * 128,
        4 << 20,
        token_route,
        layer_input,
        out_grad,
        limit=60,
    )
    arrived = exchange(sorted_rows.reshape(32, 72, 128), TEAM).reshape(2, ROWS, 72, 128)
    my_input = arrived[:, :, 0:32, :].reshape(FEATURES)
    inputs = exchange(repeat(my_input), SAME_X)
    grads = spread(arrived[:, :, 32:64, :].reshape(FEATURES))
    codes = arrived[0, :, 64, 0:64].astype(F32)
    slots = (codes[:, 0:32] * 16 + codes[:, 32:64]).astype(jnp.int32).reshape(TOK)

    lengths = lax.dynamic_index_in_dim(seq_lengths, y_lo, 0, keepdims=False)[0]
    bound_one = lengths[0]
    bound_two = bound_one + lengths[1]
    bound_three = bound_two + lengths[2]
    first = jnp.where(slots >= bound_one, bound_one, 0)
    first = jnp.where(slots >= bound_two, bound_two, first)
    first = jnp.where(slots >= bound_three, bound_three, first)
    table = jnp.concatenate(
        [slots.astype(F32)[None], first.astype(F32)[None], jnp.zeros((6, TOK), F32)], axis=0
    )
    my_positions = lax.dynamic_index_in_dim(positions, y_lo, 0, keepdims=False)
    position = jnp.sum(
        jnp.where(slots[:, None] == places[None, :], my_positions[None, :], 0), axis=1
    )
    freq_steps = jnp.arange(0, HEAD_SIZE, 2).astype(F32) / HEAD_SIZE
    frequency = 1.0 / ROPE_BASE**freq_steps
    angles = position.astype(F32)[:, None] * frequency[None, :]
    cosine = jnp.cos(angles)
    sine = jnp.sin(angles)
    rope = jnp.concatenate([cosine, cosine, -sine, sine], axis=-1)
    inputs, table, rope = fence((inputs, table, rope))

    sent = [("h", WIDE, BF)]
    send, full, normed_one, proj, q_rows, k_rows, v_rows, attended, lse = call(
        attend_body,
        "hhhhh",
        sent + [("h", (TOK, D), BF), ("h", (TOK, D), BF), ("h", (2, TOK, 384), F32), ("h", (2, TOK, 256), BF),
                ("h", FEATURES, BF), ("h", FEATURES, BF), ("h", (2, TOK, 256), BF), ("h", (TOK, 128), F32)],
        [((TOK, D), BF), (EARLY + (768,), BF), ((8, TOK), F32), ((TOK, 256), F32), ((8, D), F32), ((TOK, TOK), F32),
         ((TILE, D), F32), ((TOK, D), BF), ((2, TOK, 384), F32), ((2, TOK, 256), BF), (FEATURES, BF), (FEATURES, BF),
         ((2, TOK, 256), BF), ((TOK, 128), F32), (WIDE, BF)],
        SENT + 2,
        3 << 30,
        16 << 20,
        inputs, early, table, rope, all_gains,
    )
    send, grads = fence((send, grads))
    wide = merge(exchange(send, SAME_X), my_input)
    wide = exchange(wide, SAME_X)

    send, delta_out, normed_two, hidden, dgu, mlp_sum = call(
        feed_body,
        "s" + "h" * 7,
        sent + [("h", (TOK, D), BF)] * 2 + [("h", (2, TOK, 384), BF), ("h", (2, TOK, 768), BF), ("v", (8, D), F32)],
        [((TOK, D), BF), (LATE + (1152,), BF), ((TILE, D), F32), ((8, D), F32), ((TOK, D), BF), ((TOK, D), BF),
         ((2, TOK, 384), BF), ((2, TOK, 768), BF), (WIDE, BF)],
        SENT + 8,
        5 << 30,
        16 << 20,
        where, wide, *grads, late, all_gains,
    )
    parts = exchange(send, SAME_X)
    out_home, keep, give = call(
        feed_grad_body,
        "s" + "h" * 6,
        [("h", WIDE, BF)] + [("h", (16, 64, 1152), BF)] * 2,
        [((2, TOK, 384), BF), ((2, TOK, 768), BF), ((TOK, D), BF), ((TOK, D), BF), (LATE + (384,), BF), (FEATURES, BF),
         ((TILE, D), F32), ((256, 768), BF), ((256, 384), BF), (WIDE, BF)]
        + [((16, 64, 1152), BF)] * 2,
        20,
        4 << 30,
        16 << 20,
        where, hidden, dgu, normed_two, delta_out, late, wide,
    )
    parts, out_home, keep, give = fence((parts, out_home, keep, give))
    wide = merge(parts, grads[0])
    wide = exchange(wide, SAME_X)
    late_own, late_sends = blocks_z(where, keep, shift(give, dcore=1))
    late_parts = [shift(late_sends[k - 1], dz=k) for k in (1, 2, 3)]
    wide, _ = fence((wide, late_sends))

    mine_delta, *delta_sends, keep, give = call(
        attend_back_body,
        "s" + "h" * 14,
        [("h", FEATURES, F32)] + [("h", FEATURES, BF)] * 3 + [("h", (16, 72, 768), BF)] * 2,
        [((TOK, D), BF), (EARLY + (768,), BF), ((2, TOK, 384), F32), ((2, TOK, 256), BF), (FEATURES, BF), (FEATURES, BF),
         ((TOK, 128), F32), ((8, TOK), F32), ((TOK, 256), F32), ((8, D), F32), ((TOK, TOK), F32), ((2, 128, TOK), F32),
         ((2, 128, TOK), F32), ((TILE, 256), BF), ((2, TOK, 512), BF), ((TOK, D), BF), ((TILE, D), F32),
         (FEATURES, F32), ((3,) + FEATURES, BF), ((TOK, D), BF), ((2, TOK, 256), BF), ((256, 512), BF), ((256, 256), BF)]
        + [((16, 64, 768), BF)] * 2
        + [((8, 128), F32), ((8, D), F32), ((8, D), F32), ((16, 8, 768), BF)],
        52,
        7 << 30,
        32 << 20,
        where, wide, early, proj, q_rows, k_rows, v_rows, lse, table, rope, all_gains, full, normed_one, attended, mlp_sum,
    )
    mine_delta, delta_sends, keep, give, late_parts = fence(
        (mine_delta, delta_sends, keep, give, late_parts)
    )
    own, sends = blocks_z(where, keep, shift(give, dcore=1))
    sends, delta_sends = fence((sends, delta_sends))
    early_parts = [shift(sends[k - 1], dz=k) for k in (1, 2, 3)]
    delta_mine = add_up(mine_delta, collect(delta_sends)).astype(BF)
    output_mine = lax.psum_scatter(
        out_home, BOTH, scatter_dimension=0, tiled=True, axis_index_groups=SAME_X
    )
    back = jnp.concatenate(
        [delta_mine.reshape(2, ROWS, 32, 128), output_mine.reshape(2, ROWS, 32, 128)], axis=2
    )
    home = exchange(back.reshape(32, 64, 128), TEAM).reshape(2, ROWS, 64, 128)
    late_own, late_parts = fence((late_own, late_parts))
    late_total = add_up(late_own, late_parts)
    late_parts = [shift(take(late_total, where[2] + k).astype(BF), dy=k) for k in (1, 2, 3)]
    early_parts, late_parts = fence((early_parts, late_parts))
    late_total = add_up(take(late_total, where[2]), late_parts)
    early_total = reduce_y(where, add_up(own, early_parts))
    layer_output, input_grad = call(
        unsort_body,
        "vh",
        [("v", (2, TOK, 128), BF)] * 2,
        [((2, ROWS, 64, 128), BF)],
        2,
        4 * 2 * TOK * TOK * 128,
        2 << 20,
        token_route,
        home,
        limit=60,
    )
    gains = early_total[64:72]
    gains = add_up(gains, [shift(gains, dx=k) for k in (1, 2, 3)])[0:3].reshape(3 * 768)
    early_total = early_total[0:64]
    return (
        layer_output,
        input_grad,
        gains[0:D],
        early_total[:, 0:256],
        early_total[:, 256:384],
        early_total[:, 384:512],
        gains[2 * D : 2 * D + 128],
        gains[2 * D + 128 :],
        early_total[:, 512:768].T,
        gains[D : 2 * D],
        late_total[:, 0:384],
        late_total[:, 384:768],
        late_total[:, 768:1152].T,
    )


def solution(mesh):
    in_specs = (
        P(None, "row", "col"),
        P(None, "row", "col"),
        P(None, "row"),
        P(None, "row", None),
        P(None, "row"),
        P(),
        P("row", "col"),
        P("row", "col"),
        P("row", "col"),
        P(),
        P(),
        P("col", "row"),
        P(),
        P("row", "col"),
        P("row", "col"),
        P("col", "row"),
    )
    out_specs = (
        P(None, "row", "col"),
        P(None, "row", "col"),
        P(),
        P("row", "col"),
        P("row", "col"),
        P("row", "col"),
        P(),
        P(),
        P("col", "row"),
        P(),
        P("row", "col"),
        P("row", "col"),
        P("col", "row"),
    )
    return jax.shard_map(body, mesh=mesh, in_specs=in_specs, out_specs=out_specs, check_vma=False)
```

```python
import functools
import math

import jax
import jax.numpy as jnp
from jax import lax
from jax.experimental import pallas as pl
from jax.experimental.pallas import tpu as pltpu
from jax.sharding import PartitionSpec as P

D = 1024
HEAD_SIZE = 128
EPSILON = 1e-06
ROPE_BASE = 1000000.0
NEGATIVE = -1e30
BOTH = ("row", "col")
ROWS = 16
TOK = 512
TILE = 256
SENT = 40
BF = jnp.bfloat16
F32 = jnp.float32
SCALE = 1.0 / math.sqrt(HEAD_SIZE)


def flat(row, col):
    return row * 8 + col


def spot(z, y, core, x):
    return flat(z * 4 + (y // 2) * 2 + core, (y % 2) * 4 + x)


SQUAD = [
    [flat(2 * k + core, 4 * y_lo + x) for k in range(8) for y_lo in range(2) for core in range(2)]
    for x in range(4)
]
SAME_X = [[flat(row, 4 * y_lo + x) for x in range(4)] for row in range(ROWS) for y_lo in range(2)]
TEAM = [[flat(row, 4 * y_lo + x) for y_lo in range(2) for row in range(ROWS)] for x in range(4)]


def moves(dz=0, dy=0, dcore=0, dx=0):
    return [
        (spot(z, y, core, x), spot((z + dz) % 4, (y + dy) % 4, core ^ dcore, (x + dx) % 4))
        for z in range(4)
        for y in range(4)
        for core in range(2)
        for x in range(4)
    ]


def shift(value, **step):
    return lax.ppermute(value, BOTH, moves(**step))


def dot(a, b, dims):
    return lax.dot_general(a, b, (dims, ((), ())), preferred_element_type=F32)


def nn(a, b):
    return dot(a, b, ((1,), (0,)))


def nt(a, b):
    return dot(a, b, ((1,), (1,)))


def tn(a, b):
    return dot(a, b, ((0,), (0,)))


def call(body, ins, outs, scratch, copies, flops, traffic, *args, limit=60):
    spaces = {"s": pltpu.SMEM, "v": pltpu.VMEM, "h": pl.ANY}
    return pl.pallas_call(
        body,
        out_shape=[jax.ShapeDtypeStruct(s, t) for _, s, t in outs],
        in_specs=[pl.BlockSpec(memory_space=spaces[k]) for k in ins],
        out_specs=[pl.BlockSpec(memory_space=spaces[k]) for k, _, _ in outs],
        scratch_shapes=[pltpu.VMEM(s, t) for s, t in scratch] + [pltpu.SemaphoreType.DMA((copies,))],
        compiler_params=pltpu.CompilerParams(vmem_limit_bytes=limit * 1024 * 1024),
        cost_estimate=pl.CostEstimate(flops=flops >> 6, bytes_accessed=traffic >> 6, transcendentals=0),
    )(*args)


class Mover:
    def __init__(self, sems):
        self.sems = sems
        self.used = 0

    def start(self, source, target):
        copy = pltpu.make_async_copy(source, target, self.sems.at[self.used])
        self.used += 1
        copy.start()
        return copy


def wait(copies):
    for copy in copies:
        copy.wait()


def ranks(row):
    column = jnp.transpose(jnp.broadcast_to(row, (8, TOK)))[:, 0:1]
    across = jnp.sum((column < row).astype(F32), axis=0, keepdims=True)
    down = jnp.sum((row < column).astype(F32), axis=1, keepdims=True)
    return column, across, down


def sort_body(route_ref, x_hbm, g_hbm, out_ref, x_ref, g_ref, sems):
    mover = Mover(sems)
    loads = [mover.start(x_hbm, x_ref), mover.start(g_hbm, g_ref)]
    for m in range(2):
        column, across, down = ranks(route_ref[m : m + 1, :].astype(F32))
        place = lax.broadcasted_iota(jnp.int32, (TOK, TOK), 0).astype(F32)
        pick = (place == across).astype(BF)
        slot = column - jnp.floor(column * (1.0 / TOK)) * TOK
        high = jnp.floor(slot * (1.0 / 16))
        low = slot - high * 16
        group = jnp.floor(down * (1.0 / 32))
        inner = down - group * 32
        lane = lax.broadcasted_iota(jnp.int32, (TOK, 128), 1).astype(F32)
        spread = jnp.where(lane == inner, high, jnp.where(lane == inner + 32, low, 0.0)).astype(BF)
        owner = jnp.floor(across * (1.0 / 32))
        member = (lax.broadcasted_iota(jnp.int32, (ROWS, TOK), 0).astype(F32) == owner).astype(BF)
        codes = nn(member, spread).astype(BF)
        out_ref[m, :, 64:72, :] = jnp.broadcast_to(codes[:, None, :], (ROWS, 8, 128))
        if m == 0:
            wait(loads)
        out_ref[m, :, 0:32, :] = nn(pick, x_ref[m]).astype(BF).reshape(ROWS, 32, 128)
        out_ref[m, :, 32:64, :] = nn(pick, g_ref[m]).astype(BF).reshape(ROWS, 32, 128)


def unsort_body(route_ref, home_hbm, y_ref, dx_ref, home_ref, sems):
    mover = Mover(sems)
    loads = [mover.start(home_hbm.at[m], home_ref.at[m]) for m in range(2)]
    for m in range(2):
        _, _, down = ranks(route_ref[m : m + 1, :].astype(F32))
        lane = lax.broadcasted_iota(jnp.int32, (TOK, TOK), 1).astype(F32)
        pick = (lane == down).astype(BF)
        loads[m].wait()
        for at, target_ref in ((0, dx_ref), (32, y_ref)):
            rows = home_ref[m, :, at : at + 32, :].reshape(TOK, 128)
            target_ref[m] = nn(pick, rows).astype(BF)


def features_of(mover, blocks, x, full_ref):
    return [
        mover.start(block.at[y], full_ref.at[:, mine(lax.rem(x + 4 - k, 4), y)])
        for k, block in enumerate(blocks)
        for y in range(2)
    ]


def features_in_order(mover, blocks, full_ref):
    return [
        mover.start(blocks.at[k, y], full_ref.at[:, pl.ds(y * 512 + k * 128, 128)])
        for k in range(4)
        for y in range(2)
    ]


def weight(w_ref, y, lanes):
    value = w_ref[(slice(None),) * (len(w_ref.shape) - 4) + (y, slice(None), slice(None), lanes)]
    return value.reshape(D, value.shape[-1])


def mine(x, y):
    return pl.ds(pl.multiple_of(y * 512 + x * 128, 128), 128)


def split_features(part_ref, rows, send_ref):
    for k in range(4):
        for y in range(2):
            lanes = slice(y * 512 + k * 128, y * 512 + k * 128 + 128)
            send_ref[k, y, rows, :] = part_ref[:, lanes].astype(BF)


def merge_body(got_ref, base_ref, wide_ref, sems):
    for y in range(2):
        total = base_ref[y].astype(F32)
        for k in range(4):
            total = total + got_ref[k, y].astype(F32)
        for k in range(4):
            wide_ref[k, y] = total.astype(BF)


def sent_tiles(send_ref, send_hbm, sems):
    return [
        pltpu.make_async_copy(
            send_ref.at[:, :, pl.ds(i * TILE, TILE)], send_hbm.at[:, :, pl.ds(i * TILE, TILE)], sems.at[SENT + i]
        )
        for i in range(TOK // TILE)
    ]


def norm_rope(proj, gain, cosine, sine):
    inv = lax.rsqrt(jnp.mean(proj * proj, axis=-1, keepdims=True) + EPSILON)
    normed = proj * inv * gain
    return normed * cosine + pltpu.roll(normed, 64, 1) * sine


def bias_of(table_ref, bias_ref):
    columns = jnp.transpose(table_ref[...])
    slot_row = table_ref[0:1, :]
    allowed = (slot_row <= columns[:, 0:1]) & (slot_row >= columns[:, 1:2])
    bias_ref[...] = jnp.where(allowed, 0.0, NEGATIVE)


def tile(i):
    return pl.ds(pl.multiple_of(i * TILE, TILE), TILE)


def attend_body(
    x_hbm, w_hbm, table_hbm, rope_hbm, gain_hbm,
    send_hbm, full_hbm, n_hbm, proj_hbm, q_hbm, k_hbm, v_hbm, a_hbm, lse_hbm,
    full_ref, w_ref, table_ref, rope_ref, gain_ref, bias_ref, part_ref, n_ref, proj_ref, q_ref, k_ref, v_ref, a_ref,
    lse_ref, send_ref, sems,
):
    mover = Mover(sems)
    cut = pl.ds(0, 512)
    rest = pl.ds(512, 256)
    first = features_in_order(mover, x_hbm, full_ref) + [mover.start(gain_hbm, gain_ref)]
    load_table = mover.start(table_hbm, table_ref)
    loads = [
        mover.start(w_hbm.at[:, :, :, :, cut], w_ref.at[:, :, :, :, cut]),
        mover.start(rope_hbm, rope_ref),
    ]
    load_rest = mover.start(w_hbm.at[:, :, :, :, rest], w_ref.at[:, :, :, :, rest])
    load_table.wait()
    bias_of(table_ref, bias_ref)
    wait(first)
    stores = [mover.start(full_ref, full_hbm)]

    def norm(i, carry):
        rows = tile(i)
        value = full_ref[rows, :].astype(F32)
        inv = lax.rsqrt(jnp.mean(value * value, axis=-1, keepdims=True) + EPSILON)
        n_ref[rows, :] = (value * inv * gain_ref[0:1, :]).astype(BF)
        return carry

    lax.fori_loop(0, TOK // TILE, norm, 0)
    stores.append(mover.start(n_ref, n_hbm))
    wait(loads)

    def project(i, carry):
        rows = tile(i)
        cosine, sine = rope_ref[rows, 0:128], rope_ref[rows, 128:256]
        for y in range(2):
            out = nn(n_ref[rows, :], weight(w_ref, y, slice(0, 512)))
            proj_ref[y, rows, :] = out[:, 0:384]
            for h in range(2):
                lanes = slice(h * 128, h * 128 + 128)
                q_ref[y, rows, lanes] = norm_rope(
                    out[:, lanes], gain_ref[2:3, 0:128], cosine, sine
                ).astype(BF)
            k_ref[y, rows, :] = norm_rope(
                out[:, 256:384], gain_ref[2:3, 128:256], cosine, sine
            ).astype(BF)
            v_ref[y, rows, :] = out[:, 384:512].astype(BF)
        return carry

    lax.fori_loop(0, TOK // TILE, project, 0)
    stores += [
        mover.start(proj_ref, proj_hbm),
        mover.start(q_ref, q_hbm),
        mover.start(k_ref, k_hbm),
        mover.start(v_ref, v_hbm),
    ]
    load_rest.wait()

    def attend(i, carry):
        rows = tile(i)
        bias = bias_ref[rows, :]
        lane = lax.broadcasted_iota(jnp.int32, (TILE, 128), 1)
        logs = jnp.zeros((TILE, 128), F32)
        for y in range(2):
            for h in range(2):
                lanes = slice(h * 128, h * 128 + 128)
                scores = nt(q_ref[y, rows, lanes], k_ref[y]) * SCALE + bias
                top = jnp.max(scores, axis=-1, keepdims=True)
                power = jnp.exp(scores - top)
                total = jnp.sum(power, axis=-1, keepdims=True)
                weights = (power * (1.0 / total)).astype(BF)
                a_ref[y, rows, lanes] = nn(weights, v_ref[y]).astype(BF)
                logs = jnp.where(lane == y * 2 + h, top + jnp.log(total), logs)
        lse_ref[rows, :] = logs
        return carry

    lax.fori_loop(0, TOK // TILE, attend, 0)
    stores += [mover.start(a_ref, a_hbm), mover.start(lse_ref, lse_hbm)]

    def leave(i, carry):
        rows = tile(i)
        part_ref[...] = nt(a_ref[0, rows, :], weight(w_ref, 0, slice(512, 768))) + nt(
            a_ref[1, rows, :], weight(w_ref, 1, slice(512, 768))
        )
        split_features(part_ref, rows, send_ref)
        pltpu.make_async_copy(send_ref.at[:, :, rows], send_hbm.at[:, :, rows], sems.at[SENT + i]).start()
        return carry

    lax.fori_loop(0, TOK // TILE, leave, 0)
    wait(stores + sent_tiles(send_ref, send_hbm, sems))


def feed_body(
    where_ref, h_hbm, g0, g1, g2, g3, w_hbm, gain_hbm,
    send_hbm, dy_hbm, n_hbm, hid_hbm, dgu_hbm, sum_ref,
    full_ref, w_ref, part_ref, gain_ref, dy_ref, n_ref, hid_ref, dgu_ref, send_ref, sems,
):
    mover = Mover(sems)
    cut = pl.ds(0, 768)
    rest = pl.ds(768, 384)
    loads = features_in_order(mover, h_hbm, full_ref)
    loads.append(mover.start(gain_hbm, gain_ref))
    loads.append(mover.start(w_hbm.at[:, :, :, :, cut], w_ref.at[:, :, :, :, cut]))
    later = features_of(mover, (g0, g1, g2, g3), where_ref[0], dy_ref)
    later.append(mover.start(w_hbm.at[:, :, :, :, rest], w_ref.at[:, :, :, :, rest]))
    sum_ref[...] = jnp.zeros_like(sum_ref)
    wait(loads + later)
    stores = [mover.start(dy_ref, dy_hbm)]

    def step(i, carry):
        rows = tile(i)
        gain = gain_ref[1:2, :]
        value = full_ref[rows, :].astype(F32)
        inv = lax.rsqrt(jnp.mean(value * value, axis=-1, keepdims=True) + EPSILON)
        hat = value * inv
        normed = (hat * gain).astype(BF)
        n_ref[rows, :] = normed
        delta = dy_ref[rows, :]
        for y in range(2):
            gate = nn(normed, weight(w_ref, y, slice(0, 384)))
            up = nn(normed, weight(w_ref, y, slice(384, 768)))
            down = nn(delta, weight(w_ref, y, slice(768, 1152)))
            sigma = jax.nn.sigmoid(gate)
            act = gate * sigma
            hid_ref[y, rows, :] = (act * up).astype(BF)
            dgu_ref[y, rows, 0:384] = (down * up * sigma * (1.0 + gate * (1.0 - sigma))).astype(BF)
            dgu_ref[y, rows, 384:768] = (down * act).astype(BF)
            out = nt(dgu_ref[y, rows, :], weight(w_ref, y, slice(0, 768)))
            if y == 0:
                part_ref[...] = out
            else:
                out = part_ref[...] + out
                sum_ref[0:1, :] += jnp.sum(out * hat, axis=0, keepdims=True)
                scaled = out * gain
                inner = jnp.mean(scaled * hat, axis=-1, keepdims=True)
                part_ref[...] = inv * (scaled - hat * inner)
        split_features(part_ref, rows, send_ref)
        pltpu.make_async_copy(send_ref.at[:, :, rows], send_hbm.at[:, :, rows], sems.at[SENT + i]).start()
        pltpu.make_async_copy(n_ref.at[rows], n_hbm.at[rows], sems.at[SENT + 2 + i]).start()
        pltpu.make_async_copy(hid_ref.at[:, rows], hid_hbm.at[:, rows], sems.at[SENT + 4 + i]).start()
        pltpu.make_async_copy(dgu_ref.at[:, rows], dgu_hbm.at[:, rows], sems.at[SENT + 6 + i]).start()
        return carry

    lax.fori_loop(0, TOK // TILE, step, 0)
    for i in range(TOK // TILE):
        rows = pl.ds(i * TILE, TILE)
        stores.append(pltpu.make_async_copy(n_ref.at[rows], n_hbm.at[rows], sems.at[SENT + 2 + i]))
        stores.append(pltpu.make_async_copy(hid_ref.at[:, rows], hid_hbm.at[:, rows], sems.at[SENT + 4 + i]))
        stores.append(pltpu.make_async_copy(dgu_ref.at[:, rows], dgu_hbm.at[:, rows], sems.at[SENT + 6 + i]))
    wait(stores + sent_tiles(send_ref, send_hbm, sems))


def store_grad(value_ref, core, chunk, y, lanes, keep_ref, give_ref):
    for k in range(2):
        kept = pl.multiple_of((k * 2 + core) * 64, 64)
        given = pl.multiple_of((k * 2 + 1 - core) * 64, 64)
        keep_ref[(chunk * 2 + k) * 2 + y, :, lanes] = value_ref[pl.ds(kept, 64), :]
        give_ref[(chunk * 2 + k) * 2 + y, :, lanes] = value_ref[pl.ds(given, 64), :]


def feed_grad_body(
    where_ref, hid_hbm, dgu_hbm, n_hbm, dy_hbm, w_hbm, h_hbm,
    out_hbm, keep_hbm, give_hbm,
    hid_ref, dgu_ref, n_ref, dy_ref, w_ref, resid_ref, part_ref, wide_ref, thin_ref, out_ref, keep_ref,
    give_ref, sems,
):
    x, core = where_ref[0], where_ref[3]
    mover = Mover(sems)
    first = [
        mover.start(hid_hbm, hid_ref),
        mover.start(w_hbm.at[:, :, :, :, pl.ds(768, 384)], w_ref),
        mover.start(h_hbm.at[x], resid_ref),
    ]
    loads = [
        mover.start(n_hbm, n_ref),
        mover.start(dgu_hbm, dgu_ref),
        mover.start(dy_hbm, dy_ref),
    ]
    wait(first)

    def step(i, carry):
        rows = tile(i)
        part_ref[...] = nt(hid_ref[0, rows, :], weight(w_ref, 0, slice(0, 384))) + nt(
            hid_ref[1, rows, :], weight(w_ref, 1, slice(0, 384))
        )
        for y in range(2):
            part_ref[:, mine(x, y)] += resid_ref[y, rows, :].astype(F32)
        split_features(part_ref, rows, out_ref)
        return carry

    lax.fori_loop(0, TOK // TILE, step, 0)
    stores = [mover.start(out_ref, out_hbm)]
    wait(loads)
    for j in range(4):
        lanes = slice(j * 256, j * 256 + 256)
        normed = jnp.transpose(n_ref[:, lanes])
        delta = jnp.transpose(dy_ref[:, lanes])
        for y in range(2):
            wide_ref[...] = nn(normed, dgu_ref[y]).astype(BF)
            store_grad(wide_ref, core, j, y, slice(0, 768), keep_ref, give_ref)
            thin_ref[...] = nn(delta, hid_ref[y]).astype(BF)
            store_grad(thin_ref, core, j, y, slice(768, 1152), keep_ref, give_ref)
        done = pl.ds(j * 4, 4)
        stores.append(mover.start(give_ref.at[done], give_hbm.at[done]))
        stores.append(mover.start(keep_ref.at[done], keep_hbm.at[done]))
    wait(stores)


def attend_back_body(
    where_ref, d_hbm, w_hbm, proj_hbm, q_hbm, k_hbm, v_hbm, lse_hbm, table_hbm,
    rope_hbm, gain_hbm, full_hbm, n_hbm, a_hbm, mlp_sum_hbm, out_hbm,
    back_hbm, keep_hbm, give_hbm, gains_hbm,
    delta_ref, w_ref, proj_ref, q_ref, k_ref, v_ref, lse_ref, table_ref, rope_ref, gain_ref, bias_ref, dk_ref, dv_ref,
    da_ref, dproj_ref, full_ref, part_ref, back_ref, n_ref, a_ref, wide_ref, thin_ref, keep_ref, give_ref,
    head_ref, sum_ref, mlp_sum_ref, rows_ref, sems,
):
    x, core = where_ref[0], where_ref[3]
    mover = Mover(sems)
    loads = [
        mover.start(table_hbm, table_ref),
        mover.start(lse_hbm, lse_ref),
        mover.start(q_hbm, q_ref),
        mover.start(k_hbm, k_ref),
        mover.start(v_hbm, v_ref),
    ]
    loads += features_in_order(mover, d_hbm, delta_ref)
    loads.append(mover.start(w_hbm.at[:, :, :, :, pl.ds(512, 256)], w_ref.at[:, :, :, :, pl.ds(512, 256)]))
    loads += [
        mover.start(proj_hbm, proj_ref),
        mover.start(rope_hbm, rope_ref),
        mover.start(gain_hbm, gain_ref),
        mover.start(mlp_sum_hbm, mlp_sum_ref),
    ]
    more = [
        mover.start(w_hbm.at[:, :, :, :, pl.ds(0, 512)], w_ref.at[:, :, :, :, pl.ds(0, 512)]),
        mover.start(full_hbm, full_ref),
    ]
    much = [mover.start(n_hbm, n_ref), mover.start(a_hbm, a_ref)]
    last = mover.start(out_hbm, back_ref.at[:, :, :, 1])
    head_ref[...] = jnp.zeros_like(head_ref)
    sum_ref[...] = jnp.zeros_like(sum_ref)
    dk_ref[...] = jnp.zeros_like(dk_ref)
    dv_ref[...] = jnp.zeros_like(dv_ref)
    loads[0].wait()
    bias_of(table_ref, bias_ref)
    wait(loads[1:])
    stores = []

    def back(rotated, proj, gain, rows, at):
        turned = rotated * rope_ref[rows, 0:128] - pltpu.roll(rotated, 64, 1) * rope_ref[rows, 128:256]
        inv = lax.rsqrt(jnp.mean(proj * proj, axis=-1, keepdims=True) + EPSILON)
        hat = proj * inv
        head_ref[at : at + 1, :] += jnp.sum(turned * hat, axis=0, keepdims=True)
        scaled = turned * gain
        return (inv * (scaled - hat * jnp.mean(scaled * hat, axis=-1, keepdims=True))).astype(BF)

    def attend(i, carry):
        rows = tile(i)
        bias = bias_ref[rows, :]
        logs = lse_ref[rows, :]
        for y in range(2):
            da_ref[...] = nn(delta_ref[rows, :], weight(w_ref, y, slice(512, 768))).astype(BF)
            for h in range(2):
                lanes = slice(h * 128, h * 128 + 128)
                query = q_ref[y, rows, lanes]
                da = da_ref[:, lanes]
                scores = nt(query, k_ref[y]) * SCALE + bias
                soft = jnp.exp(scores - logs[:, y * 2 + h : y * 2 + h + 1])
                dp = nt(da, v_ref[y])
                dv_ref[y] += tn(da, soft.astype(BF))
                ds = (soft * (dp - jnp.sum(dp * soft, axis=-1, keepdims=True))).astype(BF)
                dk_ref[y] += tn(query, ds)
                dq = nn(ds, k_ref[y]) * SCALE
                dproj_ref[y, rows, lanes] = back(
                    dq, proj_ref[y, rows, lanes], gain_ref[2:3, 0:128], rows, 0
                )
        return carry

    lax.fori_loop(0, TOK // TILE, attend, 0)

    for i in range(TOK // TILE):
        rows = pl.ds(i * TILE, TILE)
        for y in range(2):
            dproj_ref[y, rows, 256:384] = back(
                jnp.transpose(dk_ref[y, :, rows]) * SCALE, proj_ref[y, rows, 256:384], gain_ref[2:3, 128:256], rows, 1
            )
            dproj_ref[y, rows, 384:512] = jnp.transpose(dv_ref[y, :, rows]).astype(BF)
    wait(much)
    for j in range(4):
        lanes = slice(j * 256, j * 256 + 256)
        normed = jnp.transpose(n_ref[:, lanes])
        delta = jnp.transpose(delta_ref[:, lanes])
        for y in range(2):
            wide_ref[...] = nn(normed, dproj_ref[y]).astype(BF)
            store_grad(wide_ref, core, j, y, slice(0, 512), keep_ref, give_ref)
            thin_ref[...] = nn(delta, a_ref[y]).astype(BF)
            store_grad(thin_ref, core, j, y, slice(512, 768), keep_ref, give_ref)
        done = pl.ds(j * 4, 4)
        stores.append(mover.start(give_ref.at[done], give_hbm.at[done]))
        stores.append(mover.start(keep_ref.at[done], keep_hbm.at[done]))
    wait(more)
    for i in range(TOK // TILE):
        rows = pl.ds(i * TILE, TILE)
        value = full_ref[rows, :].astype(F32)
        inv = lax.rsqrt(jnp.mean(value * value, axis=-1, keepdims=True) + EPSILON)
        hat = value * inv
        out = nt(dproj_ref[0, rows, :], weight(w_ref, 0, slice(0, 512))) + nt(
            dproj_ref[1, rows, :], weight(w_ref, 1, slice(0, 512))
        )
        sum_ref[0:1, :] += jnp.sum(out * hat, axis=0, keepdims=True)
        scaled = out * gain_ref[0:1, :]
        inner = jnp.mean(scaled * hat, axis=-1, keepdims=True)
        part_ref[...] = inv * (scaled - hat * inner)
        for y in range(2):
            part_ref[:, mine(x, y)] += delta_ref[rows, mine(x, y)].astype(F32)
        places = pl.ds(i * (TILE // 32), TILE // 32)
        for k in range(4):
            for y in range(2):
                lanes = slice(y * 512 + k * 128, y * 512 + k * 128 + 128)
                back_ref[k, y, places, 0] = part_ref[:, lanes].astype(BF).reshape(TILE // 32, 32, 128)
        if i == 0:
            last.wait()
        stores.append(mover.start(back_ref.at[:, :, places], back_hbm.at[:, :, places]))
    attn_sum, mlp_sum = sum_ref[0:1, :], mlp_sum_ref[0:1, :]
    rows_ref[0:1, :] = attn_sum[:, 0:768]
    rows_ref[1:2, 0:256] = attn_sum[:, 768:1024]
    rows_ref[1:2, 256:768] = mlp_sum[:, 0:512]
    rows_ref[2:3, 0:512] = mlp_sum[:, 512:1024]
    rows_ref[2:3, 512:640] = head_ref[0:1, :]
    rows_ref[2:3, 640:768] = head_ref[1:2, :]
    rows_ref[3:8, :] = jnp.zeros((5, 768), F32)
    stores.append(mover.start(rows_ref, gains_hbm))
    wait(stores)


def spread(value):
    return [value] + [shift(value, dx=k) for k in (1, 2, 3)]


def collect(sends):
    return [shift(sends[k - 1], dx=k) for k in (1, 2, 3)]


def repeat(value):
    return jnp.broadcast_to(value[None], (4,) + value.shape)


def collect_weight(parts):
    shard = jnp.concatenate(parts, axis=1)
    full = lax.all_gather(shard, BOTH, axis=0, tiled=False, axis_index_groups=SQUAD)
    return full.reshape(8, 2, 2, 64, shard.shape[1])


def merge(got, base):
    return call(
        merge_body, "vv", [("v", WIDE, BF)], [], 1, 1 << 20, 4 << 20, got, base, limit=16
    )[0]


def add_up(own, parts):
    return own.astype(F32) + (
        parts[0].astype(F32) + parts[1].astype(F32) + parts[2].astype(F32)
    )


def exchange(blocks, groups):
    return lax.all_to_all(blocks, BOTH, 0, 0, axis_index_groups=groups, tiled=True)


FEATURES = (2, TOK, 128)
EARLY = (8, 2, 2, 64)
WIDE = (4, 2, TOK, 128)
LATE = (8, 2, 2, 64)


fence = lax.optimization_barrier


def take(blocks, at):
    return lax.dynamic_index_in_dim(blocks, at % 4, 0, keepdims=False)


def blocks_z(where, keep, other):
    shape = (4, 4) + keep.shape[1:]
    keep, other = keep.reshape(shape), other.reshape(shape)

    def block(k):
        return take(keep, where[1] + k).astype(F32) + take(other, where[1] + k).astype(F32)

    return block(0), [block(k).astype(BF) for k in (1, 2, 3)]


def reduce_y(where, total):
    return add_up(
        take(total, where[2]), [shift(take(total, where[2] + k).astype(BF), dy=k) for k in (1, 2, 3)]
    )


def body(
    layer_input,
    out_grad,
    token_route,
    seq_lengths,
    positions,
    attn_gain,
    query_weight,
    key_weight,
    value_weight,
    query_gain,
    key_gain,
    out_weight,
    mlp_gain,
    gate_weight,
    up_weight,
    down_weight,
):
    row = lax.axis_index("row")
    col = lax.axis_index("col")
    y_lo = col // 4
    x = col % 4
    where = jnp.stack([x, row // 4, ((row // 2) % 2) * 2 + y_lo, row % 2]).astype(jnp.int32)
    places = jnp.arange(TOK, dtype=jnp.int32)
    heads = jnp.concatenate([query_gain, key_gain, jnp.zeros((D - 256,), BF)])
    all_gains = jnp.stack([attn_gain, mlp_gain, heads] + [jnp.zeros((D,), BF)] * 5).astype(F32)

    early = collect_weight([query_weight, key_weight, value_weight, out_weight.T])
    late = collect_weight([gate_weight, up_weight, down_weight.T])

    (sorted_rows,) = call(
        sort_body,
        "vhh",
        [("v", (2, ROWS, 72, 128), BF)],
        [((2, TOK, 128), BF)] * 2,
        2,
        2 * 2 * 2 * TOK * TOK * 128,
        4 << 20,
        token_route,
        layer_input,
        out_grad,
        limit=60,
    )
    arrived = exchange(sorted_rows.reshape(32, 72, 128), TEAM).reshape(2, ROWS, 72, 128)
    my_input = arrived[:, :, 0:32, :].reshape(FEATURES)
    inputs = exchange(repeat(my_input), SAME_X)
    my_grad = arrived[:, :, 32:64, :].reshape(FEATURES)
    inputs, my_grad = fence((inputs, my_grad))
    grads = spread(my_grad)
    codes = arrived[0, :, 64, 0:64].astype(F32)
    slots = (codes[:, 0:32] * 16 + codes[:, 32:64]).astype(jnp.int32).reshape(TOK)

    lengths = lax.dynamic_index_in_dim(seq_lengths, y_lo, 0, keepdims=False)[0]
    bound_one = lengths[0]
    bound_two = bound_one + lengths[1]
    bound_three = bound_two + lengths[2]
    first = jnp.where(slots >= bound_one, bound_one, 0)
    first = jnp.where(slots >= bound_two, bound_two, first)
    first = jnp.where(slots >= bound_three, bound_three, first)
    table = jnp.concatenate(
        [slots.astype(F32)[None], first.astype(F32)[None], jnp.zeros((6, TOK), F32)], axis=0
    )
    my_positions = lax.dynamic_index_in_dim(positions, y_lo, 0, keepdims=False)
    position = jnp.sum(
        jnp.where(slots[:, None] == places[None, :], my_positions[None, :], 0), axis=1
    )
    freq_steps = jnp.arange(0, HEAD_SIZE, 2).astype(F32) / HEAD_SIZE
    frequency = 1.0 / ROPE_BASE**freq_steps
    angles = position.astype(F32)[:, None] * frequency[None, :]
    cosine = jnp.cos(angles)
    sine = jnp.sin(angles)
    rope = jnp.concatenate([cosine, cosine, -sine, sine], axis=-1)
    inputs, table, rope = fence((inputs, table, rope))

    sent = [("h", WIDE, BF)]
    send, full, normed_one, proj, q_rows, k_rows, v_rows, attended, lse = call(
        attend_body,
        "hhhhh",
        sent + [("h", (TOK, D), BF), ("h", (TOK, D), BF), ("h", (2, TOK, 384), F32), ("h", (2, TOK, 256), BF),
                ("h", FEATURES, BF), ("h", FEATURES, BF), ("h", (2, TOK, 256), BF), ("h", (TOK, 128), F32)],
        [((TOK, D), BF), (EARLY + (768,), BF), ((8, TOK), F32), ((TOK, 256), F32), ((8, D), F32), ((TOK, TOK), F32),
         ((TILE, D), F32), ((TOK, D), BF), ((2, TOK, 384), F32), ((2, TOK, 256), BF), (FEATURES, BF), (FEATURES, BF),
         ((2, TOK, 256), BF), ((TOK, 128), F32), (WIDE, BF)],
        SENT + 2,
        3 << 30,
        16 << 20,
        inputs, early, table, rope, all_gains,
    )
    send, grads = fence((send, grads))
    wide = merge(exchange(send, SAME_X), my_input)
    wide = exchange(wide, SAME_X)

    send, delta_out, normed_two, hidden, dgu, mlp_sum = call(
        feed_body,
        "s" + "h" * 7,
        sent + [("h", (TOK, D), BF)] * 2 + [("h", (2, TOK, 384), BF), ("h", (2, TOK, 768), BF), ("v", (8, D), F32)],
        [((TOK, D), BF), (LATE + (1152,), BF), ((TILE, D), F32), ((8, D), F32), ((TOK, D), BF), ((TOK, D), BF),
         ((2, TOK, 384), BF), ((2, TOK, 768), BF), (WIDE, BF)],
        SENT + 8,
        5 << 30,
        16 << 20,
        where, wide, *grads, late, all_gains,
    )
    parts = exchange(send, SAME_X)
    out_home, keep, give = call(
        feed_grad_body,
        "s" + "h" * 6,
        [("h", WIDE, BF)] + [("h", (16, 64, 1152), BF)] * 2,
        [((2, TOK, 384), BF), ((2, TOK, 768), BF), ((TOK, D), BF), ((TOK, D), BF), (LATE + (384,), BF), (FEATURES, BF),
         ((TILE, D), F32), ((256, 768), BF), ((256, 384), BF), (WIDE, BF)]
        + [((16, 64, 1152), BF)] * 2,
        20,
        4 << 30,
        16 << 20,
        where, hidden, dgu, normed_two, delta_out, late, wide,
    )
    parts, out_home, keep, give = fence((parts, out_home, keep, give))
    wide = merge(parts, grads[0])
    wide = exchange(wide, SAME_X)
    late_own, late_sends = blocks_z(where, keep, shift(give, dcore=1))
    late_parts = [shift(late_sends[k - 1], dz=k) for k in (1, 2, 3)]
    wide, _ = fence((wide, late_sends))

    back, keep, give, gains = call(
        attend_back_body,
        "s" + "h" * 15,
        [("h", (4, 2, ROWS, 2, 32, 128), BF)] + [("h", (16, 64, 768), BF)] * 2 + [("h", (8, 768), F32)],
        [((TOK, D), BF), (EARLY + (768,), BF), ((2, TOK, 384), F32), ((2, TOK, 256), BF), (FEATURES, BF), (FEATURES, BF),
         ((TOK, 128), F32), ((8, TOK), F32), ((TOK, 256), F32), ((8, D), F32), ((TOK, TOK), F32), ((2, 128, TOK), F32),
         ((2, 128, TOK), F32), ((TILE, 256), BF), ((2, TOK, 512), BF), ((TOK, D), BF), ((TILE, D), F32),
         ((4, 2, ROWS, 2, 32, 128), BF), ((TOK, D), BF), ((2, TOK, 256), BF), ((256, 512), BF), ((256, 256), BF)]
        + [((16, 64, 768), BF)] * 2
        + [((8, 128), F32), ((8, D), F32), ((8, D), F32), ((8, 768), F32)],
        52,
        7 << 30,
        32 << 20,
        where, wide, early, proj, q_rows, k_rows, v_rows, lse, table, rope, all_gains, full, normed_one, attended, mlp_sum,
        out_home.reshape(4, 2, ROWS, 32, 128),
    )
    back, keep, give, gains, late_parts = fence((back, keep, give, gains, late_parts))
    gains = add_up(gains, [shift(gains, dx=k) for k in (1, 2, 3)])
    gains = (gains + shift(gains, dcore=1)).astype(BF)
    own, sends = blocks_z(where, keep, shift(give, dcore=1))
    gains = jnp.broadcast_to(gains[None], (4, 8, 768))
    own, *sends = [jnp.concatenate([rows, gains.astype(rows.dtype)], axis=1) for rows in [own] + sends]
    back = lax.psum_scatter(
        back, BOTH, scatter_dimension=0, tiled=True, axis_index_groups=SAME_X
    )
    home = exchange(back.reshape(32, 64, 128), TEAM).reshape(2, ROWS, 64, 128)
    sends, late_own, late_parts = fence((sends, late_own, late_parts))
    early_parts = [shift(sends[k - 1], dz=k) for k in (1, 2, 3)]
    late_total = add_up(late_own, late_parts)
    late_parts = [shift(take(late_total, where[2] + k).astype(BF), dy=k) for k in (1, 2, 3)]
    early_parts, late_parts = fence((early_parts, late_parts))
    late_total = add_up(take(late_total, where[2]), late_parts)
    early_parts, home = fence((early_parts, home))
    early_total = add_up(own, early_parts)
    early_total = reduce_y(where, early_total)
    layer_output, input_grad = call(
        unsort_body,
        "vh",
        [("v", (2, TOK, 128), BF)] * 2,
        [((2, ROWS, 64, 128), BF)],
        2,
        4 * 2 * TOK * TOK * 128,
        2 << 20,
        token_route,
        home,
        limit=60,
    )
    gains = early_total[64:67].reshape(3 * 768)
    early_total = early_total[0:64]
    return (
        layer_output,
        input_grad,
        gains[0:D],
        early_total[:, 0:256],
        early_total[:, 256:384],
        early_total[:, 384:512],
        gains[2 * D : 2 * D + 128],
        gains[2 * D + 128 :],
        early_total[:, 512:768].T,
        gains[D : 2 * D],
        late_total[:, 0:384],
        late_total[:, 384:768],
        late_total[:, 768:1152].T,
    )


def solution(mesh):
    in_specs = (
        P(None, "row", "col"),
        P(None, "row", "col"),
        P(None, "row"),
        P(None, "row", None),
        P(None, "row"),
        P(),
        P("row", "col"),
        P("row", "col"),
        P("row", "col"),
        P(),
        P(),
        P("col", "row"),
        P(),
        P("row", "col"),
        P("row", "col"),
        P("col", "row"),
    )
    out_specs = (
        P(None, "row", "col"),
        P(None, "row", "col"),
        P(),
        P("row", "col"),
        P("row", "col"),
        P("row", "col"),
        P(),
        P(),
        P("col", "row"),
        P(),
        P("row", "col"),
        P("row", "col"),
        P("col", "row"),
    )
    return jax.shard_map(body, mesh=mesh, in_specs=in_specs, out_specs=out_specs, check_vma=False)
```

```python
import functools
import math

import jax
import jax.numpy as jnp
from jax import lax
from jax.experimental import pallas as pl
from jax.experimental.pallas import tpu as pltpu
from jax.sharding import PartitionSpec as P

D = 1024
HEAD_SIZE = 128
EPSILON = 1e-06
ROPE_BASE = 1000000.0
NEGATIVE = -1e30
BOTH = ("row", "col")
ROWS = 16
TOK = 512
TILE = 256
SENT = 40
BF = jnp.bfloat16
F32 = jnp.float32
SCALE = 1.0 / math.sqrt(HEAD_SIZE)


def flat(row, col):
    return row * 8 + col


def spot(z, y, core, x):
    return flat(z * 4 + (y // 2) * 2 + core, (y % 2) * 4 + x)


SQUAD = [
    [flat(2 * k + core, 4 * y_lo + x) for k in range(8) for y_lo in range(2) for core in range(2)]
    for x in range(4)
]
SAME_X = [[flat(row, 4 * y_lo + x) for x in range(4)] for row in range(ROWS) for y_lo in range(2)]
TEAM = [[flat(row, 4 * y_lo + x) for y_lo in range(2) for row in range(ROWS)] for x in range(4)]


def moves(dz=0, dy=0, dcore=0, dx=0):
    return [
        (spot(z, y, core, x), spot((z + dz) % 4, (y + dy) % 4, core ^ dcore, (x + dx) % 4))
        for z in range(4)
        for y in range(4)
        for core in range(2)
        for x in range(4)
    ]


def shift(value, **step):
    return lax.ppermute(value, BOTH, moves(**step))


def dot(a, b, dims):
    return lax.dot_general(a, b, (dims, ((), ())), preferred_element_type=F32)


def nn(a, b):
    return dot(a, b, ((1,), (0,)))


def nt(a, b):
    return dot(a, b, ((1,), (1,)))


def tn(a, b):
    return dot(a, b, ((0,), (0,)))


def call(body, ins, outs, scratch, copies, flops, traffic, *args, limit=60):
    spaces = {"s": pltpu.SMEM, "v": pltpu.VMEM, "h": pl.ANY}
    return pl.pallas_call(
        body,
        out_shape=[jax.ShapeDtypeStruct(s, t) for _, s, t in outs],
        in_specs=[pl.BlockSpec(memory_space=spaces[k]) for k in ins],
        out_specs=[pl.BlockSpec(memory_space=spaces[k]) for k, _, _ in outs],
        scratch_shapes=[pltpu.VMEM(s, t) for s, t in scratch] + [pltpu.SemaphoreType.DMA((copies,))],
        compiler_params=pltpu.CompilerParams(vmem_limit_bytes=limit * 1024 * 1024),
        cost_estimate=pl.CostEstimate(flops=flops >> 6, bytes_accessed=traffic >> 6, transcendentals=0),
    )(*args)


class Mover:
    def __init__(self, sems):
        self.sems = sems
        self.used = 0

    def start(self, source, target):
        copy = pltpu.make_async_copy(source, target, self.sems.at[self.used])
        self.used += 1
        copy.start()
        return copy


def wait(copies):
    for copy in copies:
        copy.wait()


def ranks(row):
    column = jnp.transpose(jnp.broadcast_to(row, (8, TOK)))[:, 0:1]
    across = jnp.sum((column < row).astype(F32), axis=0, keepdims=True)
    down = jnp.sum((row < column).astype(F32), axis=1, keepdims=True)
    return column, across, down


def sort_body(route_ref, x_hbm, g_hbm, out_ref, x_ref, g_ref, sems):
    mover = Mover(sems)
    loads = [mover.start(x_hbm, x_ref), mover.start(g_hbm, g_ref)]
    for m in range(2):
        column, across, down = ranks(route_ref[m : m + 1, :].astype(F32))
        place = lax.broadcasted_iota(jnp.int32, (TOK, TOK), 0).astype(F32)
        pick = (place == across).astype(BF)
        slot = column - jnp.floor(column * (1.0 / TOK)) * TOK
        high = jnp.floor(slot * (1.0 / 16))
        low = slot - high * 16
        group = jnp.floor(down * (1.0 / 32))
        inner = down - group * 32
        lane = lax.broadcasted_iota(jnp.int32, (TOK, 128), 1).astype(F32)
        spread = jnp.where(lane == inner, high, jnp.where(lane == inner + 32, low, 0.0)).astype(BF)
        owner = jnp.floor(across * (1.0 / 32))
        member = (lax.broadcasted_iota(jnp.int32, (ROWS, TOK), 0).astype(F32) == owner).astype(BF)
        codes = nn(member, spread).astype(BF)
        out_ref[m, :, 64:72, :] = jnp.broadcast_to(codes[:, None, :], (ROWS, 8, 128))
        if m == 0:
            wait(loads)
        out_ref[m, :, 0:32, :] = nn(pick, x_ref[m]).astype(BF).reshape(ROWS, 32, 128)
        out_ref[m, :, 32:64, :] = nn(pick, g_ref[m]).astype(BF).reshape(ROWS, 32, 128)


def unsort_body(route_ref, home_hbm, y_ref, dx_ref, home_ref, sems):
    mover = Mover(sems)
    loads = [mover.start(home_hbm.at[m], home_ref.at[m]) for m in range(2)]
    for m in range(2):
        _, _, down = ranks(route_ref[m : m + 1, :].astype(F32))
        lane = lax.broadcasted_iota(jnp.int32, (TOK, TOK), 1).astype(F32)
        pick = (lane == down).astype(BF)
        loads[m].wait()
        for at, target_ref in ((0, dx_ref), (32, y_ref)):
            rows = home_ref[m, :, at : at + 32, :].reshape(TOK, 128)
            target_ref[m] = nn(pick, rows).astype(BF)


def features_of(mover, blocks, x, full_ref):
    return [
        mover.start(block.at[y], full_ref.at[:, mine(lax.rem(x + 4 - k, 4), y)])
        for k, block in enumerate(blocks)
        for y in range(2)
    ]


def features_in_order(mover, blocks, full_ref):
    return [
        mover.start(blocks.at[k, y], full_ref.at[:, pl.ds(y * 512 + k * 128, 128)])
        for k in range(4)
        for y in range(2)
    ]


def weight(w_ref, y, lanes):
    value = w_ref[(slice(None),) * (len(w_ref.shape) - 4) + (y, slice(None), slice(None), lanes)]
    return value.reshape(D, value.shape[-1])


def mine(x, y):
    return pl.ds(pl.multiple_of(y * 512 + x * 128, 128), 128)


def split_features(part_ref, rows, send_ref):
    for k in range(4):
        for y in range(2):
            lanes = slice(y * 512 + k * 128, y * 512 + k * 128 + 128)
            send_ref[k, y, rows, :] = part_ref[:, lanes].astype(BF)


def merge_body(got_ref, base_ref, wide_ref, sems):
    for y in range(2):
        total = base_ref[y].astype(F32)
        for k in range(4):
            total = total + got_ref[k, y].astype(F32)
        for k in range(4):
            wide_ref[k, y] = total.astype(BF)


def sent_tiles(send_ref, send_hbm, sems):
    return [
        pltpu.make_async_copy(
            send_ref.at[:, :, pl.ds(i * TILE, TILE)], send_hbm.at[:, :, pl.ds(i * TILE, TILE)], sems.at[SENT + i]
        )
        for i in range(TOK // TILE)
    ]


def norm_rope(proj, gain, cosine, sine):
    inv = lax.rsqrt(jnp.mean(proj * proj, axis=-1, keepdims=True) + EPSILON)
    normed = proj * inv * gain
    return normed * cosine + pltpu.roll(normed, 64, 1) * sine


def bias_of(table_ref, bias_ref):
    columns = jnp.transpose(table_ref[...])
    slot_row = table_ref[0:1, :]
    allowed = (slot_row <= columns[:, 0:1]) & (slot_row >= columns[:, 1:2])
    bias_ref[...] = jnp.where(allowed, 0.0, NEGATIVE)


def tile(i):
    return pl.ds(pl.multiple_of(i * TILE, TILE), TILE)


def attend_body(
    x_hbm, w_hbm, table_hbm, rope_hbm, gain_hbm,
    send_hbm, full_hbm, n_hbm, proj_hbm, q_hbm, k_hbm, v_hbm, a_hbm, lse_hbm,
    full_ref, w_ref, table_ref, rope_ref, gain_ref, bias_ref, part_ref, n_ref, proj_ref, q_ref, k_ref, v_ref, a_ref,
    lse_ref, send_ref, sems,
):
    mover = Mover(sems)
    cut = pl.ds(0, 512)
    rest = pl.ds(512, 256)
    first = features_in_order(mover, x_hbm, full_ref) + [mover.start(gain_hbm, gain_ref)]
    load_table = mover.start(table_hbm, table_ref)
    loads = [
        mover.start(w_hbm.at[:, :, :, :, cut], w_ref.at[:, :, :, :, cut]),
        mover.start(rope_hbm, rope_ref),
    ]
    load_rest = mover.start(w_hbm.at[:, :, :, :, rest], w_ref.at[:, :, :, :, rest])
    load_table.wait()
    bias_of(table_ref, bias_ref)
    wait(first)
    stores = [mover.start(full_ref, full_hbm)]

    def norm(i, carry):
        rows = tile(i)
        value = full_ref[rows, :].astype(F32)
        inv = lax.rsqrt(jnp.mean(value * value, axis=-1, keepdims=True) + EPSILON)
        n_ref[rows, :] = (value * inv * gain_ref[0:1, :]).astype(BF)
        return carry

    lax.fori_loop(0, TOK // TILE, norm, 0)
    stores.append(mover.start(n_ref, n_hbm))
    wait(loads)

    def project(i, carry):
        rows = tile(i)
        cosine, sine = rope_ref[rows, 0:128], rope_ref[rows, 128:256]
        for y in range(2):
            out = nn(n_ref[rows, :], weight(w_ref, y, slice(0, 512)))
            proj_ref[y, rows, :] = out[:, 0:384]
            for h in range(2):
                lanes = slice(h * 128, h * 128 + 128)
                q_ref[y, rows, lanes] = norm_rope(
                    out[:, lanes], gain_ref[2:3, 0:128], cosine, sine
                ).astype(BF)
            k_ref[y, rows, :] = norm_rope(
                out[:, 256:384], gain_ref[2:3, 128:256], cosine, sine
            ).astype(BF)
            v_ref[y, rows, :] = out[:, 384:512].astype(BF)
        return carry

    lax.fori_loop(0, TOK // TILE, project, 0)
    stores += [
        mover.start(proj_ref, proj_hbm),
        mover.start(q_ref, q_hbm),
        mover.start(k_ref, k_hbm),
        mover.start(v_ref, v_hbm),
    ]
    load_rest.wait()

    def attend(i, carry):
        rows = tile(i)
        bias = bias_ref[rows, :]
        lane = lax.broadcasted_iota(jnp.int32, (TILE, 128), 1)
        logs = jnp.zeros((TILE, 128), F32)
        for y in range(2):
            for h in range(2):
                lanes = slice(h * 128, h * 128 + 128)
                scores = nt(q_ref[y, rows, lanes], k_ref[y]) * SCALE + bias
                top = jnp.max(scores, axis=-1, keepdims=True)
                power = jnp.exp(scores - top)
                total = jnp.sum(power, axis=-1, keepdims=True)
                weights = (power * (1.0 / total)).astype(BF)
                a_ref[y, rows, lanes] = nn(weights, v_ref[y]).astype(BF)
                logs = jnp.where(lane == y * 2 + h, top + jnp.log(total), logs)
        lse_ref[rows, :] = logs
        return carry

    lax.fori_loop(0, TOK // TILE, attend, 0)
    stores += [mover.start(a_ref, a_hbm), mover.start(lse_ref, lse_hbm)]

    def leave(i, carry):
        rows = tile(i)
        part_ref[...] = nt(a_ref[0, rows, :], weight(w_ref, 0, slice(512, 768))) + nt(
            a_ref[1, rows, :], weight(w_ref, 1, slice(512, 768))
        )
        split_features(part_ref, rows, send_ref)
        pltpu.make_async_copy(send_ref.at[:, :, rows], send_hbm.at[:, :, rows], sems.at[SENT + i]).start()
        return carry

    lax.fori_loop(0, TOK // TILE, leave, 0)
    wait(stores + sent_tiles(send_ref, send_hbm, sems))


def feed_body(
    where_ref, h_hbm, g0, g1, g2, g3, w_hbm, gain_hbm,
    send_hbm, dy_hbm, n_hbm, hid_hbm, dgu_hbm, sum_ref,
    full_ref, w_ref, part_ref, gain_ref, dy_ref, n_ref, hid_ref, dgu_ref, send_ref, sems,
):
    mover = Mover(sems)
    cut = pl.ds(0, 768)
    rest = pl.ds(768, 384)
    loads = features_in_order(mover, h_hbm, full_ref)
    loads.append(mover.start(gain_hbm, gain_ref))
    later = [mover.start(w_hbm.at[:, :, :, :, cut], w_ref.at[:, :, :, :, cut])]
    later += features_of(mover, (g0, g1, g2, g3), where_ref[0], dy_ref)
    later.append(mover.start(w_hbm.at[:, :, :, :, rest], w_ref.at[:, :, :, :, rest]))
    sum_ref[...] = jnp.zeros_like(sum_ref)
    wait(loads)

    def norm(i, carry):
        rows = tile(i)
        value = full_ref[rows, :].astype(F32)
        inv = lax.rsqrt(jnp.mean(value * value, axis=-1, keepdims=True) + EPSILON)
        n_ref[rows, :] = (value * inv * gain_ref[1:2, :]).astype(BF)
        return carry

    lax.fori_loop(0, TOK // TILE, norm, 0)
    wait(later)
    stores = [mover.start(dy_ref, dy_hbm), mover.start(n_ref, n_hbm)]

    def step(i, carry):
        rows = tile(i)
        gain = gain_ref[1:2, :]
        value = full_ref[rows, :].astype(F32)
        inv = lax.rsqrt(jnp.mean(value * value, axis=-1, keepdims=True) + EPSILON)
        hat = value * inv
        normed = n_ref[rows, :]
        delta = dy_ref[rows, :]
        for y in range(2):
            gate = nn(normed, weight(w_ref, y, slice(0, 384)))
            up = nn(normed, weight(w_ref, y, slice(384, 768)))
            down = nn(delta, weight(w_ref, y, slice(768, 1152)))
            sigma = jax.nn.sigmoid(gate)
            act = gate * sigma
            hid_ref[y, rows, :] = (act * up).astype(BF)
            dgu_ref[y, rows, 0:384] = (down * up * sigma * (1.0 + gate * (1.0 - sigma))).astype(BF)
            dgu_ref[y, rows, 384:768] = (down * act).astype(BF)
            out = nt(dgu_ref[y, rows, :], weight(w_ref, y, slice(0, 768)))
            if y == 0:
                part_ref[...] = out
            else:
                out = part_ref[...] + out
                sum_ref[0:1, :] += jnp.sum(out * hat, axis=0, keepdims=True)
                scaled = out * gain
                inner = jnp.mean(scaled * hat, axis=-1, keepdims=True)
                part_ref[...] = inv * (scaled - hat * inner)
        split_features(part_ref, rows, send_ref)
        pltpu.make_async_copy(send_ref.at[:, :, rows], send_hbm.at[:, :, rows], sems.at[SENT + i]).start()
        pltpu.make_async_copy(hid_ref.at[:, rows], hid_hbm.at[:, rows], sems.at[SENT + 4 + i]).start()
        pltpu.make_async_copy(dgu_ref.at[:, rows], dgu_hbm.at[:, rows], sems.at[SENT + 6 + i]).start()
        return carry

    lax.fori_loop(0, TOK // TILE, step, 0)
    for i in range(TOK // TILE):
        rows = pl.ds(i * TILE, TILE)
        stores.append(pltpu.make_async_copy(hid_ref.at[:, rows], hid_hbm.at[:, rows], sems.at[SENT + 4 + i]))
        stores.append(pltpu.make_async_copy(dgu_ref.at[:, rows], dgu_hbm.at[:, rows], sems.at[SENT + 6 + i]))
    wait(stores + sent_tiles(send_ref, send_hbm, sems))


def store_grad(value_ref, core, chunk, y, lanes, keep_ref, give_ref):
    for k in range(2):
        kept = pl.multiple_of((k * 2 + core) * 64, 64)
        given = pl.multiple_of((k * 2 + 1 - core) * 64, 64)
        keep_ref[(chunk * 2 + k) * 2 + y, :, lanes] = value_ref[pl.ds(kept, 64), :]
        give_ref[(chunk * 2 + k) * 2 + y, :, lanes] = value_ref[pl.ds(given, 64), :]


def feed_grad_body(
    where_ref, hid_hbm, dgu_hbm, n_hbm, dy_hbm, w_hbm, h_hbm,
    out_hbm, keep_hbm, give_hbm,
    hid_ref, dgu_ref, n_ref, dy_ref, w_ref, resid_ref, part_ref, wide_ref, thin_ref, out_ref, keep_ref,
    give_ref, sems,
):
    x, core = where_ref[0], where_ref[3]
    mover = Mover(sems)
    first = [
        mover.start(hid_hbm, hid_ref),
        mover.start(w_hbm.at[:, :, :, :, pl.ds(768, 384)], w_ref),
        mover.start(h_hbm.at[x], resid_ref),
    ]
    loads = [
        mover.start(n_hbm, n_ref),
        mover.start(dgu_hbm, dgu_ref),
        mover.start(dy_hbm, dy_ref),
    ]
    wait(first)

    def step(i, carry):
        rows = tile(i)
        part_ref[...] = nt(hid_ref[0, rows, :], weight(w_ref, 0, slice(0, 384))) + nt(
            hid_ref[1, rows, :], weight(w_ref, 1, slice(0, 384))
        )
        for y in range(2):
            part_ref[:, mine(x, y)] += resid_ref[y, rows, :].astype(F32)
        split_features(part_ref, rows, out_ref)
        return carry

    lax.fori_loop(0, TOK // TILE, step, 0)
    stores = [mover.start(out_ref, out_hbm)]
    wait(loads)
    for j in range(4):
        lanes = slice(j * 256, j * 256 + 256)
        normed = jnp.transpose(n_ref[:, lanes])
        delta = jnp.transpose(dy_ref[:, lanes])
        for y in range(2):
            wide_ref[...] = nn(normed, dgu_ref[y]).astype(BF)
            store_grad(wide_ref, core, j, y, slice(0, 768), keep_ref, give_ref)
            thin_ref[...] = nn(delta, hid_ref[y]).astype(BF)
            store_grad(thin_ref, core, j, y, slice(768, 1152), keep_ref, give_ref)
        done = pl.ds(j * 4, 4)
        stores.append(mover.start(give_ref.at[done], give_hbm.at[done]))
        stores.append(mover.start(keep_ref.at[done], keep_hbm.at[done]))
    wait(stores)


def attend_back_body(
    where_ref, d_hbm, w_hbm, proj_hbm, q_hbm, k_hbm, v_hbm, lse_hbm, table_hbm,
    rope_hbm, gain_hbm, full_hbm, n_hbm, a_hbm, mlp_sum_hbm, out_hbm,
    back_hbm, keep_hbm, give_hbm, gains_hbm,
    delta_ref, w_ref, proj_ref, q_ref, k_ref, v_ref, lse_ref, table_ref, rope_ref, gain_ref, bias_ref, dk_ref, dv_ref,
    da_ref, dproj_ref, full_ref, part_ref, back_ref, n_ref, a_ref, wide_ref, thin_ref, keep_ref, give_ref,
    head_ref, sum_ref, mlp_sum_ref, rows_ref, sems,
):
    x, core = where_ref[0], where_ref[3]
    mover = Mover(sems)
    loads = [
        mover.start(table_hbm, table_ref),
        mover.start(lse_hbm, lse_ref),
        mover.start(q_hbm, q_ref),
        mover.start(k_hbm, k_ref),
        mover.start(v_hbm, v_ref),
    ]
    loads += features_in_order(mover, d_hbm, delta_ref)
    loads.append(mover.start(w_hbm.at[:, :, :, :, pl.ds(512, 256)], w_ref.at[:, :, :, :, pl.ds(512, 256)]))
    loads += [
        mover.start(proj_hbm, proj_ref),
        mover.start(rope_hbm, rope_ref),
        mover.start(gain_hbm, gain_ref),
        mover.start(mlp_sum_hbm, mlp_sum_ref),
    ]
    head_ref[...] = jnp.zeros_like(head_ref)
    sum_ref[...] = jnp.zeros_like(sum_ref)
    dk_ref[...] = jnp.zeros_like(dk_ref)
    dv_ref[...] = jnp.zeros_like(dv_ref)
    loads[0].wait()
    bias_of(table_ref, bias_ref)
    wait(loads[1:])
    more = [
        mover.start(w_hbm.at[:, :, :, :, pl.ds(0, 512)], w_ref.at[:, :, :, :, pl.ds(0, 512)]),
        mover.start(full_hbm, full_ref),
    ]
    much = [mover.start(n_hbm, n_ref), mover.start(a_hbm, a_ref)]
    last = mover.start(out_hbm, back_ref.at[:, :, :, 1])
    stores = []

    def back(rotated, proj, gain, rows, at):
        turned = rotated * rope_ref[rows, 0:128] - pltpu.roll(rotated, 64, 1) * rope_ref[rows, 128:256]
        inv = lax.rsqrt(jnp.mean(proj * proj, axis=-1, keepdims=True) + EPSILON)
        hat = proj * inv
        head_ref[at : at + 1, :] += jnp.sum(turned * hat, axis=0, keepdims=True)
        scaled = turned * gain
        return (inv * (scaled - hat * jnp.mean(scaled * hat, axis=-1, keepdims=True))).astype(BF)

    def attend(i, carry):
        rows = tile(i)
        bias = bias_ref[rows, :]
        logs = lse_ref[rows, :]
        for y in range(2):
            da_ref[...] = nn(delta_ref[rows, :], weight(w_ref, y, slice(512, 768))).astype(BF)
            for h in range(2):
                lanes = slice(h * 128, h * 128 + 128)
                query = q_ref[y, rows, lanes]
                da = da_ref[:, lanes]
                scores = nt(query, k_ref[y]) * SCALE + bias
                soft = jnp.exp(scores - logs[:, y * 2 + h : y * 2 + h + 1])
                dp = nt(da, v_ref[y])
                dv_ref[y] += tn(da, soft.astype(BF))
                ds = (soft * (dp - jnp.sum(dp * soft, axis=-1, keepdims=True))).astype(BF)
                dk_ref[y] += tn(query, ds)
                dq = nn(ds, k_ref[y]) * SCALE
                dproj_ref[y, rows, lanes] = back(
                    dq, proj_ref[y, rows, lanes], gain_ref[2:3, 0:128], rows, 0
                )
        return carry

    lax.fori_loop(0, TOK // TILE, attend, 0)

    for i in range(TOK // TILE):
        rows = pl.ds(i * TILE, TILE)
        for y in range(2):
            dproj_ref[y, rows, 256:384] = back(
                jnp.transpose(dk_ref[y, :, rows]) * SCALE, proj_ref[y, rows, 256:384], gain_ref[2:3, 128:256], rows, 1
            )
            dproj_ref[y, rows, 384:512] = jnp.transpose(dv_ref[y, :, rows]).astype(BF)
    wait(much)
    for j in range(4):
        lanes = slice(j * 256, j * 256 + 256)
        normed = jnp.transpose(n_ref[:, lanes])
        delta = jnp.transpose(delta_ref[:, lanes])
        for y in range(2):
            wide_ref[...] = nn(normed, dproj_ref[y]).astype(BF)
            store_grad(wide_ref, core, j, y, slice(0, 512), keep_ref, give_ref)
            thin_ref[...] = nn(delta, a_ref[y]).astype(BF)
            store_grad(thin_ref, core, j, y, slice(512, 768), keep_ref, give_ref)
        done = pl.ds(j * 4, 4)
        stores.append(mover.start(give_ref.at[done], give_hbm.at[done]))
        stores.append(mover.start(keep_ref.at[done], keep_hbm.at[done]))
    wait(more)
    for i in range(TOK // TILE):
        rows = pl.ds(i * TILE, TILE)
        value = full_ref[rows, :].astype(F32)
        inv = lax.rsqrt(jnp.mean(value * value, axis=-1, keepdims=True) + EPSILON)
        hat = value * inv
        out = nt(dproj_ref[0, rows, :], weight(w_ref, 0, slice(0, 512))) + nt(
            dproj_ref[1, rows, :], weight(w_ref, 1, slice(0, 512))
        )
        sum_ref[0:1, :] += jnp.sum(out * hat, axis=0, keepdims=True)
        scaled = out * gain_ref[0:1, :]
        inner = jnp.mean(scaled * hat, axis=-1, keepdims=True)
        part_ref[...] = inv * (scaled - hat * inner)
        for y in range(2):
            part_ref[:, mine(x, y)] += delta_ref[rows, mine(x, y)].astype(F32)
        places = pl.ds(i * (TILE // 32), TILE // 32)
        for k in range(4):
            for y in range(2):
                lanes = slice(y * 512 + k * 128, y * 512 + k * 128 + 128)
                back_ref[k, y, places, 0] = part_ref[:, lanes].astype(BF).reshape(TILE // 32, 32, 128)
        if i == 0:
            last.wait()
        stores.append(mover.start(back_ref.at[:, :, places], back_hbm.at[:, :, places]))
    attn_sum, mlp_sum = sum_ref[0:1, :], mlp_sum_ref[0:1, :]
    rows_ref[0:1, :] = attn_sum[:, 0:768]
    rows_ref[1:2, 0:256] = attn_sum[:, 768:1024]
    rows_ref[1:2, 256:768] = mlp_sum[:, 0:512]
    rows_ref[2:3, 0:512] = mlp_sum[:, 512:1024]
    rows_ref[2:3, 512:640] = head_ref[0:1, :]
    rows_ref[2:3, 640:768] = head_ref[1:2, :]
    rows_ref[3:8, :] = jnp.zeros((5, 768), F32)
    stores.append(mover.start(rows_ref, gains_hbm))
    wait(stores)


def spread(value):
    return [value] + [shift(value, dx=k) for k in (1, 2, 3)]


def collect(sends):
    return [shift(sends[k - 1], dx=k) for k in (1, 2, 3)]


def repeat(value):
    return jnp.broadcast_to(value[None], (4,) + value.shape)


def collect_weight(parts):
    shard = jnp.concatenate(parts, axis=1)
    full = lax.all_gather(shard, BOTH, axis=0, tiled=False, axis_index_groups=SQUAD)
    return full.reshape(8, 2, 2, 64, shard.shape[1])


def merge(got, base):
    return call(
        merge_body, "vv", [("v", WIDE, BF)], [], 1, 1 << 20, 4 << 20, got, base, limit=16
    )[0]


def add_up(own, parts):
    return own.astype(F32) + (
        parts[0].astype(F32) + parts[1].astype(F32) + parts[2].astype(F32)
    )


def exchange(blocks, groups):
    return lax.all_to_all(blocks, BOTH, 0, 0, axis_index_groups=groups, tiled=True)


FEATURES = (2, TOK, 128)
EARLY = (8, 2, 2, 64)
WIDE = (4, 2, TOK, 128)
LATE = (8, 2, 2, 64)


fence = lax.optimization_barrier


def take(blocks, at):
    return lax.dynamic_index_in_dim(blocks, at % 4, 0, keepdims=False)


def blocks_z(where, keep, other):
    shape = (4, 4) + keep.shape[1:]
    keep, other = keep.reshape(shape), other.reshape(shape)

    def block(k):
        return take(keep, where[1] + k).astype(F32) + take(other, where[1] + k).astype(F32)

    return block(0), [block(k).astype(BF) for k in (1, 2, 3)]


def reduce_y(where, total):
    return add_up(
        take(total, where[2]), [shift(take(total, where[2] + k).astype(BF), dy=k) for k in (1, 2, 3)]
    )


def body(
    layer_input,
    out_grad,
    token_route,
    seq_lengths,
    positions,
    attn_gain,
    query_weight,
    key_weight,
    value_weight,
    query_gain,
    key_gain,
    out_weight,
    mlp_gain,
    gate_weight,
    up_weight,
    down_weight,
):
    row = lax.axis_index("row")
    col = lax.axis_index("col")
    y_lo = col // 4
    x = col % 4
    where = jnp.stack([x, row // 4, ((row // 2) % 2) * 2 + y_lo, row % 2]).astype(jnp.int32)
    places = jnp.arange(TOK, dtype=jnp.int32)
    heads = jnp.concatenate([query_gain, key_gain, jnp.zeros((D - 256,), BF)])
    all_gains = jnp.stack([attn_gain, mlp_gain, heads] + [jnp.zeros((D,), BF)] * 5).astype(F32)

    early = collect_weight([query_weight, key_weight, value_weight, out_weight.T])
    late = collect_weight([gate_weight, up_weight, down_weight.T])

    (sorted_rows,) = call(
        sort_body,
        "vhh",
        [("v", (2, ROWS, 72, 128), BF)],
        [((2, TOK, 128), BF)] * 2,
        2,
        2 * 2 * 2 * TOK * TOK * 128,
        4 << 20,
        token_route,
        layer_input,
        out_grad,
        limit=60,
    )
    arrived = exchange(sorted_rows.reshape(32, 72, 128), TEAM).reshape(2, ROWS, 72, 128)
    my_input = arrived[:, :, 0:32, :].reshape(FEATURES)
    inputs = exchange(repeat(my_input), SAME_X)
    my_grad = arrived[:, :, 32:64, :].reshape(FEATURES)
    inputs, my_grad = fence((inputs, my_grad))
    grads = spread(my_grad)
    codes = arrived[0, :, 64, 0:64].astype(F32)
    slots = (codes[:, 0:32] * 16 + codes[:, 32:64]).astype(jnp.int32).reshape(TOK)

    lengths = lax.dynamic_index_in_dim(seq_lengths, y_lo, 0, keepdims=False)[0]
    bound_one = lengths[0]
    bound_two = bound_one + lengths[1]
    bound_three = bound_two + lengths[2]
    first = jnp.where(slots >= bound_one, bound_one, 0)
    first = jnp.where(slots >= bound_two, bound_two, first)
    first = jnp.where(slots >= bound_three, bound_three, first)
    table = jnp.concatenate(
        [slots.astype(F32)[None], first.astype(F32)[None], jnp.zeros((6, TOK), F32)], axis=0
    )
    my_positions = lax.dynamic_index_in_dim(positions, y_lo, 0, keepdims=False)
    position = jnp.sum(
        jnp.where(slots[:, None] == places[None, :], my_positions[None, :], 0), axis=1
    )
    freq_steps = jnp.arange(0, HEAD_SIZE, 2).astype(F32) / HEAD_SIZE
    frequency = 1.0 / ROPE_BASE**freq_steps
    angles = position.astype(F32)[:, None] * frequency[None, :]
    cosine = jnp.cos(angles)
    sine = jnp.sin(angles)
    rope = jnp.concatenate([cosine, cosine, -sine, sine], axis=-1)
    inputs, table, rope = fence((inputs, table, rope))

    sent = [("h", WIDE, BF)]
    send, full, normed_one, proj, q_rows, k_rows, v_rows, attended, lse = call(
        attend_body,
        "hhhhh",
        sent + [("h", (TOK, D), BF), ("h", (TOK, D), BF), ("h", (2, TOK, 384), F32), ("h", (2, TOK, 256), BF),
                ("h", FEATURES, BF), ("h", FEATURES, BF), ("h", (2, TOK, 256), BF), ("h", (TOK, 128), F32)],
        [((TOK, D), BF), (EARLY + (768,), BF), ((8, TOK), F32), ((TOK, 256), F32), ((8, D), F32), ((TOK, TOK), F32),
         ((TILE, D), F32), ((TOK, D), BF), ((2, TOK, 384), F32), ((2, TOK, 256), BF), (FEATURES, BF), (FEATURES, BF),
         ((2, TOK, 256), BF), ((TOK, 128), F32), (WIDE, BF)],
        SENT + 2,
        3 << 30,
        16 << 20,
        inputs, early, table, rope, all_gains,
    )
    send, grads = fence((send, grads))
    wide = merge(exchange(send, SAME_X), my_input)
    wide = exchange(wide, SAME_X)

    send, delta_out, normed_two, hidden, dgu, mlp_sum = call(
        feed_body,
        "s" + "h" * 7,
        sent + [("h", (TOK, D), BF)] * 2 + [("h", (2, TOK, 384), BF), ("h", (2, TOK, 768), BF), ("v", (8, D), F32)],
        [((TOK, D), BF), (LATE + (1152,), BF), ((TILE, D), F32), ((8, D), F32), ((TOK, D), BF), ((TOK, D), BF),
         ((2, TOK, 384), BF), ((2, TOK, 768), BF), (WIDE, BF)],
        SENT + 8,
        5 << 30,
        16 << 20,
        where, wide, *grads, late, all_gains,
    )
    parts = exchange(send, SAME_X)
    out_home, keep, give = call(
        feed_grad_body,
        "s" + "h" * 6,
        [("h", WIDE, BF)] + [("h", (16, 64, 1152), BF)] * 2,
        [((2, TOK, 384), BF), ((2, TOK, 768), BF), ((TOK, D), BF), ((TOK, D), BF), (LATE + (384,), BF), (FEATURES, BF),
         ((TILE, D), F32), ((256, 768), BF), ((256, 384), BF), (WIDE, BF)]
        + [((16, 64, 1152), BF)] * 2,
        20,
        4 << 30,
        16 << 20,
        where, hidden, dgu, normed_two, delta_out, late, wide,
    )
    parts, out_home, keep, give = fence((parts, out_home, keep, give))
    wide = merge(parts, grads[0])
    wide = exchange(wide, SAME_X)
    late_own, late_sends = blocks_z(where, keep, shift(give, dcore=1))
    late_parts = [shift(late_sends[k - 1], dz=k) for k in (1, 2, 3)]
    wide, _ = fence((wide, late_sends))

    back, keep, give, gains = call(
        attend_back_body,
        "s" + "h" * 15,
        [("h", (4, 2, ROWS, 2, 32, 128), BF)] + [("h", (16, 64, 768), BF)] * 2 + [("h", (8, 768), F32)],
        [((TOK, D), BF), (EARLY + (768,), BF), ((2, TOK, 384), F32), ((2, TOK, 256), BF), (FEATURES, BF), (FEATURES, BF),
         ((TOK, 128), F32), ((8, TOK), F32), ((TOK, 256), F32), ((8, D), F32), ((TOK, TOK), F32), ((2, 128, TOK), F32),
         ((2, 128, TOK), F32), ((TILE, 256), BF), ((2, TOK, 512), BF), ((TOK, D), BF), ((TILE, D), F32),
         ((4, 2, ROWS, 2, 32, 128), BF), ((TOK, D), BF), ((2, TOK, 256), BF), ((256, 512), BF), ((256, 256), BF)]
        + [((16, 64, 768), BF)] * 2
        + [((8, 128), F32), ((8, D), F32), ((8, D), F32), ((8, 768), F32)],
        52,
        7 << 30,
        32 << 20,
        where, wide, early, proj, q_rows, k_rows, v_rows, lse, table, rope, all_gains, full, normed_one, attended, mlp_sum,
        out_home.reshape(4, 2, ROWS, 32, 128),
    )
    back, keep, give, gains, late_parts = fence((back, keep, give, gains, late_parts))
    gains = add_up(gains, [shift(gains, dx=k) for k in (1, 2, 3)])
    gains = (gains + shift(gains, dcore=1)).astype(BF)
    own, sends = blocks_z(where, keep, shift(give, dcore=1))
    gains = jnp.broadcast_to(gains[None], (4, 8, 768))
    own, *sends = [jnp.concatenate([rows, gains.astype(rows.dtype)], axis=1) for rows in [own] + sends]
    back = lax.psum_scatter(
        back, BOTH, scatter_dimension=0, tiled=True, axis_index_groups=SAME_X
    )
    home = exchange(back.reshape(32, 64, 128), TEAM).reshape(2, ROWS, 64, 128)
    sends, late_own, late_parts = fence((sends, late_own, late_parts))
    early_parts = [shift(sends[k - 1], dz=k) for k in (1, 2, 3)]
    late_total = add_up(late_own, late_parts)
    late_parts = [shift(take(late_total, where[2] + k).astype(BF), dy=k) for k in (1, 2, 3)]
    early_parts, late_parts = fence((early_parts, late_parts))
    late_total = add_up(take(late_total, where[2]), late_parts)
    early_parts, home = fence((early_parts, home))
    early_total = add_up(own, early_parts)
    early_total = reduce_y(where, early_total)
    layer_output, input_grad = call(
        unsort_body,
        "vh",
        [("v", (2, TOK, 128), BF)] * 2,
        [((2, ROWS, 64, 128), BF)],
        2,
        4 * 2 * TOK * TOK * 128,
        2 << 20,
        token_route,
        home,
        limit=60,
    )
    gains = early_total[64:67].reshape(3 * 768)
    early_total = early_total[0:64]
    return (
        layer_output,
        input_grad,
        gains[0:D],
        early_total[:, 0:256],
        early_total[:, 256:384],
        early_total[:, 384:512],
        gains[2 * D : 2 * D + 128],
        gains[2 * D + 128 :],
        early_total[:, 512:768].T,
        gains[D : 2 * D],
        late_total[:, 0:384],
        late_total[:, 384:768],
        late_total[:, 768:1152].T,
    )


def solution(mesh):
    in_specs = (
        P(None, "row", "col"),
        P(None, "row", "col"),
        P(None, "row"),
        P(None, "row", None),
        P(None, "row"),
        P(),
        P("row", "col"),
        P("row", "col"),
        P("row", "col"),
        P(),
        P(),
        P("col", "row"),
        P(),
        P("row", "col"),
        P("row", "col"),
        P("col", "row"),
    )
    out_specs = (
        P(None, "row", "col"),
        P(None, "row", "col"),
        P(),
        P("row", "col"),
        P("row", "col"),
        P("row", "col"),
        P(),
        P(),
        P("col", "row"),
        P(),
        P("row", "col"),
        P("row", "col"),
        P("col", "row"),
    )
    return jax.shard_map(body, mesh=mesh, in_specs=in_specs, out_specs=out_specs, check_vma=False)
```

```python
import functools
import math

import jax
import jax.numpy as jnp
from jax import lax
from jax.experimental import pallas as pl
from jax.experimental.pallas import tpu as pltpu
from jax.sharding import PartitionSpec as P

D = 1024
HEAD_SIZE = 128
EPSILON = 1e-06
ROPE_BASE = 1000000.0
NEGATIVE = -1e30
BOTH = ("row", "col")
ROWS = 16
TOK = 512
TILE = 256
SENT = 40
BF = jnp.bfloat16
F32 = jnp.float32
SCALE = 1.0 / math.sqrt(HEAD_SIZE)


def flat(row, col):
    return row * 8 + col


def spot(z, y, core, x):
    return flat(z * 4 + (y // 2) * 2 + core, (y % 2) * 4 + x)


SQUAD = [
    [flat(2 * k + core, 4 * y_lo + x) for k in range(8) for y_lo in range(2) for core in range(2)]
    for x in range(4)
]
SAME_X = [[flat(row, 4 * y_lo + x) for x in range(4)] for row in range(ROWS) for y_lo in range(2)]
TEAM = [[flat(row, 4 * y_lo + x) for y_lo in range(2) for row in range(ROWS)] for x in range(4)]


def moves(dz=0, dy=0, dcore=0, dx=0):
    return [
        (spot(z, y, core, x), spot((z + dz) % 4, (y + dy) % 4, core ^ dcore, (x + dx) % 4))
        for z in range(4)
        for y in range(4)
        for core in range(2)
        for x in range(4)
    ]


def shift(value, **step):
    return lax.ppermute(value, BOTH, moves(**step))


def dot(a, b, dims):
    return lax.dot_general(a, b, (dims, ((), ())), preferred_element_type=F32)


def nn(a, b):
    return dot(a, b, ((1,), (0,)))


def nt(a, b):
    return dot(a, b, ((1,), (1,)))


def tn(a, b):
    return dot(a, b, ((0,), (0,)))


def call(body, ins, outs, scratch, copies, flops, traffic, *args, limit=60):
    spaces = {"s": pltpu.SMEM, "v": pltpu.VMEM, "h": pl.ANY}
    return pl.pallas_call(
        body,
        out_shape=[jax.ShapeDtypeStruct(s, t) for _, s, t in outs],
        in_specs=[pl.BlockSpec(memory_space=spaces[k]) for k in ins],
        out_specs=[pl.BlockSpec(memory_space=spaces[k]) for k, _, _ in outs],
        scratch_shapes=[pltpu.VMEM(s, t) for s, t in scratch] + [pltpu.SemaphoreType.DMA((copies,))],
        compiler_params=pltpu.CompilerParams(vmem_limit_bytes=limit * 1024 * 1024),
        cost_estimate=pl.CostEstimate(flops=flops >> 6, bytes_accessed=traffic >> 6, transcendentals=0),
    )(*args)


class Mover:
    def __init__(self, sems):
        self.sems = sems
        self.used = 0

    def start(self, source, target):
        copy = pltpu.make_async_copy(source, target, self.sems.at[self.used])
        self.used += 1
        copy.start()
        return copy


def wait(copies):
    for copy in copies:
        copy.wait()


def ranks(row):
    column = jnp.transpose(jnp.broadcast_to(row, (8, TOK)))[:, 0:1]
    across = jnp.sum((column < row).astype(F32), axis=0, keepdims=True)
    down = jnp.sum((row < column).astype(F32), axis=1, keepdims=True)
    return column, across, down


def sort_body(route_ref, x_hbm, g_hbm, out_ref, x_ref, g_ref, sems):
    mover = Mover(sems)
    loads = [mover.start(x_hbm, x_ref), mover.start(g_hbm, g_ref)]
    for m in range(2):
        column, across, down = ranks(route_ref[m : m + 1, :].astype(F32))
        place = lax.broadcasted_iota(jnp.int32, (TOK, TOK), 0).astype(F32)
        pick = (place == across).astype(BF)
        slot = column - jnp.floor(column * (1.0 / TOK)) * TOK
        high = jnp.floor(slot * (1.0 / 16))
        low = slot - high * 16
        group = jnp.floor(down * (1.0 / 32))
        inner = down - group * 32
        lane = lax.broadcasted_iota(jnp.int32, (TOK, 128), 1).astype(F32)
        spread = jnp.where(lane == inner, high, jnp.where(lane == inner + 32, low, 0.0)).astype(BF)
        owner = jnp.floor(across * (1.0 / 32))
        member = (lax.broadcasted_iota(jnp.int32, (ROWS, TOK), 0).astype(F32) == owner).astype(BF)
        codes = nn(member, spread).astype(BF)
        out_ref[m, :, 64:72, :] = jnp.broadcast_to(codes[:, None, :], (ROWS, 8, 128))
        if m == 0:
            wait(loads)
        out_ref[m, :, 0:32, :] = nn(pick, x_ref[m]).astype(BF).reshape(ROWS, 32, 128)
        out_ref[m, :, 32:64, :] = nn(pick, g_ref[m]).astype(BF).reshape(ROWS, 32, 128)


def unsort_body(route_ref, home_hbm, y_ref, dx_ref, home_ref, sems):
    mover = Mover(sems)
    loads = [mover.start(home_hbm.at[m], home_ref.at[m]) for m in range(2)]
    for m in range(2):
        _, _, down = ranks(route_ref[m : m + 1, :].astype(F32))
        lane = lax.broadcasted_iota(jnp.int32, (TOK, TOK), 1).astype(F32)
        pick = (lane == down).astype(BF)
        loads[m].wait()
        for at, target_ref in ((0, dx_ref), (32, y_ref)):
            rows = home_ref[m, :, at : at + 32, :].reshape(TOK, 128)
            target_ref[m] = nn(pick, rows).astype(BF)


def features_of(mover, blocks, x, full_ref):
    return [
        mover.start(block.at[y], full_ref.at[:, mine(lax.rem(x + 4 - k, 4), y)])
        for k, block in enumerate(blocks)
        for y in range(2)
    ]


def features_in_order(mover, blocks, full_ref):
    return [
        mover.start(blocks.at[k, y], full_ref.at[:, pl.ds(y * 512 + k * 128, 128)])
        for k in range(4)
        for y in range(2)
    ]


def weight(w_ref, y, lanes):
    value = w_ref[(slice(None),) * (len(w_ref.shape) - 4) + (y, slice(None), slice(None), lanes)]
    return value.reshape(D, value.shape[-1])


def mine(x, y):
    return pl.ds(pl.multiple_of(y * 512 + x * 128, 128), 128)


def split_features(part_ref, rows, send_ref):
    for k in range(4):
        for y in range(2):
            lanes = slice(y * 512 + k * 128, y * 512 + k * 128 + 128)
            send_ref[k, y, rows, :] = part_ref[:, lanes].astype(BF)


def merge_body(got_ref, base_ref, wide_ref, sems):
    for y in range(2):
        total = base_ref[y].astype(F32)
        for k in range(4):
            total = total + got_ref[k, y].astype(F32)
        for k in range(4):
            wide_ref[k, y] = total.astype(BF)


def sent_tiles(send_ref, send_hbm, sems):
    return [
        pltpu.make_async_copy(
            send_ref.at[:, :, pl.ds(i * TILE, TILE)], send_hbm.at[:, :, pl.ds(i * TILE, TILE)], sems.at[SENT + i]
        )
        for i in range(TOK // TILE)
    ]


def norm_rope(proj, gain, cosine, sine):
    inv = lax.rsqrt(jnp.mean(proj * proj, axis=-1, keepdims=True) + EPSILON)
    normed = proj * inv * gain
    return normed * cosine + pltpu.roll(normed, 64, 1) * sine


def bias_of(table_ref, bias_ref):
    columns = jnp.transpose(table_ref[...])
    slot_row = table_ref[0:1, :]
    allowed = (slot_row <= columns[:, 0:1]) & (slot_row >= columns[:, 1:2])
    bias_ref[...] = jnp.where(allowed, 0.0, NEGATIVE)


def tile(i):
    return pl.ds(pl.multiple_of(i * TILE, TILE), TILE)


def attend_body(
    x_hbm, w_hbm, table_hbm, rope_hbm, gain_hbm,
    send_hbm, full_hbm, n_hbm, proj_hbm, q_hbm, k_hbm, v_hbm, a_hbm, lse_hbm,
    full_ref, w_ref, table_ref, rope_ref, gain_ref, bias_ref, part_ref, n_ref, proj_ref, q_ref, k_ref, v_ref, a_ref,
    lse_ref, send_ref, sems,
):
    mover = Mover(sems)
    cut = pl.ds(0, 512)
    rest = pl.ds(512, 256)
    first = features_in_order(mover, x_hbm, full_ref) + [mover.start(gain_hbm, gain_ref)]
    load_table = mover.start(table_hbm, table_ref)
    loads = [
        mover.start(w_hbm.at[:, :, :, :, cut], w_ref.at[:, :, :, :, cut]),
        mover.start(rope_hbm, rope_ref),
    ]
    load_rest = mover.start(w_hbm.at[:, :, :, :, rest], w_ref.at[:, :, :, :, rest])
    load_table.wait()
    bias_of(table_ref, bias_ref)
    wait(first)
    stores = [mover.start(full_ref, full_hbm)]

    def norm(i, carry):
        rows = tile(i)
        value = full_ref[rows, :].astype(F32)
        inv = lax.rsqrt(jnp.mean(value * value, axis=-1, keepdims=True) + EPSILON)
        n_ref[rows, :] = (value * inv * gain_ref[0:1, :]).astype(BF)
        return carry

    lax.fori_loop(0, TOK // TILE, norm, 0)
    stores.append(mover.start(n_ref, n_hbm))
    wait(loads)

    def project(i, carry):
        rows = tile(i)
        cosine, sine = rope_ref[rows, 0:128], rope_ref[rows, 128:256]
        for y in range(2):
            out = nn(n_ref[rows, :], weight(w_ref, y, slice(0, 512)))
            proj_ref[y, rows, :] = out[:, 0:384]
            for h in range(2):
                lanes = slice(h * 128, h * 128 + 128)
                q_ref[y, rows, lanes] = norm_rope(
                    out[:, lanes], gain_ref[2:3, 0:128], cosine, sine
                ).astype(BF)
            k_ref[y, rows, :] = norm_rope(
                out[:, 256:384], gain_ref[2:3, 128:256], cosine, sine
            ).astype(BF)
            v_ref[y, rows, :] = out[:, 384:512].astype(BF)
        return carry

    lax.fori_loop(0, TOK // TILE, project, 0)
    stores += [
        mover.start(proj_ref, proj_hbm),
        mover.start(q_ref, q_hbm),
        mover.start(k_ref, k_hbm),
        mover.start(v_ref, v_hbm),
    ]
    load_rest.wait()

    def attend(i, carry):
        rows = tile(i)
        bias = bias_ref[rows, :]
        lane = lax.broadcasted_iota(jnp.int32, (TILE, 128), 1)
        logs = jnp.zeros((TILE, 128), F32)
        for y in range(2):
            for h in range(2):
                lanes = slice(h * 128, h * 128 + 128)
                scores = nt(q_ref[y, rows, lanes], k_ref[y]) * SCALE + bias
                top = jnp.max(scores, axis=-1, keepdims=True)
                power = jnp.exp(scores - top)
                total = jnp.sum(power, axis=-1, keepdims=True)
                weights = (power * (1.0 / total)).astype(BF)
                a_ref[y, rows, lanes] = nn(weights, v_ref[y]).astype(BF)
                logs = jnp.where(lane == y * 2 + h, top + jnp.log(total), logs)
        lse_ref[rows, :] = logs
        return carry

    lax.fori_loop(0, TOK // TILE, attend, 0)
    stores += [mover.start(a_ref, a_hbm), mover.start(lse_ref, lse_hbm)]

    def leave(i, carry):
        rows = tile(i)
        part_ref[...] = nt(a_ref[0, rows, :], weight(w_ref, 0, slice(512, 768))) + nt(
            a_ref[1, rows, :], weight(w_ref, 1, slice(512, 768))
        )
        split_features(part_ref, rows, send_ref)
        pltpu.make_async_copy(send_ref.at[:, :, rows], send_hbm.at[:, :, rows], sems.at[SENT + i]).start()
        return carry

    lax.fori_loop(0, TOK // TILE, leave, 0)
    wait(stores + sent_tiles(send_ref, send_hbm, sems))


def feed_body(
    where_ref, h_hbm, g0, g1, g2, g3, w_hbm, gain_hbm,
    send_hbm, dy_hbm, n_hbm, hid_hbm, dgu_hbm, sum_ref,
    full_ref, w_ref, part_ref, gain_ref, dy_ref, n_ref, hid_ref, dgu_ref, send_ref, sems,
):
    mover = Mover(sems)
    cut = pl.ds(0, 768)
    rest = pl.ds(768, 384)
    loads = features_in_order(mover, h_hbm, full_ref)
    loads.append(mover.start(gain_hbm, gain_ref))
    later = [mover.start(w_hbm.at[:, :, :, :, cut], w_ref.at[:, :, :, :, cut])]
    later += features_of(mover, (g0, g1, g2, g3), where_ref[0], dy_ref)
    later.append(mover.start(w_hbm.at[:, :, :, :, rest], w_ref.at[:, :, :, :, rest]))
    sum_ref[...] = jnp.zeros_like(sum_ref)
    wait(loads)

    def norm(i, carry):
        rows = tile(i)
        value = full_ref[rows, :].astype(F32)
        inv = lax.rsqrt(jnp.mean(value * value, axis=-1, keepdims=True) + EPSILON)
        n_ref[rows, :] = (value * inv * gain_ref[1:2, :]).astype(BF)
        return carry

    lax.fori_loop(0, TOK // TILE, norm, 0)
    wait(later)
    stores = [mover.start(dy_ref, dy_hbm), mover.start(n_ref, n_hbm)]

    def step(i, carry):
        rows = tile(i)
        gain = gain_ref[1:2, :]
        value = full_ref[rows, :].astype(F32)
        inv = lax.rsqrt(jnp.mean(value * value, axis=-1, keepdims=True) + EPSILON)
        hat = value * inv
        normed = n_ref[rows, :]
        delta = dy_ref[rows, :]
        for y in range(2):
            gate = nn(normed, weight(w_ref, y, slice(0, 384)))
            up = nn(normed, weight(w_ref, y, slice(384, 768)))
            down = nn(delta, weight(w_ref, y, slice(768, 1152)))
            sigma = jax.nn.sigmoid(gate)
            act = gate * sigma
            hid_ref[y, rows, :] = (act * up).astype(BF)
            dgu_ref[y, rows, 0:384] = (down * up * sigma * (1.0 + gate * (1.0 - sigma))).astype(BF)
            dgu_ref[y, rows, 384:768] = (down * act).astype(BF)
            out = nt(dgu_ref[y, rows, :], weight(w_ref, y, slice(0, 768)))
            if y == 0:
                part_ref[...] = out
            else:
                out = part_ref[...] + out
                sum_ref[0:1, :] += jnp.sum(out * hat, axis=0, keepdims=True)
                scaled = out * gain
                inner = jnp.mean(scaled * hat, axis=-1, keepdims=True)
                part_ref[...] = inv * (scaled - hat * inner)
        split_features(part_ref, rows, send_ref)
        pltpu.make_async_copy(send_ref.at[:, :, rows], send_hbm.at[:, :, rows], sems.at[SENT + i]).start()
        pltpu.make_async_copy(hid_ref.at[:, rows], hid_hbm.at[:, rows], sems.at[SENT + 4 + i]).start()
        pltpu.make_async_copy(dgu_ref.at[:, rows], dgu_hbm.at[:, rows], sems.at[SENT + 6 + i]).start()
        return carry

    lax.fori_loop(0, TOK // TILE, step, 0)
    for i in range(TOK // TILE):
        rows = pl.ds(i * TILE, TILE)
        stores.append(pltpu.make_async_copy(hid_ref.at[:, rows], hid_hbm.at[:, rows], sems.at[SENT + 4 + i]))
        stores.append(pltpu.make_async_copy(dgu_ref.at[:, rows], dgu_hbm.at[:, rows], sems.at[SENT + 6 + i]))
    wait(stores + sent_tiles(send_ref, send_hbm, sems))


def store_grad(value_ref, core, chunk, y, lanes, keep_ref, give_ref):
    for k in range(2):
        kept = pl.multiple_of((k * 2 + core) * 64, 64)
        given = pl.multiple_of((k * 2 + 1 - core) * 64, 64)
        keep_ref[(chunk * 2 + k) * 2 + y, :, lanes] = value_ref[pl.ds(kept, 64), :]
        give_ref[(chunk * 2 + k) * 2 + y, :, lanes] = value_ref[pl.ds(given, 64), :]


def feed_grad_body(
    where_ref, hid_hbm, dgu_hbm, n_hbm, dy_hbm, w_hbm, h_hbm,
    out_hbm, keep_hbm, give_hbm,
    hid_ref, dgu_ref, n_ref, dy_ref, w_ref, resid_ref, part_ref, wide_ref, thin_ref, out_ref, keep_ref,
    give_ref, sems,
):
    x, core = where_ref[0], where_ref[3]
    mover = Mover(sems)
    first = [
        mover.start(hid_hbm, hid_ref),
        mover.start(w_hbm.at[:, :, :, :, pl.ds(768, 384)], w_ref),
        mover.start(h_hbm.at[x], resid_ref),
    ]
    loads = [
        mover.start(n_hbm, n_ref),
        mover.start(dgu_hbm, dgu_ref),
        mover.start(dy_hbm, dy_ref),
    ]
    wait(first)

    def step(i, carry):
        rows = tile(i)
        part_ref[...] = nt(hid_ref[0, rows, :], weight(w_ref, 0, slice(0, 384))) + nt(
            hid_ref[1, rows, :], weight(w_ref, 1, slice(0, 384))
        )
        for y in range(2):
            part_ref[:, mine(x, y)] += resid_ref[y, rows, :].astype(F32)
        split_features(part_ref, rows, out_ref)
        return carry

    lax.fori_loop(0, TOK // TILE, step, 0)
    stores = [mover.start(out_ref, out_hbm)]
    wait(loads)
    for j in range(4):
        lanes = slice(j * 256, j * 256 + 256)
        normed = jnp.transpose(n_ref[:, lanes])
        delta = jnp.transpose(dy_ref[:, lanes])
        for y in range(2):
            wide_ref[...] = nn(normed, dgu_ref[y]).astype(BF)
            store_grad(wide_ref, core, j, y, slice(0, 768), keep_ref, give_ref)
            thin_ref[...] = nn(delta, hid_ref[y]).astype(BF)
            store_grad(thin_ref, core, j, y, slice(768, 1152), keep_ref, give_ref)
        done = pl.ds(j * 4, 4)
        stores.append(mover.start(give_ref.at[done], give_hbm.at[done]))
        stores.append(mover.start(keep_ref.at[done], keep_hbm.at[done]))
    wait(stores)


def attend_back_body(
    where_ref, d_hbm, w_hbm, proj_hbm, q_hbm, k_hbm, v_hbm, lse_hbm, table_hbm,
    rope_hbm, gain_hbm, full_hbm, n_hbm, a_hbm, mlp_sum_hbm, out_hbm,
    back_hbm, keep_hbm, give_hbm, gains_hbm,
    delta_ref, w_ref, proj_ref, q_ref, k_ref, v_ref, lse_ref, table_ref, rope_ref, gain_ref, bias_ref, dk_ref, dv_ref,
    da_ref, dproj_ref, full_ref, part_ref, back_ref, n_ref, a_ref, wide_ref, thin_ref, keep_ref, give_ref,
    head_ref, sum_ref, mlp_sum_ref, rows_ref, sems,
):
    x, core = where_ref[0], where_ref[3]
    mover = Mover(sems)
    loads = [
        mover.start(table_hbm, table_ref),
        mover.start(lse_hbm, lse_ref),
        mover.start(q_hbm, q_ref),
        mover.start(k_hbm, k_ref),
        mover.start(v_hbm, v_ref),
    ]
    loads += features_in_order(mover, d_hbm, delta_ref)
    loads.append(mover.start(w_hbm.at[:, :, :, :, pl.ds(512, 256)], w_ref.at[:, :, :, :, pl.ds(512, 256)]))
    loads += [
        mover.start(proj_hbm, proj_ref),
        mover.start(rope_hbm, rope_ref),
        mover.start(gain_hbm, gain_ref),
        mover.start(mlp_sum_hbm, mlp_sum_ref),
    ]
    head_ref[...] = jnp.zeros_like(head_ref)
    sum_ref[...] = jnp.zeros_like(sum_ref)
    dk_ref[...] = jnp.zeros_like(dk_ref)
    dv_ref[...] = jnp.zeros_like(dv_ref)
    loads[0].wait()
    bias_of(table_ref, bias_ref)
    wait(loads[1:])
    more = [
        mover.start(w_hbm.at[:, :, :, :, pl.ds(0, 512)], w_ref.at[:, :, :, :, pl.ds(0, 512)]),
        mover.start(full_hbm, full_ref),
    ]
    much = [mover.start(n_hbm, n_ref), mover.start(a_hbm, a_ref)]
    last = mover.start(out_hbm, back_ref.at[:, :, :, 1])
    stores = []

    def back(rotated, proj, gain, rows, at):
        turned = rotated * rope_ref[rows, 0:128] - pltpu.roll(rotated, 64, 1) * rope_ref[rows, 128:256]
        inv = lax.rsqrt(jnp.mean(proj * proj, axis=-1, keepdims=True) + EPSILON)
        hat = proj * inv
        head_ref[at : at + 1, :] += jnp.sum(turned * hat, axis=0, keepdims=True)
        scaled = turned * gain
        return (inv * (scaled - hat * jnp.mean(scaled * hat, axis=-1, keepdims=True))).astype(BF)

    def attend(i, carry):
        rows = tile(i)
        bias = bias_ref[rows, :]
        logs = lse_ref[rows, :]
        for y in range(2):
            da_ref[...] = nn(delta_ref[rows, :], weight(w_ref, y, slice(512, 768))).astype(BF)
            for h in range(2):
                lanes = slice(h * 128, h * 128 + 128)
                query = q_ref[y, rows, lanes]
                da = da_ref[:, lanes]
                scores = nt(query, k_ref[y]) * SCALE + bias
                soft = jnp.exp(scores - logs[:, y * 2 + h : y * 2 + h + 1])
                dp = nt(da, v_ref[y])
                dv_ref[y] += tn(da, soft.astype(BF))
                ds = (soft * (dp - jnp.sum(dp * soft, axis=-1, keepdims=True))).astype(BF)
                dk_ref[y] += tn(query, ds)
                dq = nn(ds, k_ref[y]) * SCALE
                dproj_ref[y, rows, lanes] = back(
                    dq, proj_ref[y, rows, lanes], gain_ref[2:3, 0:128], rows, 0
                )
        return carry

    lax.fori_loop(0, TOK // TILE, attend, 0)

    for i in range(TOK // TILE):
        rows = pl.ds(i * TILE, TILE)
        for y in range(2):
            dproj_ref[y, rows, 256:384] = back(
                jnp.transpose(dk_ref[y, :, rows]) * SCALE, proj_ref[y, rows, 256:384], gain_ref[2:3, 128:256], rows, 1
            )
            dproj_ref[y, rows, 384:512] = jnp.transpose(dv_ref[y, :, rows]).astype(BF)
    wait(much)
    for j in range(4):
        lanes = slice(j * 256, j * 256 + 256)
        normed = jnp.transpose(n_ref[:, lanes])
        delta = jnp.transpose(delta_ref[:, lanes])
        for y in range(2):
            wide_ref[...] = nn(normed, dproj_ref[y]).astype(BF)
            store_grad(wide_ref, core, j, y, slice(0, 512), keep_ref, give_ref)
            thin_ref[...] = nn(delta, a_ref[y]).astype(BF)
            store_grad(thin_ref, core, j, y, slice(512, 768), keep_ref, give_ref)
        done = pl.ds(j * 4, 4)
        stores.append(mover.start(give_ref.at[done], give_hbm.at[done]))
        stores.append(mover.start(keep_ref.at[done], keep_hbm.at[done]))
    wait(more)
    for i in range(TOK // TILE):
        rows = pl.ds(i * TILE, TILE)
        value = full_ref[rows, :].astype(F32)
        inv = lax.rsqrt(jnp.mean(value * value, axis=-1, keepdims=True) + EPSILON)
        hat = value * inv
        out = nt(dproj_ref[0, rows, :], weight(w_ref, 0, slice(0, 512))) + nt(
            dproj_ref[1, rows, :], weight(w_ref, 1, slice(0, 512))
        )
        sum_ref[0:1, :] += jnp.sum(out * hat, axis=0, keepdims=True)
        scaled = out * gain_ref[0:1, :]
        inner = jnp.mean(scaled * hat, axis=-1, keepdims=True)
        part_ref[...] = inv * (scaled - hat * inner)
        for y in range(2):
            part_ref[:, mine(x, y)] += delta_ref[rows, mine(x, y)].astype(F32)
        places = pl.ds(i * (TILE // 32), TILE // 32)
        for k in range(4):
            for y in range(2):
                lanes = slice(y * 512 + k * 128, y * 512 + k * 128 + 128)
                back_ref[k, y, places, 0] = part_ref[:, lanes].astype(BF).reshape(TILE // 32, 32, 128)
        if i == 0:
            last.wait()
        stores.append(mover.start(back_ref.at[:, :, places], back_hbm.at[:, :, places]))
    attn_sum, mlp_sum = sum_ref[0:1, :], mlp_sum_ref[0:1, :]
    rows_ref[0:1, :] = attn_sum[:, 0:768]
    rows_ref[1:2, 0:256] = attn_sum[:, 768:1024]
    rows_ref[1:2, 256:768] = mlp_sum[:, 0:512]
    rows_ref[2:3, 0:512] = mlp_sum[:, 512:1024]
    rows_ref[2:3, 512:640] = head_ref[0:1, :]
    rows_ref[2:3, 640:768] = head_ref[1:2, :]
    rows_ref[3:8, :] = jnp.zeros((5, 768), F32)
    stores.append(mover.start(rows_ref, gains_hbm))
    wait(stores)


def spread(value):
    return [value] + [shift(value, dx=k) for k in (1, 2, 3)]


def collect(sends):
    return [shift(sends[k - 1], dx=k) for k in (1, 2, 3)]


def repeat(value):
    return jnp.broadcast_to(value[None], (4,) + value.shape)


def collect_weight(parts):
    shard = jnp.concatenate(parts, axis=1)
    full = lax.all_gather(shard, BOTH, axis=0, tiled=False, axis_index_groups=SQUAD)
    return full.reshape(8, 2, 2, 64, shard.shape[1])


def merge(got, base):
    return call(
        merge_body, "vv", [("v", WIDE, BF)], [], 1, 1 << 20, 4 << 20, got, base, limit=16
    )[0]


def add_up(own, parts):
    return own.astype(F32) + (
        parts[0].astype(F32) + parts[1].astype(F32) + parts[2].astype(F32)
    )


def exchange(blocks, groups):
    return lax.all_to_all(blocks, BOTH, 0, 0, axis_index_groups=groups, tiled=True)


FEATURES = (2, TOK, 128)
EARLY = (8, 2, 2, 64)
WIDE = (4, 2, TOK, 128)
LATE = (8, 2, 2, 64)


fence = lax.optimization_barrier


def take(blocks, at):
    return lax.dynamic_index_in_dim(blocks, at % 4, 0, keepdims=False)


def blocks_z(where, keep, other):
    shape = (4, 4) + keep.shape[1:]
    keep, other = keep.reshape(shape), other.reshape(shape)

    def block(k):
        return take(keep, where[1] + k).astype(F32) + take(other, where[1] + k).astype(F32)

    return block(0), [block(k).astype(BF) for k in (1, 2, 3)]


def reduce_y(where, total):
    return add_up(
        take(total, where[2]), [shift(take(total, where[2] + k).astype(BF), dy=k) for k in (1, 2, 3)]
    )


def body(
    layer_input,
    out_grad,
    token_route,
    seq_lengths,
    positions,
    attn_gain,
    query_weight,
    key_weight,
    value_weight,
    query_gain,
    key_gain,
    out_weight,
    mlp_gain,
    gate_weight,
    up_weight,
    down_weight,
):
    row = lax.axis_index("row")
    col = lax.axis_index("col")
    y_lo = col // 4
    x = col % 4
    where = jnp.stack([x, row // 4, ((row // 2) % 2) * 2 + y_lo, row % 2]).astype(jnp.int32)
    places = jnp.arange(TOK, dtype=jnp.int32)
    heads = jnp.concatenate([query_gain, key_gain, jnp.zeros((D - 256,), BF)])
    all_gains = jnp.stack([attn_gain, mlp_gain, heads] + [jnp.zeros((D,), BF)] * 5).astype(F32)

    early = collect_weight([query_weight, key_weight, value_weight, out_weight.T])
    late = collect_weight([gate_weight, up_weight, down_weight.T])

    (sorted_rows,) = call(
        sort_body,
        "vhh",
        [("v", (2, ROWS, 72, 128), BF)],
        [((2, TOK, 128), BF)] * 2,
        2,
        2 * 2 * 2 * TOK * TOK * 128,
        4 << 20,
        token_route,
        layer_input,
        out_grad,
        limit=60,
    )
    arrived = exchange(sorted_rows.reshape(32, 72, 128), TEAM).reshape(2, ROWS, 72, 128)
    my_input = arrived[:, :, 0:32, :].reshape(FEATURES)
    inputs = exchange(repeat(my_input), SAME_X)
    my_grad = arrived[:, :, 32:64, :].reshape(FEATURES)
    codes = arrived[0, :, 64, 0:64].astype(F32)
    slots = (codes[:, 0:32] * 16 + codes[:, 32:64]).astype(jnp.int32).reshape(TOK)

    lengths = lax.dynamic_index_in_dim(seq_lengths, y_lo, 0, keepdims=False)[0]
    bound_one = lengths[0]
    bound_two = bound_one + lengths[1]
    bound_three = bound_two + lengths[2]
    first = jnp.where(slots >= bound_one, bound_one, 0)
    first = jnp.where(slots >= bound_two, bound_two, first)
    first = jnp.where(slots >= bound_three, bound_three, first)
    table = jnp.concatenate(
        [slots.astype(F32)[None], first.astype(F32)[None], jnp.zeros((6, TOK), F32)], axis=0
    )
    my_positions = lax.dynamic_index_in_dim(positions, y_lo, 0, keepdims=False)
    position = jnp.sum(
        jnp.where(slots[:, None] == places[None, :], my_positions[None, :], 0), axis=1
    )
    freq_steps = jnp.arange(0, HEAD_SIZE, 2).astype(F32) / HEAD_SIZE
    frequency = 1.0 / ROPE_BASE**freq_steps
    angles = position.astype(F32)[:, None] * frequency[None, :]
    cosine = jnp.cos(angles)
    sine = jnp.sin(angles)
    rope = jnp.concatenate([cosine, cosine, -sine, sine], axis=-1)
    inputs, my_grad, table, rope = fence((inputs, my_grad, table, rope))
    grads = spread(my_grad)

    sent = [("h", WIDE, BF)]
    send, full, normed_one, proj, q_rows, k_rows, v_rows, attended, lse = call(
        attend_body,
        "hhhhh",
        sent + [("h", (TOK, D), BF), ("h", (TOK, D), BF), ("h", (2, TOK, 384), F32), ("h", (2, TOK, 256), BF),
                ("h", FEATURES, BF), ("h", FEATURES, BF), ("h", (2, TOK, 256), BF), ("h", (TOK, 128), F32)],
        [((TOK, D), BF), (EARLY + (768,), BF), ((8, TOK), F32), ((TOK, 256), F32), ((8, D), F32), ((TOK, TOK), F32),
         ((TILE, D), F32), ((TOK, D), BF), ((2, TOK, 384), F32), ((2, TOK, 256), BF), (FEATURES, BF), (FEATURES, BF),
         ((2, TOK, 256), BF), ((TOK, 128), F32), (WIDE, BF)],
        SENT + 2,
        3 << 30,
        16 << 20,
        inputs, early, table, rope, all_gains,
    )
    send, grads = fence((send, grads))
    wide = merge(exchange(send, SAME_X), my_input)
    wide = exchange(wide, SAME_X)

    send, delta_out, normed_two, hidden, dgu, mlp_sum = call(
        feed_body,
        "s" + "h" * 7,
        sent + [("h", (TOK, D), BF)] * 2 + [("h", (2, TOK, 384), BF), ("h", (2, TOK, 768), BF), ("v", (8, D), F32)],
        [((TOK, D), BF), (LATE + (1152,), BF), ((TILE, D), F32), ((8, D), F32), ((TOK, D), BF), ((TOK, D), BF),
         ((2, TOK, 384), BF), ((2, TOK, 768), BF), (WIDE, BF)],
        SENT + 8,
        5 << 30,
        16 << 20,
        where, wide, *grads, late, all_gains,
    )
    parts = exchange(send, SAME_X)
    out_home, keep, give = call(
        feed_grad_body,
        "s" + "h" * 6,
        [("h", WIDE, BF)] + [("h", (16, 64, 1152), BF)] * 2,
        [((2, TOK, 384), BF), ((2, TOK, 768), BF), ((TOK, D), BF), ((TOK, D), BF), (LATE + (384,), BF), (FEATURES, BF),
         ((TILE, D), F32), ((256, 768), BF), ((256, 384), BF), (WIDE, BF)]
        + [((16, 64, 1152), BF)] * 2,
        20,
        4 << 30,
        16 << 20,
        where, hidden, dgu, normed_two, delta_out, late, wide,
    )
    parts, out_home, keep, give = fence((parts, out_home, keep, give))
    wide = merge(parts, grads[0])
    wide = exchange(wide, SAME_X)
    late_own, late_sends = blocks_z(where, keep, shift(give, dcore=1))
    late_parts = [shift(late_sends[k - 1], dz=k) for k in (1, 2, 3)]
    wide, _ = fence((wide, late_sends))

    back, keep, give, gains = call(
        attend_back_body,
        "s" + "h" * 15,
        [("h", (4, 2, ROWS, 2, 32, 128), BF)] + [("h", (16, 64, 768), BF)] * 2 + [("h", (8, 768), F32)],
        [((TOK, D), BF), (EARLY + (768,), BF), ((2, TOK, 384), F32), ((2, TOK, 256), BF), (FEATURES, BF), (FEATURES, BF),
         ((TOK, 128), F32), ((8, TOK), F32), ((TOK, 256), F32), ((8, D), F32), ((TOK, TOK), F32), ((2, 128, TOK), F32),
         ((2, 128, TOK), F32), ((TILE, 256), BF), ((2, TOK, 512), BF), ((TOK, D), BF), ((TILE, D), F32),
         ((4, 2, ROWS, 2, 32, 128), BF), ((TOK, D), BF), ((2, TOK, 256), BF), ((256, 512), BF), ((256, 256), BF)]
        + [((16, 64, 768), BF)] * 2
        + [((8, 128), F32), ((8, D), F32), ((8, D), F32), ((8, 768), F32)],
        52,
        7 << 30,
        32 << 20,
        where, wide, early, proj, q_rows, k_rows, v_rows, lse, table, rope, all_gains, full, normed_one, attended, mlp_sum,
        out_home.reshape(4, 2, ROWS, 32, 128),
    )
    back, keep, give, gains, late_parts = fence((back, keep, give, gains, late_parts))
    gains = add_up(gains, [shift(gains, dx=k) for k in (1, 2, 3)])
    gains = (gains + shift(gains, dcore=1)).astype(BF)
    own, sends = blocks_z(where, keep, shift(give, dcore=1))
    gains = jnp.broadcast_to(gains[None], (4, 8, 768))
    own, *sends = [jnp.concatenate([rows, gains.astype(rows.dtype)], axis=1) for rows in [own] + sends]
    back = lax.psum_scatter(
        back, BOTH, scatter_dimension=0, tiled=True, axis_index_groups=SAME_X
    )
    home = exchange(back.reshape(32, 64, 128), TEAM).reshape(2, ROWS, 64, 128)
    sends, late_own, late_parts = fence((sends, late_own, late_parts))
    early_parts = [shift(sends[k - 1], dz=k) for k in (1, 2, 3)]
    late_total = add_up(late_own, late_parts)
    late_parts = [shift(take(late_total, where[2] + k).astype(BF), dy=k) for k in (1, 2, 3)]
    early_parts, late_parts = fence((early_parts, late_parts))
    late_total = add_up(take(late_total, where[2]), late_parts)
    early_parts, home = fence((early_parts, home))
    early_total = add_up(own, early_parts)
    early_total = reduce_y(where, early_total)
    layer_output, input_grad = call(
        unsort_body,
        "vh",
        [("v", (2, TOK, 128), BF)] * 2,
        [((2, ROWS, 64, 128), BF)],
        2,
        4 * 2 * TOK * TOK * 128,
        2 << 20,
        token_route,
        home,
        limit=60,
    )
    gains = early_total[64:67].reshape(3 * 768)
    early_total = early_total[0:64]
    return (
        layer_output,
        input_grad,
        gains[0:D],
        early_total[:, 0:256],
        early_total[:, 256:384],
        early_total[:, 384:512],
        gains[2 * D : 2 * D + 128],
        gains[2 * D + 128 :],
        early_total[:, 512:768].T,
        gains[D : 2 * D],
        late_total[:, 0:384],
        late_total[:, 384:768],
        late_total[:, 768:1152].T,
    )


def solution(mesh):
    in_specs = (
        P(None, "row", "col"),
        P(None, "row", "col"),
        P(None, "row"),
        P(None, "row", None),
        P(None, "row"),
        P(),
        P("row", "col"),
        P("row", "col"),
        P("row", "col"),
        P(),
        P(),
        P("col", "row"),
        P(),
        P("row", "col"),
        P("row", "col"),
        P("col", "row"),
    )
    out_specs = (
        P(None, "row", "col"),
        P(None, "row", "col"),
        P(),
        P("row", "col"),
        P("row", "col"),
        P("row", "col"),
        P(),
        P(),
        P("col", "row"),
        P(),
        P("row", "col"),
        P("row", "col"),
        P("col", "row"),
    )
    return jax.shard_map(body, mesh=mesh, in_specs=in_specs, out_specs=out_specs, check_vma=False)
```
